32 devices in a mesh: wide: 8 (over y, x, core), depth: 4 (over z).
Axes of the slice: x: 2, y: 2, z: 4, core: 2. Of those that a mesh axis runs over, the one named last changes fastest.
Arguments:
- matrix_moles: float32 [16, 128, 64, 128], P(None, 'wide', 'depth'), may hold values from 0.2 to 4
- pore_matrix: float32 [128, 64, 128], P('wide', 'depth'), may hold values from 1 to 2
- matrix_rate: float32 [3, 128, 64, 128], P(None, 'wide', 'depth'), may hold values from 0 to 0.03
- matrix_upwind: int32 [2, 3, 128, 64, 128], P(None, None, 'wide', 'depth'), may hold values 0 or 1
- frac_moles: float32 [16, 256, 1024], P(None, ('wide', 'depth')), may hold values from 0.2 to 4
- pore_frac: float32 [256, 1024], P(('wide', 'depth')), may hold values from 1 to 2
- frac_rate: float32 [3, 256, 1024], P(None, ('wide', 'depth')), may hold values from 0 to 0.03
- frac_upwind: int32 [2, 3, 256, 1024], P(None, None, ('wide', 'depth')), may hold values 0 or 1
- ff_open: int32 [256, 2], P(('wide', 'depth')), may hold values 0 or 1
- kvalues: float32 [16], replicated, may hold values from 0.5 to 2
- slot_patch: int32 [256], replicated, may hold values from 0 to 255, as said below
- patch_block: int32 [256, 3], replicated, may hold values from 0 to 63, as said below
Outputs:
- matrix_next: float32 [16, 128, 64, 128], P(None, 'wide', 'depth')
- frac_next: float32 [16, 256, 1024], P(None, ('wide', 'depth'))
The draws below stay inside these ranges and needn't reach their ends.
Inputs may be any that keep to these rules, and one draw needn't show every extreme that they name: `slot_patch`: A permutation of the patch numbers. The slots s * 8 to s * 8 + 7 belong to device s = w * 4 + d (wide index w, depth index d). Each patch q lies in its device's layers: patch_block[q, 1] // 16 == d. A device holds at most 4 patches of one square column patch_block[q, 0], and some device holds exactly 4 in every draw. `patch_block`: row q holds patch q's first-dimension square index, its layer along the second dimension and its third-dimension square index (the square of cells p0 * 32 to p0 * 32 + 31 and p2 * 32 to p2 * 32 + 31). No two patches share a square in a layer.
All inputs are finite; a program needn't handle non-finite values. No bound on the sum of `matrix_upwind` or of `frac_upwind` or of `ff_open` on one device may be relied on, other than what follows from the above.
Results may differ from the reference program's by a relative error of at most 0.0001.
Values sent between devices are 32-bit elements; how exact they have to be, the bound alone decides.
No kernel may reach another device: no remote copies, remote signals or barrier semaphores. Data moves between devices by JAX's collectives and lax.ppermute only.
A program may use at most 128 MiB of HBM per device.

```python
import math
import jax
import jax.numpy as jnp
from jax import lax

NC = 16
PS = 32
CZ = 16
NY = 128
SWEEPS = 4
SUBSTEPS = 2
PC = 1024
NX = 128
NZ = 64
NP = 256


def layout_tables(key):
    base_key = jax.random.fold_in(key, 7)
    key_columns, key_blocks, key_wides, key_ids = jax.random.split(base_key, 4)
    wide_count = NX // (PS // 2)
    depth_count = NZ // CZ
    column_count = wide_count // 2
    patch_count = NP
    slab_total = patch_count // depth_count
    slot_total = slab_total // wide_count
    per_group = CZ * (NY // PS)
    most = max(1, 4 * slot_total // wide_count)
    heavy_size = min(most * wide_count, per_group, slab_total)
    rest = slab_total - heavy_size
    others = max(column_count - 1, 1)
    base_size = rest // others
    leftover = rest % others
    column_rank = jnp.arange(column_count, dtype=jnp.int32)
    size_by_rank = jnp.where(column_rank == 0, heavy_size, base_size + (column_rank - 1 < leftover).astype(jnp.int32)).astype(jnp.int32)
    column_scores = jax.random.randint(key_columns, (depth_count, column_count), 0, 1 << 20) * column_count + column_rank[None, :]
    column_order = jnp.argsort(column_scores, axis=1).astype(jnp.int32)
    slab_rows = jnp.arange(depth_count, dtype=jnp.int32)[:, None]
    sizes = jnp.zeros((depth_count, column_count), jnp.int32).at[slab_rows, column_order].set(jnp.broadcast_to(size_by_rank[None, :], (depth_count, column_count)))
    group_ends = jnp.cumsum(sizes, axis=1)
    group_starts = group_ends - sizes
    position = jnp.arange(slab_total, dtype=jnp.int32)
    column_of = jnp.sum((position[None, :, None] >= group_ends[:, None, :]).astype(jnp.int32), axis=2)
    rank_in = position[None, :] - jnp.take_along_axis(group_starts, column_of, axis=1)
    block_scores = jax.random.randint(key_blocks, (depth_count, column_count, per_group), 0, 1 << 20) * per_group + jnp.arange(per_group, dtype=jnp.int32)[None, None, :]
    chosen = jnp.argsort(block_scores, axis=2).astype(jnp.int32)
    block_local = chosen[slab_rows, column_of, rank_in]
    z_layer = slab_rows * CZ + block_local // (NY // PS)
    y_block = block_local % (NY // PS)
    x_block = column_of
    wide_scores = jax.random.randint(key_wides, (depth_count, wide_count), 0, 1 << 20) * wide_count + jnp.arange(wide_count, dtype=jnp.int32)[None, :]
    wide_order = jnp.argsort(wide_scores, axis=1).astype(jnp.int32)
    wide_of = wide_order[slab_rows, position[None, :] % wide_count]
    owner = wide_of * depth_count + slab_rows
    slot_index = (owner * slot_total + position[None, :] // wide_count).reshape(-1)
    patch_ids = jax.random.permutation(key_ids, patch_count).astype(jnp.int32)
    entries = jnp.stack([x_block, z_layer, y_block], axis=2).reshape(-1, 3).astype(jnp.int32)
    block_table = jnp.zeros((patch_count, 3), jnp.int32).at[patch_ids].set(entries)
    slot_table = jnp.zeros((patch_count,), jnp.int32).at[slot_index].set(patch_ids)
    return (slot_table, block_table)


def draw_slot_patch(key, part):
    return layout_tables(key)[0]


def draw_patch_block(key, part):
    return layout_tables(key)[1]


def place_ends(values, stream_key, low, top_value):
    spot = [jax.random.randint(jax.random.fold_in(stream_key, axis), (), 0, length) for axis, length in enumerate(values.shape)]
    longest = values.shape.index(max(values.shape))
    beside = spot[:longest] + [(spot[longest] + 1) % values.shape[longest]] + spot[longest + 1:]
    return values.at[tuple(spot)].set(low).at[tuple(beside)].set(top_value)


def block_levels(own_key, shape, pieces, least, largest):
    gain, own = 1.0, jax.random.fold_in(own_key, 6)
    for dim, blocks in pieces:
        draws = jnp.exp(jax.random.uniform(jax.random.fold_in(own, dim), (blocks,), jnp.float32, least / len(pieces), largest / len(pieces)))
        gain = gain * jnp.repeat(draws, shape[dim] // blocks).reshape([-1 if axis == dim else 1 for axis in range(len(shape))])
    return gain


def setup_inputs(seed: int = 0) -> dict:
    arg_keys = jax.random.split(jax.random.key(seed), 13)
    return {
        "matrix_moles": jnp.clip(jnp.exp(math.log(4.0) - 2.9957323 * jax.random.uniform(arg_keys[0], (NC, NX, NZ, NY), jnp.float32) ** block_levels(arg_keys[0], (NC, NX, NZ, NY), ((1, 8), (2, 4)), -0.2, 0.2)), 0.2, 4.0),
        "pore_matrix": jnp.clip(jnp.exp(math.log(2.0) - 0.6931472 * jax.random.uniform(arg_keys[1], (NX, NZ, NY), jnp.float32) ** block_levels(arg_keys[1], (NX, NZ, NY), ((0, 8), (1, 4)), -0.2, 0.2)), 1.0, 2.0),
        "matrix_rate": jnp.clip(0.03 * jax.random.uniform(arg_keys[2], (3, NX, NZ, NY), jnp.float32) ** block_levels(arg_keys[2], (3, NX, NZ, NY), ((1, 8), (2, 4)), -0.2, 0.2), 0.0, 0.03),
        "matrix_upwind": place_ends((jax.random.randint(arg_keys[3], (SUBSTEPS, 3, NX, NZ, NY), 0, 2) < 1).astype(jnp.int32), jax.random.fold_in(arg_keys[3], 1), 0, 1),
        "frac_moles": jnp.clip(jnp.exp(math.log(4.0) - 2.9957323 * jax.random.uniform(arg_keys[4], (NC, NP, PC), jnp.float32) ** block_levels(arg_keys[4], (NC, NP, PC), ((1, 32),), -0.2, 0.2)), 0.2, 4.0),
        "pore_frac": jnp.clip(jnp.exp(math.log(2.0) - 0.6931472 * jax.random.uniform(arg_keys[5], (NP, PC), jnp.float32) ** block_levels(arg_keys[5], (NP, PC), ((0, 32),), -0.2, 0.2)), 1.0, 2.0),
        "frac_rate": jnp.clip(0.03 * jax.random.uniform(arg_keys[6], (3, NP, PC), jnp.float32) ** block_levels(arg_keys[6], (3, NP, PC), ((1, 32),), -0.2, 0.2), 0.0, 0.03),
        "frac_upwind": place_ends((jax.random.randint(arg_keys[7], (SUBSTEPS, 3, NP, PC), 0, 2) < 1).astype(jnp.int32), jax.random.fold_in(arg_keys[7], 1), 0, 1),
        "ff_open": place_ends((jax.random.randint(arg_keys[8], (NP, 2), 0, 4) < 3).astype(jnp.int32), jax.random.fold_in(arg_keys[8], 1), 0, 1),
        "kvalues": jnp.clip(jnp.exp(jax.random.uniform(arg_keys[9], (NC,), jnp.float32, math.log(0.5), math.log(2.0))), 0.5, 2.0),
        "slot_patch": draw_slot_patch(jax.random.fold_in(arg_keys[12], 71), 0),
        "patch_block": draw_patch_block(jax.random.fold_in(arg_keys[12], 71), 0),
    }


MOBILITY_RATIO = 4.0


def flash(moles, kvalues):
    moles_sum = jnp.sum(moles, axis=0)
    layout = (moles.shape[0],) + (1,) * (moles.ndim - 1)
    equilibrium = kvalues.reshape(layout)
    excess = equilibrium - 1.0
    overall = moles / moles_sum
    vapour = jnp.full(moles_sum.shape, 0.5, jnp.float32)
    for repeat in range(SWEEPS):
        divisor = 1.0 + vapour * excess
        rachford = overall * excess / divisor
        misfit = jnp.sum(rachford, axis=0)
        gradient = jnp.sum(rachford * excess / divisor, axis=0)
        vapour = jnp.clip(vapour + misfit / (gradient + 1.0), 0.0, 1.0)
    liquid = overall / (1.0 + vapour * excess)
    gaseous = equilibrium * liquid
    lam_liquid = (1.0 - vapour) * (1.0 - vapour)
    lam_vapour = MOBILITY_RATIO * vapour * vapour
    return moles_sum * (lam_liquid * liquid + lam_vapour * gaseous) / (lam_liquid + lam_vapour)


def fracture_weights(frac_rate, upwind_now, ff_open):
    cell_count = frac_rate.shape[-1]
    position = lax.broadcasted_iota(jnp.int32, (1, cell_count), 1)
    open_flag = ff_open.astype(jnp.float32)
    open_x = jnp.where(position // PS < PS - 1, 1.0, open_flag[:, 0:1])
    open_y = jnp.where(position % PS < PS - 1, 1.0, open_flag[:, 1:2])
    opening = jnp.stack([open_x, open_y, jnp.ones_like(open_x)], axis=0)
    scaled = frac_rate * opening
    upwind = upwind_now.astype(jnp.float32)
    return jnp.concatenate([scaled * upwind, scaled * (1.0 - upwind)], axis=0)


def next_along(values, dimension):
    length = values.shape[dimension]
    trailing = lax.slice_in_dim(values, 1, length, axis=dimension)
    widths = [(0, 0)] * values.ndim
    widths[dimension] = (0, 1)
    return jnp.pad(trailing, widths)


def prev_along(values, dimension):
    length = values.shape[dimension]
    leading = lax.slice_in_dim(values, 0, length - 1, axis=dimension)
    widths = [(0, 0)] * values.ndim
    widths[dimension] = (1, 0)
    return jnp.pad(leading, widths)


def reference(matrix_moles, pore_matrix, matrix_rate, matrix_upwind, frac_moles, pore_frac, frac_rate, frac_upwind, ff_open, kvalues, slot_patch, patch_block):
    grid_shape = (NX, NZ, NY)
    keep_face = jnp.stack([lax.broadcasted_iota(jnp.int32, grid_shape, dimension) < grid_shape[dimension] - 1 for dimension in range(3)], axis=0).astype(jnp.float32)
    upwind_m = matrix_upwind.astype(jnp.float32)
    out_weight = matrix_rate * upwind_m * keep_face
    in_weight = matrix_rate * (1.0 - upwind_m) * keep_face
    blocks = patch_block[slot_patch]
    cell_index = jnp.arange(PC, dtype=jnp.int32)
    global_x = blocks[:, 0:1] * PS + cell_index[None, :] // PS
    global_y = blocks[:, 2:3] * PS + cell_index[None, :] % PS
    flat_index = ((global_x * NZ + blocks[:, 1:2]) * NY + global_y).reshape(-1).astype(jnp.int32)
    cell_total = NX * NZ * NY

    def place_cells(values):
        channels = values.shape[0]
        blank_field = jnp.zeros((channels, cell_total), jnp.float32)
        return blank_field.at[:, flat_index].set(values.reshape(channels, -1)).reshape(channels, NX, NZ, NY)

    present = place_cells(jnp.ones((1, NP, PC), jnp.float32))[0]
    moles_m = matrix_moles
    moles_f = frac_moles
    for substep in range(SUBSTEPS):
        mobile_m = flash(moles_m, kvalues)
        mobile_f = place_cells(flash(moles_f, kvalues))
        weights = place_cells(fracture_weights(frac_rate, frac_upwind[substep], ff_open))
        change_m = jnp.zeros_like(moles_m)
        for direction in range(3):
            face_flux = out_weight[substep, direction] * mobile_m - in_weight[substep, direction] * next_along(mobile_m, direction + 1)
            change_m = change_m - face_flux + prev_along(face_flux, direction + 1)
        flux_x = (weights[0] * mobile_f) * next_along(present, 0) - weights[3] * next_along(mobile_f, 1)
        change_f = -flux_x + prev_along(flux_x, 1)
        flux_y = (weights[1] * mobile_f) * next_along(present, 2) - weights[4] * next_along(mobile_f, 3)
        change_f = change_f - flux_y + prev_along(flux_y, 3)
        exchange_term = weights[2] * mobile_m - weights[5] * mobile_f
        change_f = change_f + exchange_term
        change_m = change_m - exchange_term
        moles_m = moles_m + change_m / pore_matrix
        moles_f = moles_f + change_f.reshape(NC, cell_total)[:, flat_index].reshape(NC, NP, PC) / pore_frac
    return moles_m, moles_f
```

```python
import functools

import jax
import jax.numpy as jnp
from jax import lax
from jax.experimental import pallas as pl
from jax.experimental.pallas import tpu as pltpu
from jax.sharding import PartitionSpec as P

SWEEPS = 4
SUBSTEPS = 2
MOBILITY_RATIO = 4.0
LANES = 128
SUB = 8
F32 = jnp.float32
I32 = jnp.int32

VMEM = pl.BlockSpec(memory_space=pltpu.VMEM)
SMEM = pl.BlockSpec(memory_space=pltpu.SMEM)


class Sizes:
    def __init__(self, matrix_moles, frac_moles):
        self.wide = lax.axis_size("wide")
        self.depth = lax.axis_size("depth")
        self.nc, self.x, self.z, self.y = matrix_moles.shape
        self.slots, self.pc = frac_moles.shape[1:]
        self.ps = 1
        while self.ps * self.ps < self.pc:
            self.ps *= 2
        self.by = self.y // self.ps
        self.half = self.pc // 2
        self.cols = self.wide // 2
        self.most = max(1, 4 * self.slots // self.wide)
        self.cpt = SUB // self.most
        self.out_ch = self.nc + 4 + 3 * SUBSTEPS
        self.tiles_out = -(-self.out_ch // self.cpt)
        self.tiles_back = -(-self.nc // self.cpt)
        self.groups = self.wide // SUB
        self.cells = self.x * self.z
        self.xt = LANES // self.ps
        self.jt = self.half // LANES
        assert self.y == LANES and self.slots == SUB and self.z == 2 * SUB
        assert self.x * self.ps == self.half and self.groups * self.most == self.xt == self.by


def iota(shape, dim):
    return lax.broadcasted_iota(I32, shape, dim)


def lane_roll(v, by):
    by = by % LANES
    return v if by == 0 else pltpu.roll(v, by, 1)


def sub_gather(v, idx):
    return jnp.take_along_axis(v, idx, axis=0, mode="promise_in_bounds")


def group_transpose(a, ps):
    grp = iota((SUB, LANES), 1) // ps
    odd, high = (grp & 1) == 1, (grp & 2) == 2

    def pair(u, v, upper, dist):
        return (
            jnp.where(upper, lane_roll(v, dist), u),
            jnp.where(upper, v, lane_roll(u, -dist)),
        )

    b0, b1 = pair(a[0], a[1], odd, ps)
    c0, c1 = pair(a[2], a[3], odd, ps)
    t0, t2 = pair(b0, c0, high, 2 * ps)
    t1, t3 = pair(b1, c1, high, 2 * ps)
    return [t0, t1, t2, t3]


def tree_sum(terms):
    terms = list(terms)
    while len(terms) > 1:
        terms = [a + b for a, b in zip(terms[::2], terms[1::2])] + (
            [terms[-1]] if len(terms) % 2 else []
        )
    return terms[0]


def flash_block(load, store, excess, first, nc):
    total = tree_sum([load(c) for c in range(nc)])
    vapour = None
    for sweep in range(SWEEPS):
        misfits, slopes = [], []
        for c in range(nc):
            if vapour is None:
                p = first[c]
            else:
                p = excess[c] * (1.0 / (1.0 + vapour * excess[c]))
            r = load(c) * p
            misfits.append(r)
            slopes.append(r * p)
        misfit, slope = running(misfits), running(slopes)
        before = 0.5 if vapour is None else vapour
        vapour = jnp.clip(before + misfit / (slope + total), 0.0, 1.0)
    liquid = (1.0 - vapour) * (1.0 - vapour)
    gas = MOBILITY_RATIO * vapour * vapour
    share = gas / (liquid + gas)
    for c in range(nc):
        q = 1.0 / (1.0 + vapour * excess[c])
        store(c, load(c) * q * (1.0 + share * excess[c]))


def running(terms):
    sums = [terms[0], terms[1]]
    for n, t in enumerate(terms[2:]):
        sums[n % 2] = sums[n % 2] + t
    return sums[0] + sums[1]


def k_scalars(k_ref, nc):
    excess = [k_ref[c] - 1.0 for c in range(nc)]
    first = []
    for c in range(nc):
        e = jnp.full((1, LANES), excess[c], F32)
        first.append(e / (1.0 + 0.5 * e))
    return excess, first


def own_slots(z, slot_ref, block_ref, visit):
    me = lax.axis_index("wide") * z.depth + lax.axis_index("depth")
    counts = jnp.int32(0)
    for i in range(z.slots):
        q = slot_ref[me * z.slots + i]
        p0 = block_ref[q * 3]
        rank = (counts >> (4 * p0)) & 15
        counts = counts + (jnp.int32(1) << (4 * p0))
        visit(i, p0, rank)


def pack_kernel(z, slot_ref, block_ref, moles, pore, rate, upwind, openings, out, src):
    nc, slots = z.nc, z.slots
    sub = iota((SUB, LANES), 0)
    picks = [jnp.zeros((SUB, LANES), I32) for _ in range(z.cols)]

    def visit(i, p0, rank):
        for c in range(z.cols):
            hit = ((sub % z.most) == rank) & (p0 == c)
            picks[c] = jnp.where(hit, i, picks[c])

    own_slots(z, slot_ref, block_ref, visit)
    src[pl.ds(0, nc * slots), :] = moles[...]
    src[pl.ds(nc * slots, slots), :] = pore[...]
    cell = iota((slots, z.pc), 1)
    flags = openings[...].astype(F32)
    open_x = jnp.where(cell // z.ps < z.ps - 1, 1.0, flags[:, 0:1])
    open_y = jnp.where(cell % z.ps < z.ps - 1, 1.0, flags[:, 1:2])
    base = (nc + 1) * slots
    src[pl.ds(base, slots), :] = rate[pl.ds(0, slots), :] * open_x
    src[pl.ds(base + slots, slots), :] = rate[pl.ds(slots, slots), :] * open_y
    src[pl.ds(base + 2 * slots, slots), :] = rate[pl.ds(2 * slots, slots), :]
    for n in range(3 * SUBSTEPS):
        src[pl.ds(base + (3 + n) * slots, slots), :] = upwind[pl.ds(n * slots, slots), :].astype(
            F32
        )
    for n in range(z.out_ch, z.tiles_out * z.cpt):
        src[pl.ds(n * slots, slots), :] = jnp.zeros((slots, z.pc), F32)

    def tile(m, carry):
        for h in range(2):
            for j in range(z.jt):
                lanes = pl.ds(h * z.half + j * LANES, LANES)
                parts = [
                    src[pl.ds(pl.multiple_of((m * z.cpt + cp) * slots, slots), slots), lanes]
                    for cp in range(z.cpt)
                ]
                for c in range(z.cols):
                    v = sub_gather(parts[0], picks[c])
                    for cp in range(1, z.cpt):
                        v = jnp.where(sub // z.most >= cp, sub_gather(parts[cp], picks[c]), v)
                    row = (((2 * c + h) * z.jt + j) * z.tiles_out + m) * SUB
                    out[pl.ds(pl.multiple_of(row, SUB), SUB), :] = v
        return carry

    lax.fori_loop(0, z.tiles_out, tile, 0)


def spread_kernel(z, slot_ref, block_ref, recv, out):
    sub = iota((SUB, LANES), 0)
    ranks = jnp.zeros((SUB, LANES), I32)
    column = jnp.zeros((SUB, LANES), I32)

    def visit(i, p0, rank):
        nonlocal ranks, column
        ranks = jnp.where(sub == i, rank, ranks)
        column = jnp.where(sub == i, p0, column)

    own_slots(z, slot_ref, block_ref, visit)

    def tile(m, carry):
        for h in range(2):
            for j in range(z.jt):
                parts = []
                for c in range(z.cols):
                    row = (((2 * c + h) * z.jt + j) * z.tiles_back + m) * SUB
                    parts.append(recv[pl.ds(pl.multiple_of(row, SUB), SUB), :])
                for cp in range(z.cpt):
                    v = sub_gather(parts[0], cp * z.most + ranks)
                    for c in range(1, z.cols):
                        v = jnp.where(
                            column == c, sub_gather(parts[c], cp * z.most + ranks), v
                        )
                    row = (m * z.cpt + cp) * SUB
                    out[
                        pl.ds(pl.multiple_of(row, SUB), SUB),
                        pl.ds(h * z.half + j * LANES, LANES),
                    ] = v
        return carry

    lax.fori_loop(0, z.tiles_back, tile, 0)


def tables(z, slot_ref, block_ref, tab):
    sub, grp = iota((SUB, LANES), 0), iota((SUB, LANES), 1) // z.ps
    bid = [(sub + SUB * h) * z.by + grp for h in range(2)]
    pid = sub + SUB * grp
    wide, deep = lax.axis_index("wide"), lax.axis_index("depth")
    here, after = wide // 2, jnp.where(wide + 1 < z.wide, (wide + 1) // 2, -1)

    def visit(w, state):
        v0, v1, n0, n1, back = state
        counts = jnp.int32(0)
        for i in range(z.slots):
            q = slot_ref[(w * z.depth + deep) * z.slots + i]
            p0 = block_ref[q * 3]
            block = lax.rem(block_ref[q * 3 + 1], z.z) * z.by + block_ref[q * 3 + 2]
            rank = (counts >> (4 * p0)) & 15
            counts = counts + (jnp.int32(1) << (4 * p0))
            place = lax.rem(w, SUB) + SUB * (lax.div(w, SUB) * z.most + rank)
            b_here = jnp.where(p0 == here, block, -1)
            b_next = jnp.where(p0 == after, block, -1)
            p_here = jnp.where(p0 == here, place, -1)
            v0 = jnp.where(bid[0] == b_here, place, v0)
            v1 = jnp.where(bid[1] == b_here, place, v1)
            n0 = jnp.where(bid[0] == b_next, 1, n0)
            n1 = jnp.where(bid[1] == b_next, 1, n1)
            back = jnp.where(pid == p_here, block, back)
        return v0, v1, n0, n1, back

    zero = jnp.zeros((SUB, LANES), I32)
    v0, v1, n0, n1, back = lax.fori_loop(
        0, z.wide, visit, (zero - 1, zero - 1, zero, zero, zero - 1)
    )
    for h, (v, n) in enumerate(((v0, n0), (v1, n1))):
        rows = pl.ds(h * SUB, SUB)
        tab[rows, :] = jnp.where(v >= 0, v & (SUB - 1), 0)
        tab[pl.ds(2 * SUB + h * SUB, SUB), :] = jnp.where(
            v >= 0, (grp - (v >> 3)) & (z.by - 1), -1
        )
        tab[pl.ds(4 * SUB + h * SUB, SUB), :] = n
    depth_row = back // z.by
    tab[pl.ds(6 * SUB, SUB), :] = jnp.where(back >= 0, depth_row & (SUB - 1), 0)
    shift = (grp - (back & (z.by - 1))) & (z.by - 1)
    tab[pl.ds(7 * SUB, SUB), :] = jnp.where(back >= 0, shift * 2 + (depth_row >> 3), -1)


def face(z, rate, upwind, t, d, x):
    g = rate[pl.ds(pl.multiple_of(d * z.cells + x * z.z, z.z), z.z), :]
    u = upwind[pl.ds(pl.multiple_of((t * 3 + d) * z.cells + x * z.z, z.z), z.z), :].astype(F32)
    if d == 0:
        keep = (x < z.x - 1) | (lax.axis_index("wide") < z.wide - 1)
    elif d == 1:
        keep = (iota((z.z, LANES), 0) < z.z - 1) | (lax.axis_index("depth") < z.depth - 1)
    else:
        keep = iota((z.z, LANES), 1) < LANES - 1
    g = jnp.where(keep, g, 0.0)
    out = g * u
    return out, g - out


def plane(z, ref, c, x):
    return ref[pl.ds(pl.multiple_of(c * z.cells + x * z.z, z.z), z.z), :]


def matrix_messages(z, mobile, rate, upwind, t, wide_a, wide_b, deep_a, deep_b):
    nc = z.nc
    even_w = lax.rem(lax.axis_index("wide"), 2) == 0
    even_d = lax.rem(lax.axis_index("depth"), 2) == 0
    out, into = face(z, rate, upwind, t, 0, z.x - 1)
    for c in range(nc):
        ahead = plane(z, mobile, c, z.x - 1) * out
        behind = plane(z, mobile, c, 0)
        rows = pl.ds(c * z.z, z.z)
        wide_a[rows, :] = jnp.where(even_w, ahead, behind)
        wide_b[rows, :] = jnp.where(even_w, behind, ahead)
    rows = pl.ds(nc * z.z, z.z)
    wide_a[rows, :] = into
    wide_b[rows, :] = into
    edge = lax.axis_index("depth") < z.depth - 1

    def last_rows(ref, base, h):
        return ref[pl.ds(base + h * SUB * z.z + z.z - 1, SUB, stride=z.z), :]

    for h in range(z.x // SUB):
        g = jnp.where(edge, last_rows(rate, z.cells, h), 0.0)
        u = last_rows(upwind, (t * 3 + 1) * z.cells, h).astype(F32)
        out = g * u
        for c in range(nc):
            ahead = last_rows(mobile, c * z.cells, h) * out
            behind = mobile[pl.ds(c * z.cells + h * SUB * z.z, SUB, stride=z.z), :]
            rows = pl.ds(c * z.x + h * SUB, SUB)
            deep_a[rows, :] = jnp.where(even_d, ahead, behind)
            deep_b[rows, :] = jnp.where(even_d, behind, ahead)
        rows = pl.ds(nc * z.x + h * SUB, SUB)
        deep_a[rows, :] = g - out
        deep_b[rows, :] = g - out


def flash_field(z, moles, mobile, k_ref):
    excess, first = k_scalars(k_ref, z.nc)
    step = 2

    def block(n, carry):
        def rows(c):
            return pl.ds(pl.multiple_of(c * z.cells + n * step * z.z, z.z), step * z.z)

        def store(c, v):
            mobile[rows(c), :] = v

        flash_block(lambda c: moles[rows(c), :], store, excess, first, z.nc)
        return carry

    lax.fori_loop(0, z.x // step, block, 0)


def first_matrix_kernel(
    z, k_ref, slot_ref, block_ref, moles, rate, upwind, mobile, wide_a, wide_b, deep_a, deep_b, tab
):
    tables(z, slot_ref, block_ref, tab)
    flash_field(z, moles, mobile, k_ref)
    matrix_messages(z, mobile, rate, upwind, 0, wide_a, wide_b, deep_a, deep_b)


def frac_messages(z, mobile, coef, tab, t, frac_a, frac_b):
    even = lax.rem(lax.axis_index("wide"), 2) == 0
    last = lax.axis_index("wide") == z.wide - 1
    here = (tab[pl.ds(2 * SUB, 2 * SUB), :] >= 0).astype(F32)
    out = plane(z, coef, 1, z.x - 1) * plane(z, coef, 4 + 3 * t, z.x - 1)
    into = plane(z, coef, 1, z.x - 1) - out
    out = jnp.where(last, 0.0, out)
    into = jnp.where(last, 0.0, into)
    for c in range(z.nc):
        ahead = plane(z, mobile, c, z.x - 1) * out
        behind = plane(z, mobile, c, 0) * here
        rows = pl.ds(c * z.z, z.z)
        frac_a[rows, :] = jnp.where(even, ahead, behind)
        frac_b[rows, :] = jnp.where(even, behind, ahead)
    rows = pl.ds(z.nc * z.z, z.z)
    frac_a[rows, :] = into
    frac_b[rows, :] = into


def first_frac_kernel(z, k_ref, tab, recv, moles, mobile, coef, frac_a, frac_b):
    lane_tile = z.tiles_out * SUB
    stride = z.jt * lane_tile
    from_sub = [tab[pl.ds(h * SUB, SUB), :] for h in range(2)]
    shift = [tab[pl.ds(2 * SUB + h * SUB, SUB), :] for h in range(2)]

    def channel(c, dst, first_row, default):
        for j in range(z.jt):
            a = [
                recv[
                    pl.ds(
                        g * SUB * stride + j * lane_tile + c * z.most + k, SUB, stride=stride
                    ),
                    :,
                ]
                for g in range(z.groups)
                for k in range(z.most)
            ]
            for xi, v in enumerate(group_transpose(a, z.ps)):
                rolled = [lane_roll(v, n * z.ps) for n in range(z.by)]
                for h in range(2):
                    got = jnp.full((SUB, LANES), default, F32)
                    for n in range(z.by):
                        got = jnp.where(shift[h] == n, sub_gather(rolled[n], from_sub[h]), got)
                    row = first_row + (z.xt * j + xi) * z.z + h * SUB
                    dst[pl.ds(pl.multiple_of(row, SUB), SUB), :] = got

    def amount(c, carry):
        channel(c, moles, c * z.cells, 1.0)
        return carry

    def weight(c, carry):
        channel(z.nc + c, coef, c * z.cells, jnp.where(c == 0, 1.0, 0.0))
        return carry

    lax.fori_loop(0, z.nc, amount, 0)
    lax.fori_loop(0, z.out_ch - z.nc, weight, 0)
    flash_field(z, moles, mobile, k_ref)
    frac_messages(z, mobile, coef, tab, 0, frac_a, frac_b)


def matrix_update(z, t, moles, mobile, mobile_f, coef, rate, upwind, pore, halos, new):
    wide_a, wide_b, deep_a, deep_b = halos
    nc = z.nc
    even_w = lax.rem(lax.axis_index("wide"), 2) == 0
    even_d = lax.rem(lax.axis_index("depth"), 2) == 0
    sub = iota((z.z, LANES), 0)

    def side(a, b, first, row, count):
        rows = pl.ds(row, count)
        even = even_w if a is wide_a else even_d
        if first:
            return jnp.where(even, b[rows, :], a[rows, :])
        return jnp.where(even, a[rows, :], b[rows, :])

    def at(x, low, high):
        inv = 1.0 / plane(z, pore, 0, x)
        ox, ix = face(z, rate, upwind, t, 0, x)
        oz, iz = face(z, rate, upwind, t, 1, x)
        oy, iy = face(z, rate, upwind, t, 2, x)
        if low:
            pox, pix = 1.0, side(wide_a, wide_b, True, nc * z.z, z.z)
        else:
            pox, pix = face(z, rate, upwind, t, 0, x - 1)
        wz = jnp.broadcast_to(side(deep_a, deep_b, True, nc * z.x + x, 1), (z.z, LANES))
        poz = jnp.where(sub == 0, 1.0, pltpu.roll(oz, 1, 0))
        piz = jnp.where(sub == 0, wz, pltpu.roll(iz, 1, 0))
        poy, piy = lane_roll(oy, 1), lane_roll(iy, 1)
        g2 = plane(z, coef, 3, x)
        w2 = g2 * plane(z, coef, 4 + 3 * t + 2, x)
        w5 = (g2 - w2) * inv
        own = (ox + pix + oz + piz + oy + piy + w2) * inv
        ax, bx = ix * inv, pox * inv
        az, bz = iz * inv, poz * inv
        ay, by = iy * inv, poy * inv
        for c in range(nc):
            g = plane(z, mobile, c, x)
            before = (
                side(wide_a, wide_b, True, c * z.z, z.z) if low else plane(z, mobile, c, x - 1)
            )
            after = (
                side(wide_a, wide_b, False, c * z.z, z.z) if high else plane(z, mobile, c, x + 1)
            )
            hz0 = jnp.broadcast_to(side(deep_a, deep_b, True, c * z.x + x, 1), (z.z, LANES))
            hz1 = jnp.broadcast_to(side(deep_a, deep_b, False, c * z.x + x, 1), (z.z, LANES))
            zb = jnp.where(sub == 0, hz0, pltpu.roll(g, 1, 0))
            za = jnp.where(sub == z.z - 1, hz1, pltpu.roll(g, z.z - 1, 0))
            v = plane(z, moles, c, x) - own * g + ax * after + bx * before
            v = v + (az * za + bz * zb)
            v = v + (ay * lane_roll(g, -1) + by * lane_roll(g, 1))
            v = v + w5 * plane(z, mobile_f, c, x)
            new[pl.ds(pl.multiple_of(c * z.cells + x * z.z, z.z), z.z), :] = v

    at(0, True, False)

    def middle(x, carry):
        at(x, False, False)
        return carry

    lax.fori_loop(1, z.x - 1, middle, 0)
    at(z.x - 1, False, True)


def matrix_kernel(
    z, t, k_ref, moles, mobile, mobile_f, coef, rate, upwind, pore, ha, hb, hc, hd, new,
    mobile_new=None, wide_a=None, wide_b=None, deep_a=None, deep_b=None,
):
    matrix_update(
        z, t, moles, mobile, mobile_f, coef, rate, upwind, pore, (ha, hb, hc, hd), new
    )
    if mobile_new is not None:
        flash_field(z, new, mobile_new, k_ref)
        matrix_messages(z, mobile_new, rate, upwind, t + 1, wide_a, wide_b, deep_a, deep_b)


def frac_update(z, t, tab, moles, mobile, mobile_m, coef, frac_a, frac_b, new):
    nc = z.nc
    even = lax.rem(lax.axis_index("wide"), 2) == 0
    here = (tab[pl.ds(2 * SUB, 2 * SUB), :] >= 0).astype(F32)
    beyond = tab[pl.ds(4 * SUB, 2 * SUB), :].astype(F32)
    lane = iota((z.z, LANES), 1)
    next_y = jnp.where(lane == LANES - 1, 0.0, lane_roll(here, -1))

    def side(first, row):
        rows = pl.ds(row, z.z)
        if first:
            return jnp.where(even, frac_b[rows, :], frac_a[rows, :])
        return jnp.where(even, frac_a[rows, :], frac_b[rows, :])

    def split(x, d, mask):
        g = plane(z, coef, 1 + d, x) * mask
        out = g * plane(z, coef, 4 + 3 * t + d, x)
        return out, g - out

    def at(x, low, high):
        inv = 1.0 / plane(z, coef, 0, x)
        ox, ix = split(x, 0, beyond if high else here)
        if low:
            pox, pix = here, side(True, nc * z.z) * here
        else:
            pox, pix = split(x - 1, 0, here)
        oy, iy = split(x, 1, next_y)
        poy, piy = lane_roll(oy, 1), lane_roll(iy, 1)
        w2, w5 = split(x, 2, 1.0)
        own = (ox + pix + oy + piy + w5) * inv
        ax, bx = ix * inv, pox * inv
        ay, by = iy * inv, poy * inv
        w2 = w2 * inv
        for c in range(nc):
            g = plane(z, mobile, c, x)
            before = side(True, c * z.z) if low else plane(z, mobile, c, x - 1)
            after = side(False, c * z.z) if high else plane(z, mobile, c, x + 1)
            v = plane(z, moles, c, x) - own * g + (ax * after + bx * before)
            v = v + (ay * lane_roll(g, -1) + by * lane_roll(g, 1))
            v = v + w2 * plane(z, mobile_m, c, x)
            new[pl.ds(pl.multiple_of(c * z.cells + x * z.z, z.z), z.z), :] = v

    at(0, True, False)

    def middle(x, carry):
        at(x, False, False)
        return carry

    lax.fori_loop(1, z.x - 1, middle, 0)
    at(z.x - 1, False, True)


def frac_kernel(
    z, t, k_ref, tab, moles, mobile, mobile_m, coef, fa, fb, new, mobile_new, frac_a, frac_b
):
    frac_update(z, t, tab, moles, mobile, mobile_m, coef, fa, fb, new)
    flash_field(z, new, mobile_new, k_ref)
    frac_messages(z, mobile_new, coef, tab, t + 1, frac_a, frac_b)


def last_frac_kernel(z, t, tab, moles, mobile, mobile_m, coef, fa, fb, back, new):
    frac_update(z, t, tab, moles, mobile, mobile_m, coef, fa, fb, new)
    lane_tile = z.tiles_back * SUB
    stride = z.jt * lane_tile
    to_sub = tab[pl.ds(6 * SUB, SUB), :]
    code = tab[pl.ds(7 * SUB, SUB), :]

    def channel(c, carry):
        for j in range(z.jt):
            tiles = []
            for xi in range(z.xt):
                x = z.xt * j + xi
                got = jnp.zeros((SUB, LANES), F32)
                for h in range(2):
                    row = c * z.cells + x * z.z + h * SUB
                    v = new[pl.ds(pl.multiple_of(row, SUB), SUB), :]
                    for n in range(z.by):
                        got = jnp.where(
                            code == 2 * n + h, sub_gather(lane_roll(v, n * z.ps), to_sub), got
                        )
                tiles.append(got)
            for n, v in enumerate(group_transpose(tiles, z.ps)):
                g, k = divmod(n, z.most)
                start = g * SUB * stride + j * lane_tile + c * z.most + k
                back[pl.ds(start, SUB, stride=stride), :] = v
        return carry

    lax.fori_loop(0, z.nc, channel, 0)


def swap(value, axis, ahead):
    count = lax.axis_size(axis)
    if ahead:
        pairs = [(i, i ^ 1) for i in range(count)]
    else:
        pairs = [(i, (i - 1 if i % 2 == 0 else i + 1) % count) for i in range(count)]
    return lax.ppermute(value, axis, pairs)


def call(kernel, name, in_specs, out_shape, args, scratch=(), mib=24, flops=10**8):
    bytes_accessed = sum(a.size * 4 for a in args)
    return pl.pallas_call(
        kernel,
        name=name,
        out_shape=out_shape,
        in_specs=in_specs,
        out_specs=jax.tree.map(lambda _: VMEM, out_shape),
        scratch_shapes=scratch,
        compiler_params=pltpu.CompilerParams(vmem_limit_bytes=mib << 20),
        cost_estimate=pl.CostEstimate(
            flops=flops, bytes_accessed=bytes_accessed, transcendentals=0
        ),
    )(*args)


def shape(rows, lanes=LANES, dtype=F32):
    return jax.ShapeDtypeStruct((rows, lanes), dtype)


def local(
    matrix_moles,
    pore_matrix,
    matrix_rate,
    matrix_upwind,
    frac_moles,
    pore_frac,
    frac_rate,
    frac_upwind,
    ff_open,
    kvalues,
    slot_patch,
    patch_block,
):
    z = Sizes(matrix_moles, frac_moles)
    bind = lambda f, *a: functools.partial(f, z, *a)
    block_flat = patch_block.reshape(-1)
    moles = matrix_moles.reshape(-1, z.y)
    pore = pore_matrix.reshape(-1, z.y)
    rate = matrix_rate.reshape(-1, z.y)
    upwind = matrix_upwind.reshape(-1, z.y)
    field = shape(z.nc * z.cells)
    msg_w, msg_d = shape((z.nc + 1) * z.z), shape((z.nc + 1) * z.x)

    send = call(
        bind(pack_kernel), "pack", [SMEM] * 2 + [VMEM] * 5,
        shape(z.wide * z.jt * z.tiles_out * SUB),
        (
            slot_patch,
            block_flat,
            frac_moles.reshape(-1, z.pc),
            pore_frac,
            frac_rate.reshape(-1, z.pc),
            frac_upwind.reshape(-1, z.pc),
            ff_open,
        ),
        scratch=[pltpu.VMEM((z.tiles_out * z.cpt * z.slots, z.pc), F32)],
    )
    recv = lax.all_to_all(send, "wide", split_axis=0, concat_axis=0, tiled=True)
    mobile_m, wa, wb, da, db, tab = call(
        bind(first_matrix_kernel), "matrix_first", [SMEM] * 3 + [VMEM] * 3,
        (field, msg_w, msg_w, msg_d, msg_d, shape(8 * SUB, dtype=I32)),
        (kvalues, slot_patch, block_flat, moles, rate, upwind),
    )

    def exchange_m(wa, wb, da, db):
        return (
            swap(wa, "wide", True),
            swap(wb, "wide", False),
            swap(da, "depth", True),
            swap(db, "depth", False),
        )

    halos = exchange_m(wa, wb, da, db)
    moles_f, mobile_f, coef, fa, fb = call(
        bind(first_frac_kernel), "frac_first", [SMEM] + [VMEM] * 2,
        (field, field, shape((z.out_ch - z.nc) * z.cells), msg_w, msg_w),
        (kvalues, tab, recv),
    )
    fa, fb = swap(fa, "wide", True), swap(fb, "wide", False)
    for t in range(SUBSTEPS - 1):
        moles, mobile_m_new, wa, wb, da, db = call(
            bind(matrix_kernel, t), "matrix_step", [SMEM] + [VMEM] * 11,
            (field, field, msg_w, msg_w, msg_d, msg_d),
            (kvalues, moles, mobile_m, mobile_f, coef, rate, upwind, pore, *halos),
        )
        halos = exchange_m(wa, wb, da, db)
        moles_f, mobile_f, fa, fb = call(
            bind(frac_kernel, t), "frac_step", [SMEM] + [VMEM] * 7,
            (field, field, msg_w, msg_w),
            (kvalues, tab, moles_f, mobile_f, mobile_m, coef, fa, fb),
        )
        mobile_m = mobile_m_new
        fa, fb = swap(fa, "wide", True), swap(fb, "wide", False)
    t = SUBSTEPS - 1
    back = call(
        bind(last_frac_kernel, t), "frac_last", [VMEM] * 7,
        shape(z.wide * z.jt * z.tiles_back * SUB),
        (tab, moles_f, mobile_f, mobile_m, coef, fa, fb),
        scratch=[pltpu.VMEM((z.nc * z.cells, LANES), F32)],
    )
    returned = lax.all_to_all(back, "wide", split_axis=0, concat_axis=0, tiled=True)
    moles = call(
        bind(matrix_kernel, t), "matrix_last", [SMEM] + [VMEM] * 11,
        field,
        (kvalues, moles, mobile_m, mobile_f, coef, rate, upwind, pore, *halos),
    )
    frac = call(
        bind(spread_kernel), "spread", [SMEM] * 2 + [VMEM],
        shape(z.nc * z.slots, z.pc),
        (slot_patch, block_flat, returned),
    )
    return moles.reshape(matrix_moles.shape), frac.reshape(frac_moles.shape)


def solution(mesh):
    placed = (
        P(None, "wide", "depth", None),
        P("wide", "depth", None),
        P(None, "wide", "depth", None),
        P(None, None, "wide", "depth", None),
        P(None, ("wide", "depth"), None),
        P(("wide", "depth"), None),
        P(None, ("wide", "depth"), None),
        P(None, None, ("wide", "depth"), None),
        P(("wide", "depth"), None),
        P(),
        P(),
        P(),
    )
    return jax.shard_map(
        local,
        mesh=mesh,
        in_specs=placed,
        out_specs=(P(None, "wide", "depth", None), P(None, ("wide", "depth"), None)),
        check_vma=False,
    )
```

```python
import functools

import jax
import jax.numpy as jnp
from jax import lax
from jax.experimental import pallas as pl
from jax.experimental.pallas import tpu as pltpu
from jax.sharding import PartitionSpec as P


SWEEPS = 4
SUBSTEPS = 2
MOBILITY_RATIO = 4.0
LANES = 128
SUB = 8
PARTS = 4
FLASH_PLANES = 2
F32 = jnp.float32
I32 = jnp.int32

VMEM = pl.BlockSpec(memory_space=pltpu.VMEM)
SMEM = pl.BlockSpec(memory_space=pltpu.SMEM)
HBM = pl.BlockSpec(memory_space=pltpu.HBM)


class Sizes:
    def __init__(self, matrix_moles, frac_moles):
        self.wide = lax.axis_size("wide")
        self.depth = lax.axis_size("depth")
        self.nc, self.x, self.z, self.y = matrix_moles.shape
        self.slots, self.pc = frac_moles.shape[1:]
        self.ps = 1
        while self.ps * self.ps < self.pc:
            self.ps *= 2
        self.by = self.y // self.ps
        self.half = self.pc // 2
        self.cols = self.wide // 2
        self.most = max(1, 4 * self.slots // self.wide)
        self.cpt = SUB // self.most
        self.coefs = 4 + 3 * SUBSTEPS
        self.out_ch = self.nc + self.coefs
        self.tiles_out = -(-self.out_ch // self.cpt)
        self.tiles_back = -(-self.nc // self.cpt)
        self.groups = self.wide // SUB
        self.cells = self.x * self.z
        self.places = SUB * self.by
        self.blocks = self.z * self.by
        self.xt = LANES // self.ps
        self.jt = self.half // LANES
        assert self.y == LANES and self.slots == SUB and self.z == 2 * SUB
        assert self.x * self.ps == self.half and self.groups * self.most == self.xt == self.by


def iota(shape, dim):
    return lax.broadcasted_iota(I32, shape, dim)


def lane_roll(v, by):
    by = by % LANES
    return v if by == 0 else pltpu.roll(v, by, 1)


def sub_gather(v, idx):
    return jnp.take_along_axis(v, idx, axis=0, mode="promise_in_bounds")


def group_transpose(a, ps):
    grp = iota((SUB, LANES), 1) // ps
    odd, high = (grp & 1) == 1, (grp & 2) == 2

    def pair(u, v, upper, dist):
        return (
            jnp.where(upper, lane_roll(v, dist), u),
            jnp.where(upper, v, lane_roll(u, -dist)),
        )

    b0, b1 = pair(a[0], a[1], odd, ps)
    c0, c1 = pair(a[2], a[3], odd, ps)
    t0, t2 = pair(b0, c0, high, 2 * ps)
    t1, t3 = pair(b1, c1, high, 2 * ps)
    return [t0, t1, t2, t3]


def tree_sum(terms):
    terms = list(terms)
    while len(terms) > 1:
        terms = [a + b for a, b in zip(terms[::2], terms[1::2])] + (
            [terms[-1]] if len(terms) % 2 else []
        )
    return terms[0]


def flash_block(load, store, excess, first, nc):
    total = tree_sum([load(c) for c in range(nc)])
    vapour = None
    for _ in range(SWEEPS):
        misfits, slopes = [], []
        for c in range(nc):
            if vapour is None:
                p = first[c]
            else:
                p = excess[c] * (1.0 / (1.0 + vapour * excess[c]))
            r = load(c) * p
            misfits.append(r)
            slopes.append(r * p)
        misfit, slope = running(misfits), running(slopes)
        before = 0.5 if vapour is None else vapour
        vapour = jnp.clip(before + misfit / (slope + total), 0.0, 1.0)
    liquid = (1.0 - vapour) * (1.0 - vapour)
    gas = MOBILITY_RATIO * vapour * vapour
    share = gas / (liquid + gas)
    for c in range(nc):
        q = 1.0 / (1.0 + vapour * excess[c])
        store(c, load(c) * q * (1.0 + share * excess[c]))


def running(terms):
    sums = [terms[0], terms[1]]
    for n, t in enumerate(terms[2:]):
        sums[n % 2] = sums[n % 2] + t
    return sums[0] + sums[1]


def k_scalars(k_ref, nc):
    excess = [k_ref[c] - 1.0 for c in range(nc)]
    first = []
    for c in range(nc):
        e = jnp.full((1, LANES), excess[c], F32)
        first.append(e / (1.0 + 0.5 * e))
    return excess, first


def own_slots(z, slot_ref, block_ref, visit):
    me = lax.axis_index("wide") * z.depth + lax.axis_index("depth")
    counts = jnp.int32(0)
    for i in range(z.slots):
        q = slot_ref[me * z.slots + i]
        p0 = block_ref[0, q]
        rank = (counts >> (4 * p0)) & 15
        counts = counts + (jnp.int32(1) << (4 * p0))
        visit(i, p0, rank)


def pack_kernel(
    z, slot_ref, block_ref, open_ref, moles, pore, rate, upwind, out, src, flags, stage,
    in_sem, out_sem,
):
    nc, slots = z.nc, z.slots
    first = nc * slots
    reads = [
        pltpu.make_async_copy(moles, src.at[pl.ds(0, first), :], in_sem.at[0]),
        pltpu.make_async_copy(pore, src.at[pl.ds(first, slots), :], in_sem.at[1]),
        pltpu.make_async_copy(rate, src.at[pl.ds(first + slots, 3 * slots), :], in_sem.at[2]),
        pltpu.make_async_copy(upwind, flags, in_sem.at[3]),
    ]
    for copy in reads:
        copy.start()
    sub = iota((SUB, LANES), 0)
    picks = [jnp.zeros((SUB, LANES), I32) for _ in range(z.cols)]
    opens = [jnp.zeros((SUB, z.pc), I32) for _ in range(2)]
    row_id = iota((SUB, z.pc), 0)

    def visit(i, p0, rank):
        for c in range(z.cols):
            hit = ((sub % z.most) == rank) & (p0 == c)
            picks[c] = jnp.where(hit, i, picks[c])
        for d in range(2):
            opens[d] = jnp.where(row_id == i, open_ref[d, i], opens[d])

    own_slots(z, slot_ref, block_ref, visit)

    def send(c):
        per = z.jt * z.tiles_out * SUB

        def tile(m, carry):
            for h in range(2):
                for j in range(z.jt):
                    v = None
                    for cp in range(z.cpt):
                        part = sub_gather(
                            src[
                                pl.ds(pl.multiple_of((m * z.cpt + cp) * slots, slots), slots),
                                pl.ds(h * z.half + j * LANES, LANES),
                            ],
                            picks[c],
                        )
                        v = part if v is None else jnp.where(sub // z.most >= cp, part, v)
                    row = ((2 * c + h) * z.jt + j) * z.tiles_out * SUB + m * SUB
                    stage[pl.ds(pl.multiple_of(row, SUB), SUB), :] = v
            return carry

        lax.fori_loop(0, z.tiles_out, tile, 0)
        rows = pl.ds(2 * c * per, 2 * per)
        return pltpu.make_async_copy(stage.at[rows, :], out.at[rows, :], out_sem.at[c])

    for copy in reads:
        copy.wait()
    cell = iota((slots, z.pc), 1)
    g = first + slots
    open_x = jnp.where(cell // z.ps < z.ps - 1, 1, opens[0]).astype(F32)
    open_y = jnp.where(cell % z.ps < z.ps - 1, 1, opens[1]).astype(F32)
    src[pl.ds(g, slots), :] = src[pl.ds(g, slots), :] * open_x
    src[pl.ds(g + slots, slots), :] = src[pl.ds(g + slots, slots), :] * open_y
    n_flags = 3 * SUBSTEPS * slots
    src[pl.ds(g + 3 * slots, n_flags), :] = flags[...].astype(F32)
    spare = src.shape[0] - (g + 3 * slots + n_flags)
    if spare:
        src[pl.ds(g + 3 * slots + n_flags, spare), :] = jnp.zeros((spare, z.pc), F32)
    writes = []
    for c in range(z.cols):
        writes.append(send(c))
        writes[-1].start()
    for copy in writes:
        copy.wait()


def spread_kernel(z, slot_ref, block_ref, recv_hbm, out, recv, sem):
    read = pltpu.make_async_copy(recv_hbm, recv, sem)
    read.start()
    sub = iota((SUB, LANES), 0)
    ranks = jnp.zeros((SUB, LANES), I32)
    column = jnp.zeros((SUB, LANES), I32)

    def visit(i, p0, rank):
        nonlocal ranks, column
        ranks = jnp.where(sub == i, rank, ranks)
        column = jnp.where(sub == i, p0, column)

    own_slots(z, slot_ref, block_ref, visit)
    read.wait()

    def tile(m, carry):
        for h in range(2):
            for j in range(z.jt):
                parts = []
                for c in range(z.cols):
                    row = (((2 * c + h) * z.jt + j) * z.tiles_back + m) * SUB
                    parts.append(recv[pl.ds(pl.multiple_of(row, SUB), SUB), :])
                for cp in range(z.cpt):
                    v = sub_gather(parts[0], cp * z.most + ranks)
                    for c in range(1, z.cols):
                        v = jnp.where(
                            column == c, sub_gather(parts[c], cp * z.most + ranks), v
                        )
                    row = (m * z.cpt + cp) * SUB
                    out[
                        pl.ds(pl.multiple_of(row, SUB), SUB),
                        pl.ds(h * z.half + j * LANES, LANES),
                    ] = v
        return carry

    lax.fori_loop(0, z.tiles_back, tile, 0)


def tables(z, slot_ref, block_ref, tab, gather):
    sub, grp = iota((SUB, LANES), 0), iota((SUB, LANES), 1) // z.ps
    bid = [(sub + SUB * h) * z.by + grp for h in range(2)]
    wide, deep = lax.axis_index("wide"), lax.axis_index("depth")
    here, after = wide // 2, jnp.where(wide + 1 < z.wide, (wide + 1) // 2, -1)

    def visit(w, state):
        v0, v1, n0, n1 = state
        counts = jnp.int32(0)
        for i in range(z.slots):
            q = slot_ref[(w * z.depth + deep) * z.slots + i]
            p0 = block_ref[0, q]
            block = lax.rem(block_ref[1, q], z.z) * z.by + block_ref[2, q]
            rank = (counts >> (4 * p0)) & 15
            counts = counts + (jnp.int32(1) << (4 * p0))
            place = lax.rem(w, SUB) + SUB * (lax.div(w, SUB) * z.most + rank)
            b_here = jnp.where(p0 == here, block, -1)
            b_next = jnp.where(p0 == after, block, -1)
            v0 = jnp.where(bid[0] == b_here, place, v0)
            v1 = jnp.where(bid[1] == b_here, place, v1)
            n0 = jnp.where(bid[0] == b_next, 1, n0)
            n1 = jnp.where(bid[1] == b_next, 1, n1)
            column = lax.rem(block, z.by) * z.z + lax.div(block, z.by)

            @pl.when(p0 == here)
            def _():
                gather[pl.ds(place, 1), :] = (
                    (lane % z.blocks == column) & (lane < 3 * z.blocks)
                ).astype(F32)

        return v0, v1, n0, n1

    gather[...] = jnp.zeros(gather.shape, F32)
    lane = iota((1, gather.shape[1]), 1)
    zero = jnp.zeros((SUB, LANES), I32)
    v0, v1, n0, n1 = lax.fori_loop(0, z.wide, visit, (zero - 1, zero - 1, zero, zero))
    for h, (v, n) in enumerate(((v0, n0), (v1, n1))):
        rows = pl.ds(h * SUB, SUB)
        tab[rows, :] = jnp.where(v >= 0, v & (SUB - 1), 0)
        tab[pl.ds(2 * SUB + h * SUB, SUB), :] = jnp.where(
            v >= 0, (grp - (v >> 3)) & (z.by - 1), -1
        )
        tab[pl.ds(4 * SUB + h * SUB, SUB), :] = n


def split3(v):
    hi = v.astype(jnp.bfloat16)
    rest = v - hi.astype(F32)
    mid = rest.astype(jnp.bfloat16)
    low = (rest - mid.astype(F32)).astype(jnp.bfloat16)
    return jnp.concatenate([hi, mid, low], axis=0)


def field_to_rows(z, src, first_row, gather, back, c):
    lane_tile = z.tiles_back * SUB
    stride = z.jt * lane_tile
    for jj in range(0, z.jt, 2):
        columns = []
        for n in range(2):
            parts = [None] * (z.by * (z.z // SUB))
            for h in range(z.z // SUB):
                tiles_x = []
                for xi in range(z.xt):
                    row = first_row + (z.xt * (jj + n) + xi) * z.z + h * SUB
                    tiles_x.append(src[pl.ds(pl.multiple_of(row, SUB), SUB), :])
                for p, v in enumerate(group_transpose(tiles_x, z.ps)):
                    parts[p * (z.z // SUB) + h] = v
            columns.append(jnp.concatenate(parts, axis=0))
        block_rows = jnp.concatenate(columns, axis=1)
        rows = jnp.dot(gather, split3(block_rows), preferred_element_type=F32)
        for n in range(2):
            for i in range(z.by):
                g, k = divmod(i, z.most)
                start = g * SUB * stride + (jj + n) * lane_tile + c * z.most + k
                back[pl.ds(start, SUB, stride=stride), :] = rows[
                    i * SUB : (i + 1) * SUB, n * LANES : (n + 1) * LANES
                ]


def face(z, rate, upwind, t, d, x):
    g = rate[pl.ds(pl.multiple_of(d * z.cells + x * z.z, z.z), z.z), :]
    u = upwind[pl.ds(pl.multiple_of((t * 3 + d) * z.cells + x * z.z, z.z), z.z), :].astype(F32)
    if d == 0:
        keep = (x < z.x - 1) | (lax.axis_index("wide") < z.wide - 1)
    elif d == 1:
        keep = (iota((z.z, LANES), 0) < z.z - 1) | (lax.axis_index("depth") < z.depth - 1)
    else:
        keep = iota((z.z, LANES), 1) < LANES - 1
    g = jnp.where(keep, g, 0.0)
    out = g * u
    return out, g - out


def stream(z, src, dst, sem):
    rows = [pl.ds(n * z.cells // PARTS, z.cells // PARTS) for n in range(PARTS)]
    return [
        pltpu.make_async_copy(src.at[:, r, :], dst.at[:, r, :], sem.at[n])
        for n, r in enumerate(rows)
    ]


def plane(z, ref, c, x):
    if len(ref.shape) == 3:
        return ref[c, pl.ds(pl.multiple_of(x * z.z, z.z), z.z), :]
    return ref[pl.ds(pl.multiple_of(c * z.cells + x * z.z, z.z), z.z), :]


def matrix_messages(z, mobile, rate, upwind, t, wide_a, wide_b, deep_a, deep_b):
    nc = z.nc
    even_w = lax.rem(lax.axis_index("wide"), 2) == 0
    even_d = lax.rem(lax.axis_index("depth"), 2) == 0
    out, into = face(z, rate, upwind, t, 0, z.x - 1)
    for c in range(nc):
        ahead = plane(z, mobile, c, z.x - 1) * out
        behind = plane(z, mobile, c, 0)
        rows = pl.ds(c * z.z, z.z)
        wide_a[rows, :] = jnp.where(even_w, ahead, behind)
        wide_b[rows, :] = jnp.where(even_w, behind, ahead)
    rows = pl.ds(nc * z.z, z.z)
    wide_a[rows, :] = into
    wide_b[rows, :] = into
    edge = lax.axis_index("depth") < z.depth - 1

    def last_rows(ref, base, h):
        return ref[pl.ds(base + h * SUB * z.z + z.z - 1, SUB, stride=z.z), :]

    for h in range(z.x // SUB):
        g = jnp.where(edge, last_rows(rate, z.cells, h), 0.0)
        u = last_rows(upwind, (t * 3 + 1) * z.cells, h).astype(F32)
        out = g * u
        for c in range(nc):
            ahead = last_rows(mobile, c * z.cells, h) * out
            behind = mobile[pl.ds(c * z.cells + h * SUB * z.z, SUB, stride=z.z), :]
            rows = pl.ds(c * z.x + h * SUB, SUB)
            deep_a[rows, :] = jnp.where(even_d, ahead, behind)
            deep_b[rows, :] = jnp.where(even_d, behind, ahead)
        rows = pl.ds(nc * z.x + h * SUB, SUB)
        deep_a[rows, :] = g - out
        deep_b[rows, :] = g - out


def flash_field(z, moles, mobile, k_ref, low=0, high=None, hop=1):
    excess, first = k_scalars(k_ref, z.nc)
    step = FLASH_PLANES
    high = z.x // step if high is None else high

    def block(n, carry):
        def rows(c):
            return pl.ds(pl.multiple_of(c * z.cells + n * step * z.z, z.z), step * z.z)

        def store(c, v):
            mobile[rows(c), :] = v

        flash_block(lambda c: moles[rows(c), :], store, excess, first, z.nc)
        return carry

    lax.fori_loop(0, -(-(high - low) // hop), lambda i, a: block(low + i * hop, a), 0)


def first_matrix_kernel(
    z, k_ref, slot_ref, block_ref, moles, rate, upwind, mobile, wide_a, wide_b, deep_a, deep_b,
    tab, gather,
):
    tables(z, slot_ref, block_ref, tab, gather)
    flash_field(z, moles, mobile, k_ref)
    matrix_messages(z, mobile, rate, upwind, 0, wide_a, wide_b, deep_a, deep_b)


def frac_messages(z, mobile, coef, tab, t, frac_a, frac_b):
    even = lax.rem(lax.axis_index("wide"), 2) == 0
    last = lax.axis_index("wide") == z.wide - 1
    here = (tab[pl.ds(2 * SUB, 2 * SUB), :] >= 0).astype(F32)
    out = plane(z, coef, 1, z.x - 1) * plane(z, coef, 4 + 3 * t, z.x - 1)
    into = plane(z, coef, 1, z.x - 1) - out
    out = jnp.where(last, 0.0, out)
    into = jnp.where(last, 0.0, into)
    for c in range(z.nc):
        ahead = plane(z, mobile, c, z.x - 1) * out
        behind = plane(z, mobile, c, 0) * here
        rows = pl.ds(c * z.z, z.z)
        frac_a[rows, :] = jnp.where(even, ahead, behind)
        frac_b[rows, :] = jnp.where(even, behind, ahead)
    rows = pl.ds(z.nc * z.z, z.z)
    frac_a[rows, :] = into
    frac_b[rows, :] = into


def unpack_rows(z, tab, recv_hbm, recv, sem, js, moles, coef):
    lane_tile = z.tiles_out * SUB
    stride = len(js) * lane_tile
    reads = [
        pltpu.make_async_copy(
            recv_hbm.at[pl.ds((w * z.jt + j) * lane_tile, lane_tile), :],
            recv.at[pl.ds((w * len(js) + n) * lane_tile, lane_tile), :],
            sem.at[w * len(js) + n],
        )
        for w in range(z.wide)
        for n, j in enumerate(js)
    ]
    for read in reads:
        read.start()
    from_sub = [tab[pl.ds(h * SUB, SUB), :] for h in range(2)]
    shift = [tab[pl.ds(2 * SUB + h * SUB, SUB), :] for h in range(2)]
    for read in reads:
        read.wait()

    def channel(c, dst, first_row, default):
        for t, j in enumerate(js):
            a = [
                recv[
                    pl.ds(
                        g * SUB * stride + t * lane_tile + c * z.most + k, SUB, stride=stride
                    ),
                    :,
                ]
                for g in range(z.groups)
                for k in range(z.most)
            ]
            for xi, v in enumerate(group_transpose(a, z.ps)):
                rolled = [lane_roll(v, n * z.ps) for n in range(z.by)]
                for h in range(2):
                    got = jnp.full((SUB, LANES), default, F32)
                    for n in range(z.by):
                        got = jnp.where(shift[h] == n, sub_gather(rolled[n], from_sub[h]), got)
                    row = first_row + (z.xt * j + xi) * z.z + h * SUB
                    dst[pl.ds(pl.multiple_of(row, SUB), SUB), :] = got

    def amount(c, carry):
        channel(c, moles, c * z.cells, 1.0)
        return carry

    def weight(c, carry):
        channel(z.nc + c, coef, c * z.cells, jnp.where(c == 0, 1.0, 0.0))
        return carry

    unroll = max(1, 8 // len(js))
    lax.fori_loop(0, z.nc, amount, 0, unroll=unroll)
    lax.fori_loop(0, z.coefs, weight, 0, unroll=2)


def frac_edge_kernel(z, k_ref, tab, recv_hbm, moles, mobile, coef, frac_a, frac_b, recv, sem):
    unpack_rows(z, tab, recv_hbm, recv, sem, (0, z.jt - 1), moles, coef)
    last = z.x // FLASH_PLANES
    flash_field(z, moles, mobile, k_ref, 0, last, last - 1)
    frac_messages(z, mobile, coef, tab, 0, frac_a, frac_b)


def frac_inner_kernel(
    z, k_ref, tab, recv_hbm, moles_in, mobile_in, coef_in, moles, mobile, coef, recv, sem
):
    unpack_rows(z, tab, recv_hbm, recv, sem, tuple(range(1, z.jt - 1)), moles, coef)
    flash_field(z, moles, mobile, k_ref, 1, z.x // FLASH_PLANES - 1)


def each_plane(z, at, streams=()):
    def arrived(x):
        for n in range(1, PARTS):

            @pl.when(x == n * z.x // PARTS - 1)
            def _(n=n):
                for copies in streams:
                    copies[n].wait()

    def middle(x, carry):
        if streams:
            arrived(x)
        at(x, False, False)
        return carry

    for copies in streams:
        copies[0].wait()
    at(0, True, False)
    lax.fori_loop(1, z.x - 1, middle, 0)
    at(z.x - 1, False, True)


def matrix_update(z, t, moles, mobile, rate, upwind, pore, halos, new, mobile_f=None, coef=None,
                  streams=()):
    *wide, deep_a, deep_b = halos
    wide_a, wide_b = wide or (None, None)
    nc = z.nc
    even_w = lax.rem(lax.axis_index("wide"), 2) == 0
    even_d = lax.rem(lax.axis_index("depth"), 2) == 0
    sub = iota((z.z, LANES), 0)

    def side(a, b, first, row, count):
        rows = pl.ds(row, count)
        even = even_w if a is wide_a else even_d
        if first:
            return jnp.where(even, b[rows, :], a[rows, :])
        return jnp.where(even, a[rows, :], b[rows, :])

    def at(x, low, high):
        inv = 1.0 / plane(z, pore, 0, x)
        ox, ix = face(z, rate, upwind, t, 0, x)
        oz, iz = face(z, rate, upwind, t, 1, x)
        oy, iy = face(z, rate, upwind, t, 2, x)
        if low:
            pox, pix = (1.0, side(wide_a, wide_b, True, nc * z.z, z.z)) if wide else (0.0, 0.0)
        else:
            pox, pix = face(z, rate, upwind, t, 0, x - 1)
        wz = jnp.broadcast_to(side(deep_a, deep_b, True, nc * z.x + x, 1), (z.z, LANES))
        poz = jnp.where(sub == 0, 1.0, pltpu.roll(oz, 1, 0))
        piz = jnp.where(sub == 0, wz, pltpu.roll(iz, 1, 0))
        poy, piy = lane_roll(oy, 1), lane_roll(iy, 1)
        own = ox + pix + oz + piz + oy + piy
        if coef is not None:
            w2, w5 = exchange_weights(z, t, coef, x)
            own = own + w2
            w5 = w5 * inv
        own = own * inv
        ax, bx = ix * inv, pox * inv
        az, bz = iz * inv, poz * inv
        ay, by = iy * inv, poy * inv
        for c in range(nc):
            g = plane(z, mobile, c, x)
            v = plane(z, moles, c, x) - own * g
            if not low:
                v = v + bx * plane(z, mobile, c, x - 1)
            elif wide:
                v = v + bx * side(wide_a, wide_b, True, c * z.z, z.z)
            if not high:
                v = v + ax * plane(z, mobile, c, x + 1)
            elif wide:
                v = v + ax * side(wide_a, wide_b, False, c * z.z, z.z)
            hz0 = jnp.broadcast_to(side(deep_a, deep_b, True, c * z.x + x, 1), (z.z, LANES))
            hz1 = jnp.broadcast_to(side(deep_a, deep_b, False, c * z.x + x, 1), (z.z, LANES))
            zb = jnp.where(sub == 0, hz0, pltpu.roll(g, 1, 0))
            za = jnp.where(sub == z.z - 1, hz1, pltpu.roll(g, z.z - 1, 0))
            v = v + (az * za + bz * zb)
            v = v + (ay * lane_roll(g, -1) + by * lane_roll(g, 1))
            if coef is not None:
                v = v + w5 * plane(z, mobile_f, c, x)
            new[pl.ds(pl.multiple_of(c * z.cells + x * z.z, z.z), z.z), :] = v

    each_plane(z, at, streams)


def exchange_weights(z, t, coef, x):
    g = plane(z, coef, 3, x)
    into = g * plane(z, coef, 4 + 3 * t + 2, x)
    return into, g - into


def matrix_early_kernel(
    z, t, moles, mobile, rate, upwind, pore, hc, hd, new, stage, sem
):
    matrix_update(z, t, moles, mobile, rate, upwind, pore, (hc, hd), stage)
    writes = [
        pltpu.make_async_copy(stage.at[rows, :], new.at[rows, :], sem.at[n])
        for n, rows in enumerate(
            pl.ds(n * z.nc * z.cells // PARTS, z.nc * z.cells // PARTS) for n in range(PARTS)
        )
    ]
    for copy in writes:
        copy.start()
    for copy in writes:
        copy.wait()


def matrix_kernel(
    z, t, k_ref, early, mobile_hbm, mobile_f, coef, rate, upwind, pore, ha, hb, new,
    mobile_new, wide_a, wide_b, deep_a, deep_b, moles, mobile, sem,
):
    streams = (stream(z, early, moles, sem.at[0]), stream(z, mobile_hbm, mobile, sem.at[1]))
    for n in range(PARTS):
        for copies in streams:
            copies[n].start()

    even = lax.rem(lax.axis_index("wide"), 2) == 0

    def side(first, row):
        rows = pl.ds(row, z.z)
        if first:
            return jnp.where(even, hb[rows, :], ha[rows, :])
        return jnp.where(even, ha[rows, :], hb[rows, :])

    def at(x, low, high):
        inv = 1.0 / plane(z, pore, 0, x)
        w2, w5 = exchange_weights(z, t, coef, x)
        if low:
            w2 = w2 + side(True, z.nc * z.z)
        w2, w5 = w2 * inv, w5 * inv
        ax = face(z, rate, upwind, t, 0, x)[1] * inv if high else None
        for c in range(z.nc):
            v = plane(z, moles, c, x) - w2 * plane(z, mobile, c, x)
            v = v + w5 * plane(z, mobile_f, c, x)
            if low:
                v = v + inv * side(True, c * z.z)
            if high:
                v = v + ax * side(False, c * z.z)
            new[pl.ds(pl.multiple_of(c * z.cells + x * z.z, z.z), z.z), :] = v

    each_plane(z, at, streams)
    flash_field(z, new, mobile_new, k_ref)
    matrix_messages(z, mobile_new, rate, upwind, t + 1, wide_a, wide_b, deep_a, deep_b)


def last_matrix_kernel(
    z, t, moles_hbm, mobile_hbm, mobile_f_hbm, coef, rate, upwind, pore, ha, hb, hc, hd, new,
    moles, mobile, mobile_f, sem,
):
    streams = tuple(
        stream(z, src, dst, sem.at[n])
        for n, (src, dst) in enumerate(
            ((moles_hbm, moles), (mobile_hbm, mobile), (mobile_f_hbm, mobile_f))
        )
    )
    for n in range(PARTS):
        for copies in streams:
            copies[n].start()
    matrix_update(
        z, t, moles, mobile, rate, upwind, pore, (ha, hb, hc, hd), new, mobile_f, coef, streams
    )


def frac_update(z, t, tab, moles, mobile, mobile_m, coef, frac_a, frac_b, new, streams=()):
    nc = z.nc
    even = lax.rem(lax.axis_index("wide"), 2) == 0
    here = (tab[pl.ds(2 * SUB, 2 * SUB), :] >= 0).astype(F32)
    beyond = tab[pl.ds(4 * SUB, 2 * SUB), :].astype(F32)
    lane = iota((z.z, LANES), 1)
    next_y = jnp.where(lane == LANES - 1, 0.0, lane_roll(here, -1))

    def side(first, row):
        rows = pl.ds(row, z.z)
        if first:
            return jnp.where(even, frac_b[rows, :], frac_a[rows, :])
        return jnp.where(even, frac_a[rows, :], frac_b[rows, :])

    def split(x, d, mask):
        g = plane(z, coef, 1 + d, x) * mask
        out = g * plane(z, coef, 4 + 3 * t + d, x)
        return out, g - out

    def at(x, low, high):
        inv = 1.0 / plane(z, coef, 0, x)
        ox, ix = split(x, 0, beyond if high else here)
        if low:
            pox, pix = here, side(True, nc * z.z) * here
        else:
            pox, pix = split(x - 1, 0, here)
        oy, iy = split(x, 1, next_y)
        poy, piy = lane_roll(oy, 1), lane_roll(iy, 1)
        w2, w5 = split(x, 2, 1.0)
        own = (ox + pix + oy + piy + w5) * inv
        ax, bx = ix * inv, pox * inv
        ay, by = iy * inv, poy * inv
        w2 = w2 * inv
        for c in range(nc):
            g = plane(z, mobile, c, x)
            before = side(True, c * z.z) if low else plane(z, mobile, c, x - 1)
            after = side(False, c * z.z) if high else plane(z, mobile, c, x + 1)
            v = plane(z, moles, c, x) - own * g + (ax * after + bx * before)
            v = v + (ay * lane_roll(g, -1) + by * lane_roll(g, 1))
            v = v + w2 * plane(z, mobile_m, c, x)
            new[pl.ds(pl.multiple_of(c * z.cells + x * z.z, z.z), z.z), :] = v

    each_plane(z, at, streams)


def frac_kernel(
    z, t, k_ref, tab, moles, mobile, mobile_hbm, coef, fa, fb, new, mobile_new, frac_a, frac_b,
    mobile_m, sem,
):
    copies = stream(z, mobile_hbm, mobile_m, sem)
    for copy in copies:
        copy.start()
    frac_update(z, t, tab, moles, mobile, mobile_m, coef, fa, fb, new, (copies,))
    flash_field(z, new, mobile_new, k_ref)
    frac_messages(z, mobile_new, coef, tab, t + 1, frac_a, frac_b)


def last_frac_kernel(
    z, t, tab, gather, moles, mobile, mobile_m, coef, fa, fb, back, new, stage, sem
):
    frac_update(z, t, tab, moles, mobile, mobile_m, coef, fa, fb, new)
    maps = gather[:, : 3 * z.blocks].astype(jnp.bfloat16)

    def channel(c, carry):
        field_to_rows(z, new, c * z.cells, maps, stage, c)
        return carry

    lax.fori_loop(0, z.nc, channel, 0, unroll=4)
    copy = pltpu.make_async_copy(stage, back, sem)
    copy.start()
    copy.wait()


def swap(value, axis, ahead, ends=True):
    count = lax.axis_size(axis)
    if ahead:
        pairs = [(i, i ^ 1) for i in range(count)]
    else:
        pairs = [(i, i - 1 if i % 2 == 0 else i + 1) for i in range(count)]
        pairs = [(i, n % count) for i, n in pairs if ends or 0 <= n < count]
    return lax.ppermute(value, axis, pairs)


def call(
    kernel, in_specs, out_shape, args, scratch=(), mib=12, out_specs=None, kept=(),
    aliases=None,
):
    body = kernel
    if kept:
        kept = in_vmem(*kept)
        at, count = len(args), len(kept)
        body = lambda *refs: kernel(*refs[:at], *refs[at + count :])
        args = (*args, *kept)
        in_specs = in_specs + [VMEM] * count
    return pl.pallas_call(
        body,
        out_shape=out_shape,
        in_specs=in_specs,
        out_specs=out_specs or (
            (VMEM,) * len(out_shape) if isinstance(out_shape, tuple) else VMEM
        ),
        scratch_shapes=scratch,
        input_output_aliases=aliases or {},
        compiler_params=pltpu.CompilerParams(vmem_limit_bytes=mib << 20),
        cost_estimate=pl.CostEstimate(
            flops=10**8, bytes_accessed=sum(a.size * 4 for a in args), transcendentals=0
        ),
    )(*args)


def shape(rows, lanes=LANES, space=pltpu.VMEM):
    return space((rows, lanes), F32)


def in_vmem(*values):
    return tuple(pltpu.with_memory_space_constraint(v, pltpu.VMEM) for v in values)


def in_hbm(v):
    return pltpu.with_memory_space_constraint(v, pltpu.HBM)


def local(
    matrix_moles,
    pore_matrix,
    matrix_rate,
    matrix_upwind,
    frac_moles,
    pore_frac,
    frac_rate,
    frac_upwind,
    ff_open,
    kvalues,
    slot_patch,
    patch_block,
):
    z = Sizes(matrix_moles, frac_moles)
    bind = lambda f, *a: functools.partial(f, z, *a)
    blocks, slot_patch, kvalues = in_hbm(patch_block.T), in_hbm(slot_patch), in_hbm(kvalues)
    moles = matrix_moles.reshape(-1, z.y)
    pore = pore_matrix.reshape(-1, z.y)
    rate = matrix_rate.reshape(-1, z.y)
    upwind = matrix_upwind.reshape(-1, z.y)
    field = shape(z.nc * z.cells)
    msg_w, msg_d = shape((z.nc + 1) * z.z), shape((z.nc + 1) * z.x)
    rows_out = z.wide * z.jt * z.tiles_out * SUB
    rows_back = z.wide * z.jt * z.tiles_back * SUB
    src_rows = z.tiles_out * z.cpt * z.slots
    hbm_field = shape(z.nc * z.cells, space=pltpu.HBM)
    stacked = lambda v: in_hbm(v.reshape(z.nc, z.cells, LANES))
    stream_buf = pltpu.VMEM((z.nc, z.cells, LANES), F32)

    send = call(
        bind(pack_kernel), [SMEM] * 3 + [HBM] * 4,
        shape(rows_out, space=pltpu.HBM),
        (
            slot_patch,
            blocks,
            in_hbm(ff_open.T),
            in_hbm(frac_moles.reshape(-1, z.pc)),
            in_hbm(pore_frac),
            in_hbm(frac_rate.reshape(-1, z.pc)),
            in_hbm(frac_upwind.reshape(-1, z.pc)),
        ),
        scratch=[
            pltpu.VMEM((src_rows, z.pc), F32),
            pltpu.VMEM((3 * SUBSTEPS * z.slots, z.pc), I32),
            pltpu.VMEM((rows_out, LANES), F32),
            pltpu.SemaphoreType.DMA((4,)),
            pltpu.SemaphoreType.DMA((z.cols,)),
        ],
        out_specs=HBM,
    )

    def trade(v):
        return lax.all_to_all(v, "wide", split_axis=0, concat_axis=0, tiled=True)

    def exchange(a, b, axis):
        return swap(a, axis, True), swap(b, axis, False, axis == "wide")

    recv = trade(send)
    mobile_m, wa, wb, da, db, tab, gather = call(
        bind(first_matrix_kernel), [SMEM] * 3 + [VMEM] * 3,
        (
            field, msg_w, msg_w, msg_d, msg_d, pltpu.VMEM((6 * SUB, LANES), I32),
            shape(z.places, -(-3 * z.blocks // LANES) * LANES),
        ),
        (kvalues, slot_patch, blocks, *in_vmem(moles, rate, upwind)),
    )
    wide_halos = exchange(wa, wb, "wide")
    deep_halos = exchange(da, db, "depth")
    early = call(
        bind(matrix_early_kernel, 0), [VMEM] * 7, hbm_field,
        in_vmem(moles, mobile_m, rate, upwind, pore, *deep_halos),
        scratch=[
            pltpu.VMEM((z.nc * z.cells, LANES), F32), pltpu.SemaphoreType.DMA((PARTS,))
        ],
        out_specs=HBM,
    )
    coef_field = shape(z.coefs * z.cells)
    tiles = z.wide * z.tiles_out * SUB
    moles_f, mobile_f, coef, fa, fb = call(
        bind(frac_edge_kernel), [SMEM, VMEM, HBM],
        (field, field, coef_field, msg_w, msg_w),
        (kvalues, *in_vmem(tab), in_hbm(recv)),
        scratch=[pltpu.VMEM((2 * tiles, LANES), F32), pltpu.SemaphoreType.DMA((2 * z.wide,))],
    )
    fa, fb = exchange(fa, fb, "wide")
    inner = z.jt - 2
    moles_f, mobile_f, coef = call(
        bind(frac_inner_kernel), [SMEM, VMEM, HBM] + [VMEM] * 3,
        (field, field, coef_field),
        (kvalues, *in_vmem(tab), in_hbm(recv), *in_vmem(moles_f, mobile_f, coef)),
        scratch=[
            pltpu.VMEM((inner * tiles, LANES), F32),
            pltpu.SemaphoreType.DMA((inner * z.wide,)),
        ],
        aliases={3: 0, 4: 1, 5: 2},
    )
    new_f, new_mobile_f, fa, fb = call(
        bind(frac_kernel, 0), [SMEM] + [VMEM] * 3 + [HBM] + [VMEM] * 3,
        (field, field, msg_w, msg_w),
        (
            kvalues, *in_vmem(tab, moles_f, mobile_f), stacked(mobile_m),
            *in_vmem(coef, fa, fb),
        ),
        scratch=[stream_buf, pltpu.SemaphoreType.DMA((PARTS,))],
        kept=(rate, upwind, pore),
    )
    fa, fb = exchange(fa, fb, "wide")
    moles, mobile_m, wa, wb, da, db = call(
        bind(matrix_kernel, 0), [SMEM] + [HBM] * 2 + [VMEM] * 7,
        (field, field, msg_w, msg_w, msg_d, msg_d),
        (
            kvalues, stacked(early), stacked(mobile_m),
            *in_vmem(mobile_f, coef, rate, upwind, pore, *wide_halos),
        ),
        scratch=[stream_buf, stream_buf, pltpu.SemaphoreType.DMA((2, PARTS))],
        kept=(new_f, new_mobile_f, tab),
    )
    wide_halos = exchange(wa, wb, "wide")
    deep_halos = exchange(da, db, "depth")
    t = SUBSTEPS - 1
    back = call(
        bind(last_frac_kernel, t), [VMEM] * 8,
        shape(rows_back, space=pltpu.HBM),
        in_vmem(tab, gather, new_f, new_mobile_f, mobile_m, coef, fa, fb),
        scratch=[
            pltpu.VMEM((z.nc * z.cells, LANES), F32),
            pltpu.VMEM((rows_back, LANES), F32),
            pltpu.SemaphoreType.DMA,
        ],
        out_specs=HBM,
    )
    returned = trade(back)
    moles = call(
        bind(last_matrix_kernel, t), [HBM] * 3 + [VMEM] * 8,
        jax.ShapeDtypeStruct((z.nc * z.cells, LANES), F32),
        (
            stacked(moles), stacked(mobile_m), stacked(new_mobile_f),
            *in_vmem(coef, rate, upwind, pore, *wide_halos, *deep_halos),
        ),
        scratch=[stream_buf] * 3 + [pltpu.SemaphoreType.DMA((3, PARTS))],
    )
    frac = call(
        bind(spread_kernel), [SMEM] * 2 + [HBM],
        jax.ShapeDtypeStruct((z.nc * z.slots, z.pc), F32),
        (slot_patch, blocks, in_hbm(returned)),
        scratch=[pltpu.VMEM((rows_back, LANES), F32), pltpu.SemaphoreType.DMA],
    )
    return moles.reshape(matrix_moles.shape), frac.reshape(frac_moles.shape)


def solution(mesh):
    placed = (
        P(None, "wide", "depth", None),
        P("wide", "depth", None),
        P(None, "wide", "depth", None),
        P(None, None, "wide", "depth", None),
        P(None, ("wide", "depth"), None),
        P(("wide", "depth"), None),
        P(None, ("wide", "depth"), None),
        P(None, None, ("wide", "depth"), None),
        P(("wide", "depth"), None),
        P(),
        P(),
        P(),
    )
    return jax.shard_map(
        local,
        mesh=mesh,
        in_specs=placed,
        out_specs=(P(None, "wide", "depth", None), P(None, ("wide", "depth"), None)),
        check_vma=False,
    )
```

```python
import functools

import jax
import jax.numpy as jnp
from jax import lax
from jax.experimental import pallas as pl
from jax.experimental.pallas import tpu as pltpu
from jax.sharding import PartitionSpec as P


SWEEPS = 4
SUBSTEPS = 2
MOBILITY_RATIO = 4.0
NEVER = 1e30
LANES = 128
SUB = 8
PARTS = 4
FLASH_PLANES = 2
F32 = jnp.float32
I32 = jnp.int32


VMEM = pl.BlockSpec(memory_space=pltpu.VMEM)
SMEM = pl.BlockSpec(memory_space=pltpu.SMEM)
HBM = pl.BlockSpec(memory_space=pltpu.HBM)


class Sizes:
    def __init__(self, matrix_moles, frac_moles):
        self.wide = lax.axis_size("wide")
        self.depth = lax.axis_size("depth")
        self.nc, self.x, self.z, self.y = matrix_moles.shape
        self.slots, self.pc = frac_moles.shape[1:]
        self.ps = 1
        while self.ps * self.ps < self.pc:
            self.ps *= 2
        self.by = self.y // self.ps
        self.half = self.pc // 2
        self.most = max(1, 4 * self.slots // self.wide)
        self.cpt = SUB // self.most
        self.coefs = 4 + 3 * SUBSTEPS
        self.out_ch = self.nc + self.coefs
        self.tiles_out = -(-self.out_ch // self.cpt)
        self.tiles_back = -(-self.nc // self.cpt)
        self.groups = self.wide // SUB
        self.cells = self.x * self.z
        self.places = SUB * self.by
        self.blocks = self.z * self.by
        self.xt = LANES // self.ps
        self.jt = self.half // LANES
        assert self.y == LANES and self.slots == SUB and self.z == 2 * SUB
        assert self.x * self.ps == self.half and self.groups * self.most == self.xt == self.by


def iota(shape, dim):
    return lax.broadcasted_iota(I32, shape, dim)


def lane_roll(v, by):
    by = by % LANES
    return v if by == 0 else pltpu.roll(v, by, 1)


def sub_gather(v, idx):
    return jnp.take_along_axis(v, idx, axis=0, mode="promise_in_bounds")


def group_transpose(a, ps):
    grp = iota((SUB, LANES), 1) // ps
    odd, high = (grp & 1) == 1, (grp & 2) == 2

    def pair(u, v, upper, dist):
        return (
            jnp.where(upper, lane_roll(v, dist), u),
            jnp.where(upper, v, lane_roll(u, -dist)),
        )

    b0, b1 = pair(a[0], a[1], odd, ps)
    c0, c1 = pair(a[2], a[3], odd, ps)
    t0, t2 = pair(b0, c0, high, 2 * ps)
    t1, t3 = pair(b1, c1, high, 2 * ps)
    return [t0, t1, t2, t3]


def tree_sum(terms):
    terms = list(terms)
    while len(terms) > 1:
        terms = [a + b for a, b in zip(terms[::2], terms[1::2])] + (
            [terms[-1]] if len(terms) % 2 else []
        )
    return terms[0]


def flash_block(load, store, inverse, first, nc):
    total = tree_sum([load(c) for c in range(nc)])
    vapour = None
    for _ in range(SWEEPS):
        misfits, slopes = [], []
        for c in range(nc):
            p = first[c] if vapour is None else 1.0 / (vapour + inverse[c])
            r = load(c) * p
            misfits.append(r)
            slopes.append(r * p)
        misfit, slope = running(misfits), running(slopes)
        before = 0.5 if vapour is None else vapour
        vapour = jnp.clip(before + misfit / (slope + total), 0.0, 1.0)
    liquid = (1.0 - vapour) * (1.0 - vapour)
    gas = MOBILITY_RATIO * vapour * vapour
    share = gas / (liquid + gas)
    for c in range(nc):
        p = 1.0 / (vapour + inverse[c])
        store(c, load(c) * p * (share + inverse[c]))


def running(terms):
    sums = [terms[0], terms[1]]
    for n, t in enumerate(terms[2:]):
        sums[n % 2] = sums[n % 2] + t
    return sums[0] + sums[1]


def k_scalars(k_ref, nc):
    inverse, first = [], []
    for c in range(nc):
        e = jnp.full((1, LANES), k_ref[c], F32) - 1.0
        inverse.append(jnp.where(e == 0.0, NEVER, 1.0 / e))
        first.append(1.0 / (0.5 + inverse[c]))
    return inverse, first


def own_slots(z, slot_ref, block_ref, visit):
    me = lax.axis_index("wide") * z.depth + lax.axis_index("depth")
    counts = jnp.int32(0)
    for i in range(z.slots):
        q = slot_ref[me * z.slots + i]
        p0 = block_ref[0, q]
        rank = (counts >> (4 * p0)) & 15
        counts = counts + (jnp.int32(1) << (4 * p0))
        visit(i, p0, rank)


def pack_kernel(
    z, slot_ref, block_ref, open_ref, moles, pore, rate, upwind, *refs
):
    outs, (src, flags, in_sem) = refs[: z.wide], refs[z.wide :]
    nc, slots = z.nc, z.slots
    first = nc * slots
    reads = [
        pltpu.make_async_copy(moles, src.at[pl.ds(0, first), :], in_sem.at[0]),
        pltpu.make_async_copy(pore, src.at[pl.ds(first, slots), :], in_sem.at[1]),
        pltpu.make_async_copy(rate, src.at[pl.ds(first + slots, 3 * slots), :], in_sem.at[2]),
        pltpu.make_async_copy(upwind, flags, in_sem.at[3]),
    ]
    for copy in reads:
        copy.start()
    sub = iota((SUB, LANES), 0)
    picks = [jnp.zeros((SUB, LANES), I32) for _ in range(z.wide)]
    target = [lax.rem(lax.axis_index("wide") + s, z.wide) for s in range(z.wide)]
    opens = [jnp.zeros((SUB, z.pc), I32) for _ in range(2)]
    row_id = iota((SUB, z.pc), 0)

    def visit(i, p0, rank):
        for s in range(z.wide):
            hit = (sub % z.most) == jnp.where(p0 == lax.div(target[s], 2), rank, -1)
            picks[s] = jnp.where(hit, i, picks[s])
        for d in range(2):
            opens[d] = jnp.where(row_id == i, open_ref[d, i], opens[d])

    own_slots(z, slot_ref, block_ref, visit)

    for copy in reads:
        copy.wait()
    cell = iota((slots, z.pc), 1)
    g = first + slots
    open_x = jnp.where(cell // z.ps < z.ps - 1, 1, opens[0]).astype(F32)
    open_y = jnp.where(cell % z.ps < z.ps - 1, 1, opens[1]).astype(F32)
    src[pl.ds(g, slots), :] = src[pl.ds(g, slots), :] * open_x
    src[pl.ds(g + slots, slots), :] = src[pl.ds(g + slots, slots), :] * open_y
    n_flags = 3 * SUBSTEPS * slots
    src[pl.ds(g + 3 * slots, n_flags), :] = flags[...].astype(F32)
    spare = src.shape[0] - (g + 3 * slots + n_flags)
    if spare:
        src[pl.ds(g + 3 * slots + n_flags, spare), :] = jnp.zeros((spare, z.pc), F32)

    def tile(m, carry):
        for s in range(z.wide):
            left = lax.rem(target[s], 2) * z.half
            for j in range(z.jt):
                lanes = pl.ds(pl.multiple_of(left + j * LANES, LANES), LANES)
                v = None
                for cp in range(z.cpt):
                    rows = pl.ds(pl.multiple_of((m * z.cpt + cp) * slots, slots), slots)
                    part = sub_gather(src[rows, lanes], picks[s])
                    v = part if v is None else jnp.where(sub // z.most >= cp, part, v)
                row = (j * z.tiles_out + m) * SUB
                outs[s][pl.ds(pl.multiple_of(row, SUB), SUB), :] = v
        return carry

    lax.fori_loop(0, z.tiles_out, tile, 0)


def sender(z, s):
    return lax.rem(lax.axis_index("wide") + (z.wide - s), z.wide)


def spread_kernel(z, slot_ref, block_ref, *refs):
    chunks, out = refs[: z.wide], refs[z.wide]
    sub = iota((SUB, LANES), 0)
    ranks = jnp.zeros((SUB, LANES), I32)
    column = jnp.zeros((SUB, LANES), I32)

    def visit(i, p0, rank):
        nonlocal ranks, column
        ranks = jnp.where(sub == i, rank, ranks)
        column = jnp.where(sub == i, p0, column)

    own_slots(z, slot_ref, block_ref, visit)
    for s in range(z.wide):
        source = sender(z, s)
        left = lax.rem(source, 2) * z.half
        hit = column == lax.div(source, 2)

        def tile(m, carry, s=s, left=left, hit=hit):
            for j in range(z.jt):
                row = (j * z.tiles_back + m) * SUB
                part = chunks[s][pl.ds(pl.multiple_of(row, SUB), SUB), :]
                lanes = pl.ds(pl.multiple_of(left + j * LANES, LANES), LANES)
                for cp in range(z.cpt):
                    rows = pl.ds(pl.multiple_of((m * z.cpt + cp) * SUB, SUB), SUB)
                    out[rows, lanes] = jnp.where(
                        hit, sub_gather(part, cp * z.most + ranks), out[rows, lanes]
                    )
            return carry

        lax.fori_loop(0, z.tiles_back, tile, 0, unroll=2)


def tables(z, slot_ref, block_ref, tab, gather):
    sub, grp = iota((SUB, LANES), 0), iota((SUB, LANES), 1) // z.ps
    bid = [(sub + SUB * h) * z.by + grp for h in range(2)]
    wide, deep = lax.axis_index("wide"), lax.axis_index("depth")
    here, after = wide // 2, jnp.where(wide + 1 < z.wide, (wide + 1) // 2, -1)

    def visit(w, state):
        v0, v1, n0, n1 = state
        counts = jnp.int32(0)
        for i in range(z.slots):
            q = slot_ref[(w * z.depth + deep) * z.slots + i]
            p0 = block_ref[0, q]
            block = lax.rem(block_ref[1, q], z.z) * z.by + block_ref[2, q]
            rank = (counts >> (4 * p0)) & 15
            counts = counts + (jnp.int32(1) << (4 * p0))
            place = lax.rem(w, SUB) + SUB * (lax.div(w, SUB) * z.most + rank)
            b_here = jnp.where(p0 == here, block, -1)
            b_next = jnp.where(p0 == after, block, -1)
            v0 = jnp.where(bid[0] == b_here, place, v0)
            v1 = jnp.where(bid[1] == b_here, place, v1)
            n0 = jnp.where(bid[0] == b_next, 1, n0)
            n1 = jnp.where(bid[1] == b_next, 1, n1)
            column = lax.rem(block, z.by) * z.z + lax.div(block, z.by)

            @pl.when(p0 == here)
            def _():
                gather[pl.ds(place, 1), :] = (
                    (lane % z.blocks == column) & (lane < 3 * z.blocks)
                ).astype(F32)

        return v0, v1, n0, n1

    gather[...] = jnp.zeros(gather.shape, F32)
    lane = iota((1, gather.shape[1]), 1)
    zero = jnp.zeros((SUB, LANES), I32)
    v0, v1, n0, n1 = lax.fori_loop(0, z.wide, visit, (zero - 1, zero - 1, zero, zero))
    for h, (v, n) in enumerate(((v0, n0), (v1, n1))):
        rows = pl.ds(h * SUB, SUB)
        tab[rows, :] = jnp.where(v >= 0, v & (SUB - 1), 0)
        tab[pl.ds(2 * SUB + h * SUB, SUB), :] = jnp.where(
            v >= 0, (grp - (v >> 3)) & (z.by - 1), -1
        )
        tab[pl.ds(4 * SUB + h * SUB, SUB), :] = n


def split3(v):
    hi = v.astype(jnp.bfloat16)
    rest = v - hi.astype(F32)
    mid = rest.astype(jnp.bfloat16)
    low = (rest - mid.astype(F32)).astype(jnp.bfloat16)
    return jnp.concatenate([hi, mid, low], axis=0)


def field_to_rows(z, src, first_row, gather, back, c):
    lane_tile = z.tiles_back * SUB
    stride = z.jt * lane_tile
    for jj in range(0, z.jt, 2):
        columns = []
        for n in range(2):
            parts = [None] * (z.by * (z.z // SUB))
            for h in range(z.z // SUB):
                tiles_x = []
                for xi in range(z.xt):
                    row = first_row + (z.xt * (jj + n) + xi) * z.z + h * SUB
                    tiles_x.append(src[pl.ds(pl.multiple_of(row, SUB), SUB), :])
                for p, v in enumerate(group_transpose(tiles_x, z.ps)):
                    parts[p * (z.z // SUB) + h] = v
            columns.append(jnp.concatenate(parts, axis=0))
        block_rows = jnp.concatenate(columns, axis=1)
        rows = jnp.dot(gather, split3(block_rows), preferred_element_type=F32)
        for n in range(2):
            for i in range(z.by):
                g, k = divmod(i, z.most)
                start = g * SUB * stride + (jj + n) * lane_tile + c * z.most + k
                back[pl.ds(start, SUB, stride=stride), :] = rows[
                    i * SUB : (i + 1) * SUB, n * LANES : (n + 1) * LANES
                ]


def face(z, rate, upwind, t, d, x):
    g = rate[pl.ds(pl.multiple_of(d * z.cells + x * z.z, z.z), z.z), :]
    u = upwind[pl.ds(pl.multiple_of((t * 3 + d) * z.cells + x * z.z, z.z), z.z), :].astype(F32)
    if d == 0:
        keep = (x < z.x - 1) | (lax.axis_index("wide") < z.wide - 1)
    elif d == 1:
        keep = (iota((z.z, LANES), 0) < z.z - 1) | (lax.axis_index("depth") < z.depth - 1)
    else:
        keep = iota((z.z, LANES), 1) < LANES - 1
    g = jnp.where(keep, g, 0.0)
    out = g * u
    return out, g - out


def cells_of(z, ref, c, start, count):
    if len(ref.shape) == 3:
        return ref[c, pl.ds(start, count), :]
    return ref[pl.ds(pl.multiple_of(c * z.cells + start, z.z), count), :]


def plane(z, ref, c, x):
    return cells_of(z, ref, c, pl.multiple_of(x * z.z, z.z), z.z)


def matrix_messages(z, mobile, rate, upwind, t, wide_a, wide_b, deep_a, deep_b):
    nc = z.nc
    even_w = lax.rem(lax.axis_index("wide"), 2) == 0
    even_d = lax.rem(lax.axis_index("depth"), 2) == 0
    out, into = face(z, rate, upwind, t, 0, z.x - 1)
    for c in range(nc):
        ahead = plane(z, mobile, c, z.x - 1) * out
        behind = plane(z, mobile, c, 0)
        rows = pl.ds(c * z.z, z.z)
        wide_a[rows, :] = jnp.where(even_w, ahead, behind)
        wide_b[rows, :] = jnp.where(even_w, behind, ahead)
    rows = pl.ds(nc * z.z, z.z)
    wide_a[rows, :] = into
    wide_b[rows, :] = into
    edge = lax.axis_index("depth") < z.depth - 1

    def last_rows(ref, base, h):
        return ref[pl.ds(base + h * SUB * z.z + z.z - 1, SUB, stride=z.z), :]

    for h in range(z.x // SUB):
        g = jnp.where(edge, last_rows(rate, z.cells, h), 0.0)
        u = last_rows(upwind, (t * 3 + 1) * z.cells, h).astype(F32)
        out = g * u
        for c in range(nc):
            ahead = last_rows(mobile, c * z.cells, h) * out
            behind = mobile[pl.ds(c * z.cells + h * SUB * z.z, SUB, stride=z.z), :]
            rows = pl.ds(c * z.x + h * SUB, SUB)
            deep_a[rows, :] = jnp.where(even_d, ahead, behind)
            deep_b[rows, :] = jnp.where(even_d, behind, ahead)
        rows = pl.ds(nc * z.x + h * SUB, SUB)
        deep_a[rows, :] = g - out
        deep_b[rows, :] = g - out


def flash_field(z, moles, mobile, k_ref, low=0, high=None, hop=1, arrived=None):
    inverse, first = k_scalars(k_ref, z.nc)
    step = FLASH_PLANES
    high = z.x // step if high is None else high

    def block(n, carry):
        if arrived is not None:
            arrived(n * step)
        start = pl.multiple_of(n * step * z.z, step * z.z)

        def store(c, v):
            mobile[pl.ds(pl.multiple_of(c * z.cells + start, z.z), step * z.z), :] = v

        flash_block(
            lambda c: cells_of(z, moles, c, start, step * z.z), store, inverse, first, z.nc
        )
        return carry

    lax.fori_loop(0, -(-(high - low) // hop), lambda i, a: block(low + i * hop, a), 0)


def first_matrix_kernel(
    z, k_ref, slot_ref, block_ref, moles_hbm, rate_hbm, upwind_hbm, pore_hbm,
    mobile, early, wide_a, wide_b, deep_a, deep_b, tab, gather, rate, upwind, pore,
    moles, sem, part_sem,
):
    reads = [
        pltpu.make_async_copy(src, dst, sem.at[n])
        for n, (src, dst) in enumerate(
            ((rate_hbm, rate), (upwind_hbm, upwind), (pore_hbm, pore))
        )
    ]
    planes = z.x // PARTS
    parts = []
    for n in range(PARTS):
        rows = pl.ds(n * planes * z.z, planes * z.z)
        parts.append(
            pltpu.make_async_copy(moles_hbm.at[:, rows, :], moles.at[:, rows, :], part_sem.at[n])
        )
    for read in parts + reads:
        read.start()
    tables(z, slot_ref, block_ref, tab, gather)

    def arrived(x):
        for n, part in enumerate(parts):

            @pl.when(x == n * planes)
            def _(part=part):
                part.wait()

    flash_field(z, moles, mobile, k_ref, arrived=arrived)
    for read in reads:
        read.wait()
    matrix_messages(z, mobile, rate, upwind, 0, wide_a, wide_b, deep_a, deep_b)
    matrix_update(z, 0, moles, mobile, rate, upwind, pore, None, early)


def frac_messages(z, mobile, coef, tab, t, frac_a, frac_b):
    even = lax.rem(lax.axis_index("wide"), 2) == 0
    last = lax.axis_index("wide") == z.wide - 1
    here = (tab[pl.ds(2 * SUB, 2 * SUB), :] >= 0).astype(F32)
    out = plane(z, coef, 1, z.x - 1) * plane(z, coef, 4 + 3 * t, z.x - 1)
    into = plane(z, coef, 1, z.x - 1) - out
    out = jnp.where(last, 0.0, out)
    into = jnp.where(last, 0.0, into)
    for c in range(z.nc):
        ahead = plane(z, mobile, c, z.x - 1) * out
        behind = plane(z, mobile, c, 0) * here
        rows = pl.ds(c * z.z, z.z)
        frac_a[rows, :] = jnp.where(even, ahead, behind)
        frac_b[rows, :] = jnp.where(even, behind, ahead)
    rows = pl.ds(z.nc * z.z, z.z)
    frac_a[rows, :] = into
    frac_b[rows, :] = into


def staged(z, chunks, js, recv, sem):
    lane_tile = z.tiles_out * SUB
    return [
        pltpu.make_async_copy(
            chunks[s].at[pl.ds(j * lane_tile, lane_tile), :],
            recv.at[pl.ds((sender(z, s) * len(js) + n) * lane_tile, lane_tile), :],
            sem.at[s * len(js) + n],
        )
        for s in range(z.wide)
        for n, j in enumerate(js)
    ]


def unpack_rows(z, tab, recv, js, moles, coef):
    lane_tile = z.tiles_out * SUB
    stride = len(js) * lane_tile
    from_sub = [tab[pl.ds(h * SUB, SUB), :] for h in range(2)]
    shift = [tab[pl.ds(2 * SUB + h * SUB, SUB), :] for h in range(2)]

    def channel(c, dst, first_row, default):
        for t, j in enumerate(js):
            a = [
                recv[
                    pl.ds(
                        g * SUB * stride + t * lane_tile + c * z.most + k, SUB, stride=stride
                    ),
                    :,
                ]
                for g in range(z.groups)
                for k in range(z.most)
            ]
            for xi, v in enumerate(group_transpose(a, z.ps)):
                rolled = [lane_roll(v, n * z.ps) for n in range(z.by)]
                for h in range(2):
                    got = jnp.full((SUB, LANES), default, F32)
                    for n in range(z.by):
                        got = jnp.where(shift[h] == n, sub_gather(rolled[n], from_sub[h]), got)
                    row = first_row + (z.xt * j + xi) * z.z + h * SUB
                    dst[pl.ds(pl.multiple_of(row, SUB), SUB), :] = got

    def amount(c, carry):
        channel(c, moles, c * z.cells, 1.0)
        return carry

    def weight(c, carry):
        channel(z.nc + c, coef, c * z.cells, jnp.where(c == 0, 1.0, 0.0))
        return carry

    unroll = max(1, 8 // len(js))
    lax.fori_loop(0, z.nc, amount, 0, unroll=unroll)
    lax.fori_loop(0, z.coefs, weight, 0, unroll=2)


def frac_edge_kernel(z, k_ref, tab, *refs):
    chunks, refs = refs[: z.wide], refs[z.wide :]
    moles, mobile, coef, frac_a, frac_b, recv_inner, recv, sem, sem_inner = refs
    edge = (0, z.jt - 1)
    now = staged(z, chunks, edge, recv, sem)
    later = staged(z, chunks, tuple(range(1, z.jt - 1)), recv_inner, sem_inner)
    for read in now:
        read.start()
    for read in now:
        read.wait()
    for read in later:
        read.start()
    unpack_rows(z, tab, recv, edge, moles, coef)
    last = z.x // FLASH_PLANES
    flash_field(z, moles, mobile, k_ref, 0, last, last - 1)
    frac_messages(z, mobile, coef, tab, 0, frac_a, frac_b)
    for read in later:
        read.wait()


def frac_inner_kernel(z, k_ref, tab, recv, moles_in, mobile_in, coef_in, moles, mobile, coef):
    unpack_rows(z, tab, recv, tuple(range(1, z.jt - 1)), moles, coef)
    flash_field(z, moles, mobile, k_ref, 1, z.x // FLASH_PLANES - 1)


def each_plane(z, at):
    def middle(x, carry):
        at(x, False, False)
        return carry

    at(0, True, False)
    lax.fori_loop(1, z.x - 1, middle, 0)
    at(z.x - 1, False, True)


def matrix_update(z, t, moles, mobile, rate, upwind, pore, halos, new, mobile_f=None, coef=None):
    wide_a, wide_b, deep_a, deep_b = halos or (None,) * 4
    nc = z.nc
    even_w = lax.rem(lax.axis_index("wide"), 2) == 0
    even_d = lax.rem(lax.axis_index("depth"), 2) == 0
    sub = iota((z.z, LANES), 0)

    def side(a, b, first, row, count):
        rows = pl.ds(row, count)
        even = even_w if a is wide_a else even_d
        if first:
            return jnp.where(even, b[rows, :], a[rows, :])
        return jnp.where(even, a[rows, :], b[rows, :])

    def at(x, low, high):
        inv = 1.0 / plane(z, pore, 0, x)
        ox, ix = face(z, rate, upwind, t, 0, x)
        oz, iz = face(z, rate, upwind, t, 1, x)
        oy, iy = face(z, rate, upwind, t, 2, x)
        if low:
            pox, pix = (1.0, side(wide_a, wide_b, True, nc * z.z, z.z)) if halos else (0.0, 0.0)
        else:
            pox, pix = face(z, rate, upwind, t, 0, x - 1)
        if halos:
            wz = jnp.broadcast_to(side(deep_a, deep_b, True, nc * z.x + x, 1), (z.z, LANES))
            poz = jnp.where(sub == 0, 1.0, pltpu.roll(oz, 1, 0))
            piz = jnp.where(sub == 0, wz, pltpu.roll(iz, 1, 0))
            niz = iz
        else:
            poz = jnp.where(sub == 0, 0.0, pltpu.roll(oz, 1, 0))
            piz = jnp.where(sub == 0, 0.0, pltpu.roll(iz, 1, 0))
            niz = jnp.where(sub == z.z - 1, 0.0, iz)
        poy, piy = lane_roll(oy, 1), lane_roll(iy, 1)
        own = ox + pix + oz + piz + oy + piy
        if coef is not None:
            w2, w5 = exchange_weights(z, t, coef, x)
            own = own + w2
            w5 = w5 * inv
        own = own * inv
        ax, bx = ix * inv, pox * inv
        az, bz = niz * inv, poz * inv
        ay, by = iy * inv, poy * inv
        for c in range(nc):
            g = plane(z, mobile, c, x)
            v = plane(z, moles, c, x) - own * g
            if not low:
                v = v + bx * plane(z, mobile, c, x - 1)
            elif halos:
                v = v + bx * side(wide_a, wide_b, True, c * z.z, z.z)
            if not high:
                v = v + ax * plane(z, mobile, c, x + 1)
            elif halos:
                v = v + ax * side(wide_a, wide_b, False, c * z.z, z.z)
            zb, za = pltpu.roll(g, 1, 0), pltpu.roll(g, z.z - 1, 0)
            if halos:
                hz0 = jnp.broadcast_to(side(deep_a, deep_b, True, c * z.x + x, 1), (z.z, LANES))
                hz1 = jnp.broadcast_to(side(deep_a, deep_b, False, c * z.x + x, 1), (z.z, LANES))
                zb = jnp.where(sub == 0, hz0, zb)
                za = jnp.where(sub == z.z - 1, hz1, za)
            v = v + (az * za + bz * zb)
            v = v + (ay * lane_roll(g, -1) + by * lane_roll(g, 1))
            if coef is not None:
                v = v + w5 * plane(z, mobile_f, c, x)
            new[pl.ds(pl.multiple_of(c * z.cells + x * z.z, z.z), z.z), :] = v

    each_plane(z, at)


def exchange_weights(z, t, coef, x):
    g = plane(z, coef, 3, x)
    into = g * plane(z, coef, 4 + 3 * t + 2, x)
    return into, g - into


def matrix_kernel(
    z, t, k_ref, moles, mobile, mobile_f, coef, rate, upwind, pore, ha, hb, hc, hd, new,
    mobile_new, wide_a, wide_b, deep_a, deep_b,
):
    even_w = lax.rem(lax.axis_index("wide"), 2) == 0
    even_d = lax.rem(lax.axis_index("depth"), 2) == 0
    sub = iota((z.z, LANES), 0)

    def wide_side(first, row):
        rows = pl.ds(row, z.z)
        if first:
            return jnp.where(even_w, hb[rows, :], ha[rows, :])
        return jnp.where(even_w, ha[rows, :], hb[rows, :])

    def deep_side(first, row):
        rows = pl.ds(row, 1)
        v = (
            jnp.where(even_d, hd[rows, :], hc[rows, :])
            if first
            else jnp.where(even_d, hc[rows, :], hd[rows, :])
        )
        return jnp.broadcast_to(v, (z.z, LANES))

    def at(x, low, high):
        inv = 1.0 / plane(z, pore, 0, x)
        w2, w5 = exchange_weights(z, t, coef, x)
        w2 = w2 + jnp.where(sub == 0, deep_side(True, z.nc * z.x + x), 0.0)
        if low:
            w2 = w2 + wide_side(True, z.nc * z.z)
        w2, w5 = w2 * inv, w5 * inv
        bz = jnp.where(sub == 0, inv, 0.0)
        az = jnp.where(sub == z.z - 1, face(z, rate, upwind, t, 1, x)[1] * inv, 0.0)
        ax = face(z, rate, upwind, t, 0, x)[1] * inv if high else None
        for c in range(z.nc):
            v = plane(z, moles, c, x) - w2 * plane(z, mobile, c, x)
            v = v + w5 * plane(z, mobile_f, c, x)
            v = v + (bz * deep_side(True, c * z.x + x) + az * deep_side(False, c * z.x + x))
            if low:
                v = v + inv * wide_side(True, c * z.z)
            if high:
                v = v + ax * wide_side(False, c * z.z)
            new[pl.ds(pl.multiple_of(c * z.cells + x * z.z, z.z), z.z), :] = v

    each_plane(z, at)
    flash_field(z, new, mobile_new, k_ref)
    matrix_messages(z, mobile_new, rate, upwind, t + 1, wide_a, wide_b, deep_a, deep_b)


def last_matrix_kernel(
    z, t, moles, mobile, mobile_f, coef, rate, upwind, pore, ha, hb, hc, hd, new
):
    matrix_update(
        z, t, moles, mobile, rate, upwind, pore, (ha, hb, hc, hd), new, mobile_f, coef
    )


def frac_update(z, t, tab, moles, mobile, mobile_m, coef, frac_a, frac_b, new):
    nc = z.nc
    even = lax.rem(lax.axis_index("wide"), 2) == 0
    here = (tab[pl.ds(2 * SUB, 2 * SUB), :] >= 0).astype(F32)
    beyond = tab[pl.ds(4 * SUB, 2 * SUB), :].astype(F32)
    lane = iota((z.z, LANES), 1)
    next_y = jnp.where(lane == LANES - 1, 0.0, lane_roll(here, -1))

    def side(first, row):
        rows = pl.ds(row, z.z)
        if first:
            return jnp.where(even, frac_b[rows, :], frac_a[rows, :])
        return jnp.where(even, frac_a[rows, :], frac_b[rows, :])

    def split(x, d, mask):
        g = plane(z, coef, 1 + d, x) * mask
        out = g * plane(z, coef, 4 + 3 * t + d, x)
        return out, g - out

    def at(x, low, high):
        inv = 1.0 / plane(z, coef, 0, x)
        ox, ix = split(x, 0, beyond if high else here)
        if low:
            pox, pix = here, side(True, nc * z.z) * here
        else:
            pox, pix = split(x - 1, 0, here)
        oy, iy = split(x, 1, next_y)
        poy, piy = lane_roll(oy, 1), lane_roll(iy, 1)
        w2, w5 = split(x, 2, 1.0)
        own = (ox + pix + oy + piy + w5) * inv
        ax, bx = ix * inv, pox * inv
        ay, by = iy * inv, poy * inv
        w2 = w2 * inv
        for c in range(nc):
            g = plane(z, mobile, c, x)
            before = side(True, c * z.z) if low else plane(z, mobile, c, x - 1)
            after = side(False, c * z.z) if high else plane(z, mobile, c, x + 1)
            v = plane(z, moles, c, x) - own * g + (ax * after + bx * before)
            v = v + (ay * lane_roll(g, -1) + by * lane_roll(g, 1))
            v = v + w2 * plane(z, mobile_m, c, x)
            new[pl.ds(pl.multiple_of(c * z.cells + x * z.z, z.z), z.z), :] = v

    each_plane(z, at)


def frac_kernel(
    z, t, k_ref, tab, moles, mobile, mobile_m, coef, fa, fb, new, mobile_new, frac_a, frac_b
):
    frac_update(z, t, tab, moles, mobile, mobile_m, coef, fa, fb, new)
    flash_field(z, new, mobile_new, k_ref)
    frac_messages(z, mobile_new, coef, tab, t + 1, frac_a, frac_b)


def last_frac_kernel(
    z, t, tab, gather, moles, mobile, mobile_m, coef, fa, fb, *refs
):
    backs, (new, stage, sem) = refs[: z.wide], refs[z.wide :]
    frac_update(z, t, tab, moles, mobile, mobile_m, coef, fa, fb, new)
    maps = gather[:, : 3 * z.blocks].astype(jnp.bfloat16)

    def channel(c, carry):
        field_to_rows(z, new, c * z.cells, maps, stage, c)
        return carry

    lax.fori_loop(0, z.nc, channel, 0, unroll=4)
    size = z.jt * z.tiles_back * SUB
    writes = []
    for s in range(z.wide):
        target = lax.rem(lax.axis_index("wide") + s, z.wide)
        writes.append(
            pltpu.make_async_copy(
                stage.at[pl.ds(target * size, size), :], backs[s], sem.at[s]
            )
        )
        writes[-1].start()
    for copy in writes:
        copy.wait()


def swap(value, axis, ahead, ends=True):
    count = lax.axis_size(axis)
    if ahead:
        pairs = [(i, i ^ 1) for i in range(count)]
    else:
        pairs = [(i, i - 1 if i % 2 == 0 else i + 1) for i in range(count)]
        pairs = [(i, n % count) for i, n in pairs if ends or 0 <= n < count]
    return lax.ppermute(value, axis, pairs)


def call(
    kernel, in_specs, out_shape, args, scratch=(), mib=12, out_specs=None, kept=(),
    aliases=None,
):
    body = kernel
    if kept:
        kept = in_vmem(*kept)
        at, count = len(args), len(kept)
        body = lambda *refs: kernel(*refs[:at], *refs[at + count :])
        args = (*args, *kept)
        in_specs = in_specs + [VMEM] * count
    return pl.pallas_call(
        body,
        out_shape=out_shape,
        in_specs=in_specs,
        out_specs=out_specs or (
            (VMEM,) * len(out_shape) if isinstance(out_shape, tuple) else VMEM
        ),
        scratch_shapes=scratch,
        input_output_aliases=aliases or {},
        compiler_params=pltpu.CompilerParams(vmem_limit_bytes=mib << 20),
        cost_estimate=pl.CostEstimate(
            flops=10**8, bytes_accessed=sum(a.size * 4 for a in args), transcendentals=0
        ),
    )(*args)


def shape(rows, lanes=LANES, space=pltpu.VMEM):
    return space((rows, lanes), F32)


def in_vmem(*values):
    return tuple(pltpu.with_memory_space_constraint(v, pltpu.VMEM) for v in values)


def in_hbm(v):
    return pltpu.with_memory_space_constraint(v, pltpu.HBM)


def local(
    matrix_moles,
    pore_matrix,
    matrix_rate,
    matrix_upwind,
    frac_moles,
    pore_frac,
    frac_rate,
    frac_upwind,
    ff_open,
    kvalues,
    slot_patch,
    patch_block,
):
    z = Sizes(matrix_moles, frac_moles)
    bind = lambda f, *a: functools.partial(f, z, *a)
    blocks, slot_patch, kvalues = in_hbm(patch_block.T), in_hbm(slot_patch), in_hbm(kvalues)
    pore = pore_matrix.reshape(-1, z.y)
    rate = matrix_rate.reshape(-1, z.y)
    upwind = matrix_upwind.reshape(-1, z.y)
    field = shape(z.nc * z.cells)
    msg_w, msg_d = shape((z.nc + 1) * z.z), shape((z.nc + 1) * z.x)
    rows_out = z.wide * z.jt * z.tiles_out * SUB
    rows_back = z.wide * z.jt * z.tiles_back * SUB
    src_rows = z.tiles_out * z.cpt * z.slots
    send = call(
        bind(pack_kernel), [SMEM] * 3 + [HBM] * 4,
        (shape(rows_out // z.wide),) * z.wide,
        (
            slot_patch,
            blocks,
            in_hbm(ff_open.T),
            in_hbm(frac_moles.reshape(-1, z.pc)),
            in_hbm(pore_frac),
            in_hbm(frac_rate.reshape(-1, z.pc)),
            in_hbm(frac_upwind.reshape(-1, z.pc)),
        ),
        scratch=[
            pltpu.VMEM((src_rows, z.pc), F32),
            pltpu.VMEM((3 * SUBSTEPS * z.slots, z.pc), I32),
            pltpu.SemaphoreType.DMA((4,)),
        ],
    )

    def trade(chunks):
        got = [chunks[0]]
        for s in range(1, z.wide):
            pairs = [(i, (i + s) % z.wide) for i in range(z.wide)]
            got.append(lax.ppermute(chunks[s], "wide", pairs))
        return tuple(got)

    def exchange(a, b, axis):
        return swap(a, axis, True), swap(b, axis, False, axis == "wide")

    recv = trade(send)
    mobile_m, early, wa, wb, da, db, tab, gather, rate, upwind, pore = call(
        bind(first_matrix_kernel), [SMEM] * 3 + [HBM] * 4,
        (
            field, field, msg_w, msg_w, msg_d, msg_d, pltpu.VMEM((6 * SUB, LANES), I32),
            shape(z.places, -(-3 * z.blocks // LANES) * LANES),
            shape(3 * z.cells), pltpu.VMEM((3 * SUBSTEPS * z.cells, LANES), I32),
            shape(z.cells),
        ),
        (
            kvalues, slot_patch, blocks, in_hbm(matrix_moles.reshape(z.nc, z.cells, LANES)),
            in_hbm(rate), in_hbm(upwind), in_hbm(pore),
        ),
        scratch=[
            pltpu.VMEM((z.nc, z.cells, LANES), F32),
            pltpu.SemaphoreType.DMA((3,)),
            pltpu.SemaphoreType.DMA((PARTS,)),
        ],
    )
    wide_halos = exchange(wa, wb, "wide")
    deep_halos = exchange(da, db, "depth")
    coef_field = shape(z.coefs * z.cells)
    tiles, inner = z.wide * z.tiles_out * SUB, z.jt - 2
    moles_f, mobile_f, coef, fa, fb, staged_rows = call(
        bind(frac_edge_kernel), [SMEM] + [VMEM] * 2 + [HBM] * (z.wide - 1),
        (field, field, coef_field, msg_w, msg_w, shape(inner * tiles)),
        (kvalues, *in_vmem(tab, recv[0]), *(in_hbm(v) for v in recv[1:])),
        scratch=[
            pltpu.VMEM((2 * tiles, LANES), F32),
            pltpu.SemaphoreType.DMA((2 * z.wide,)),
            pltpu.SemaphoreType.DMA((inner * z.wide,)),
        ],
    )
    fa, fb = exchange(fa, fb, "wide")
    moles_f, mobile_f, coef = call(
        bind(frac_inner_kernel), [SMEM] + [VMEM] * 5,
        (field, field, coef_field),
        (kvalues, *in_vmem(tab, staged_rows, moles_f, mobile_f, coef)),
        aliases={3: 0, 4: 1, 5: 2},
    )
    new_f, new_mobile_f, fa, fb = call(
        bind(frac_kernel, 0), [SMEM] + [VMEM] * 7,
        (field, field, msg_w, msg_w),
        (kvalues, *in_vmem(tab, moles_f, mobile_f, mobile_m, coef, fa, fb)),
    )
    fa, fb = exchange(fa, fb, "wide")
    moles, mobile_m, wa, wb, da, db = call(
        bind(matrix_kernel, 0), [SMEM] + [VMEM] * 11,
        (field, field, msg_w, msg_w, msg_d, msg_d),
        (
            kvalues,
            *in_vmem(early, mobile_m, mobile_f, coef, rate, upwind, pore),
            *in_vmem(*wide_halos, *deep_halos),
        ),
    )
    wide_halos = exchange(wa, wb, "wide")
    deep_halos = exchange(da, db, "depth")
    t = SUBSTEPS - 1
    back = call(
        bind(last_frac_kernel, t), [VMEM] * 8,
        (shape(rows_back // z.wide, space=pltpu.HBM),) * z.wide,
        in_vmem(tab, gather, new_f, new_mobile_f, mobile_m, coef, fa, fb),
        scratch=[
            pltpu.VMEM((z.nc * z.cells, LANES), F32),
            pltpu.VMEM((rows_back, LANES), F32),
            pltpu.SemaphoreType.DMA((z.wide,)),
        ],
        out_specs=(HBM,) * z.wide,
    )
    returned = trade(back)
    moles = call(
        bind(last_matrix_kernel, t), [VMEM] * 11,
        jax.ShapeDtypeStruct((z.nc * z.cells, LANES), F32),
        in_vmem(moles, mobile_m, new_mobile_f, coef, rate, upwind, pore, *wide_halos, *deep_halos),
    )
    frac = call(
        bind(spread_kernel), [SMEM] * 2 + [VMEM] * z.wide,
        jax.ShapeDtypeStruct((z.nc * z.slots, z.pc), F32),
        (slot_patch, blocks, *in_vmem(*returned)),
    )
    return moles.reshape(matrix_moles.shape), frac.reshape(frac_moles.shape)


def solution(mesh):
    placed = (
        P(None, "wide", "depth", None),
        P("wide", "depth", None),
        P(None, "wide", "depth", None),
        P(None, None, "wide", "depth", None),
        P(None, ("wide", "depth"), None),
        P(("wide", "depth"), None),
        P(None, ("wide", "depth"), None),
        P(None, None, ("wide", "depth"), None),
        P(("wide", "depth"), None),
        P(),
        P(),
        P(),
    )
    return jax.shard_map(
        local,
        mesh=mesh,
        in_specs=placed,
        out_specs=(P(None, "wide", "depth", None), P(None, ("wide", "depth"), None)),
        check_vma=False,
    )
```

```python
import functools

import jax
import jax.numpy as jnp
from jax import lax
from jax.experimental import pallas as pl
from jax.experimental.pallas import tpu as pltpu
from jax.sharding import PartitionSpec as P


SWEEPS = 4
SUBSTEPS = 2
MOBILITY_RATIO = 4.0
NEVER = 1e30
LANES = 128
SUB = 8
PARTS = 4
FLASH_PLANES = 4
F32 = jnp.float32
I32 = jnp.int32


VMEM = pl.BlockSpec(memory_space=pltpu.VMEM)
SMEM = pl.BlockSpec(memory_space=pltpu.SMEM)
HBM = pl.BlockSpec(memory_space=pltpu.HBM)


class Sizes:
    def __init__(self, matrix_moles, frac_moles):
        self.wide = lax.axis_size("wide")
        self.depth = lax.axis_size("depth")
        self.nc, self.x, self.z, self.y = matrix_moles.shape
        self.slots, self.pc = frac_moles.shape[1:]
        self.ps = 1
        while self.ps * self.ps < self.pc:
            self.ps *= 2
        self.by = self.y // self.ps
        self.half = self.pc // 2
        self.most = max(1, 4 * self.slots // self.wide)
        self.cpt = SUB // self.most
        self.coefs = 4 + 3 * SUBSTEPS
        self.out_ch = self.nc + self.coefs
        self.tiles_out = -(-self.out_ch // self.cpt)
        self.tiles_back = -(-self.nc // self.cpt)
        self.groups = self.wide // SUB
        self.cells = self.x * self.z
        self.places = SUB * self.by
        self.blocks = self.z * self.by
        self.xt = LANES // self.ps
        self.jt = self.half // LANES
        assert self.y == LANES and self.slots == SUB and self.z == 2 * SUB
        assert self.x * self.ps == self.half and self.groups * self.most == self.xt == self.by


def iota(shape, dim):
    return lax.broadcasted_iota(I32, shape, dim)


def lane_roll(v, by):
    by = by % LANES
    return v if by == 0 else pltpu.roll(v, by, 1)


def sub_gather(v, idx):
    return jnp.take_along_axis(v, idx, axis=0, mode="promise_in_bounds")


def group_transpose(a, ps):
    grp = iota((SUB, LANES), 1) // ps
    odd, high = (grp & 1) == 1, (grp & 2) == 2

    def pair(u, v, upper, dist):
        return (
            jnp.where(upper, lane_roll(v, dist), u),
            jnp.where(upper, v, lane_roll(u, -dist)),
        )

    b0, b1 = pair(a[0], a[1], odd, ps)
    c0, c1 = pair(a[2], a[3], odd, ps)
    t0, t2 = pair(b0, c0, high, 2 * ps)
    t1, t3 = pair(b1, c1, high, 2 * ps)
    return [t0, t1, t2, t3]


def tree_sum(terms):
    terms = list(terms)
    while len(terms) > 1:
        terms = [a + b for a, b in zip(terms[::2], terms[1::2])] + (
            [terms[-1]] if len(terms) % 2 else []
        )
    return terms[0]


def flash_block(load, store, inverse, first, nc):
    total = tree_sum([load(c) for c in range(nc)])
    vapour = None
    for _ in range(SWEEPS):
        misfits, slopes = [], []
        for c in range(nc):
            p = first[c] if vapour is None else 1.0 / (vapour + inverse[c])
            r = load(c) * p
            misfits.append(r)
            slopes.append(r * p)
        misfit, slope = running(misfits), running(slopes)
        before = 0.5 if vapour is None else vapour
        vapour = jnp.clip(before + misfit / (slope + total), 0.0, 1.0)
    liquid = (1.0 - vapour) * (1.0 - vapour)
    gas = MOBILITY_RATIO * vapour * vapour
    share = gas / (liquid + gas)
    for c in range(nc):
        p = 1.0 / (vapour + inverse[c])
        store(c, load(c) * p * (share + inverse[c]))


def running(terms):
    sums = [terms[0], terms[1]]
    for n, t in enumerate(terms[2:]):
        sums[n % 2] = sums[n % 2] + t
    return sums[0] + sums[1]


def k_scalars(k_ref, nc):
    inverse, first = [], []
    for c in range(nc):
        e = jnp.full((1, LANES), k_ref[c], F32) - 1.0
        inverse.append(jnp.where(e == 0.0, NEVER, 1.0 / e))
        first.append(1.0 / (0.5 + inverse[c]))
    return inverse, first


def own_slots(z, slot_ref, block_ref, visit):
    me = lax.axis_index("wide") * z.depth + lax.axis_index("depth")
    counts = jnp.int32(0)
    for i in range(z.slots):
        q = slot_ref[me * z.slots + i]
        p0 = block_ref[0, q]
        rank = (counts >> (4 * p0)) & 15
        counts = counts + (jnp.int32(1) << (4 * p0))
        visit(i, p0, rank)


def pack_kernel(
    z, slot_ref, block_ref, open_ref, moles, pore, rate, upwind, *refs
):
    outs, (src, flags, in_sem) = refs[: z.wide], refs[z.wide :]
    nc, slots = z.nc, z.slots
    first = nc * slots
    reads = [
        pltpu.make_async_copy(moles, src.at[pl.ds(0, first), :], in_sem.at[0]),
        pltpu.make_async_copy(pore, src.at[pl.ds(first, slots), :], in_sem.at[1]),
        pltpu.make_async_copy(rate, src.at[pl.ds(first + slots, 3 * slots), :], in_sem.at[2]),
        pltpu.make_async_copy(upwind, flags, in_sem.at[3]),
    ]
    for copy in reads:
        copy.start()
    sub = iota((SUB, LANES), 0)
    picks = [jnp.zeros((SUB, LANES), I32) for _ in range(z.wide)]
    target = [lax.rem(lax.axis_index("wide") + s, z.wide) for s in range(z.wide)]
    opens = [jnp.zeros((SUB, z.pc), I32) for _ in range(2)]
    row_id = iota((SUB, z.pc), 0)

    def visit(i, p0, rank):
        for s in range(z.wide):
            hit = (sub % z.most) == jnp.where(p0 == lax.div(target[s], 2), rank, -1)
            picks[s] = jnp.where(hit, i, picks[s])
        for d in range(2):
            opens[d] = jnp.where(row_id == i, open_ref[d, i], opens[d])

    own_slots(z, slot_ref, block_ref, visit)

    for copy in reads:
        copy.wait()
    cell = iota((slots, z.pc), 1)
    g = first + slots
    open_x = jnp.where(cell // z.ps < z.ps - 1, 1, opens[0]).astype(F32)
    open_y = jnp.where(cell % z.ps < z.ps - 1, 1, opens[1]).astype(F32)
    src[pl.ds(g, slots), :] = src[pl.ds(g, slots), :] * open_x
    src[pl.ds(g + slots, slots), :] = src[pl.ds(g + slots, slots), :] * open_y
    n_flags = 3 * SUBSTEPS * slots
    src[pl.ds(g + 3 * slots, n_flags), :] = flags[...].astype(F32)
    spare = src.shape[0] - (g + 3 * slots + n_flags)
    if spare:
        src[pl.ds(g + 3 * slots + n_flags, spare), :] = jnp.zeros((spare, z.pc), F32)

    def tile(m, carry):
        for s in range(z.wide):
            left = lax.rem(target[s], 2) * z.half
            for j in range(z.jt):
                lanes = pl.ds(pl.multiple_of(left + j * LANES, LANES), LANES)
                v = None
                for cp in range(z.cpt):
                    rows = pl.ds(pl.multiple_of((m * z.cpt + cp) * slots, slots), slots)
                    part = sub_gather(src[rows, lanes], picks[s])
                    v = part if v is None else jnp.where(sub // z.most >= cp, part, v)
                row = (j * z.tiles_out + m) * SUB
                outs[s][pl.ds(pl.multiple_of(row, SUB), SUB), :] = v
        return carry

    lax.fori_loop(0, z.tiles_out, tile, 0)


def sender(z, s):
    return lax.rem(lax.axis_index("wide") + (z.wide - s), z.wide)


def spread_kernel(z, slot_ref, block_ref, *refs):
    chunks, out = refs[: z.wide], refs[z.wide]
    sub = iota((SUB, LANES), 0)
    ranks = jnp.zeros((SUB, LANES), I32)
    column = jnp.zeros((SUB, LANES), I32)

    def visit(i, p0, rank):
        nonlocal ranks, column
        ranks = jnp.where(sub == i, rank, ranks)
        column = jnp.where(sub == i, p0, column)

    own_slots(z, slot_ref, block_ref, visit)
    hits = [column == lax.div(sender(z, s), 2) for s in range(z.wide)]

    def tile(m, carry):
        for parity in range(2):
            group = range(parity, z.wide, 2)
            left = lax.rem(lax.axis_index("wide") + parity, 2) * z.half
            for j in range(z.jt):
                rows = pl.ds(pl.multiple_of((j * z.tiles_back + m) * SUB, SUB), SUB)
                parts = [chunks[s][rows, :] for s in group]
                lanes = pl.ds(pl.multiple_of(left + j * LANES, LANES), LANES)
                for cp in range(z.cpt):
                    v = None
                    for s, part in zip(group, parts):
                        got = sub_gather(part, cp * z.most + ranks)
                        v = got if v is None else jnp.where(hits[s], got, v)
                    row = (m * z.cpt + cp) * SUB
                    out[pl.ds(pl.multiple_of(row, SUB), SUB), lanes] = v
        return carry

    lax.fori_loop(0, z.tiles_back, tile, 0)


def tables(z, slot_ref, block_ref, tab, gather):
    sub, grp = iota((SUB, LANES), 0), iota((SUB, LANES), 1) // z.ps
    bid = [(sub + SUB * h) * z.by + grp for h in range(2)]
    wide, deep = lax.axis_index("wide"), lax.axis_index("depth")
    here, after = wide // 2, jnp.where(wide + 1 < z.wide, (wide + 1) // 2, -1)

    def visit(w, state):
        v0, v1, n0, n1 = state
        counts = jnp.int32(0)
        for i in range(z.slots):
            q = slot_ref[(w * z.depth + deep) * z.slots + i]
            p0 = block_ref[0, q]
            block = lax.rem(block_ref[1, q], z.z) * z.by + block_ref[2, q]
            rank = (counts >> (4 * p0)) & 15
            counts = counts + (jnp.int32(1) << (4 * p0))
            place = lax.rem(w, SUB) + SUB * (lax.div(w, SUB) * z.most + rank)
            b_here = jnp.where(p0 == here, block, -1)
            b_next = jnp.where(p0 == after, block, -1)
            v0 = jnp.where(bid[0] == b_here, place, v0)
            v1 = jnp.where(bid[1] == b_here, place, v1)
            n0 = jnp.where(bid[0] == b_next, 1, n0)
            n1 = jnp.where(bid[1] == b_next, 1, n1)
            column = lax.rem(block, z.by) * z.z + lax.div(block, z.by)

            @pl.when(p0 == here)
            def _():
                gather[pl.ds(place, 1), :] = (
                    (lane % z.blocks == column) & (lane < 3 * z.blocks)
                ).astype(F32)

        return v0, v1, n0, n1

    gather[...] = jnp.zeros(gather.shape, F32)
    lane = iota((1, gather.shape[1]), 1)
    zero = jnp.zeros((SUB, LANES), I32)
    v0, v1, n0, n1 = lax.fori_loop(0, z.wide, visit, (zero - 1, zero - 1, zero, zero))
    for h, (v, n) in enumerate(((v0, n0), (v1, n1))):
        rows = pl.ds(h * SUB, SUB)
        tab[rows, :] = jnp.where(v >= 0, v & (SUB - 1), 0)
        tab[pl.ds(2 * SUB + h * SUB, SUB), :] = jnp.where(
            v >= 0, (grp - (v >> 3)) & (z.by - 1), -1
        )
        tab[pl.ds(4 * SUB + h * SUB, SUB), :] = n


def split3(v):
    hi = v.astype(jnp.bfloat16)
    rest = v - hi.astype(F32)
    mid = rest.astype(jnp.bfloat16)
    low = (rest - mid.astype(F32)).astype(jnp.bfloat16)
    return jnp.concatenate([hi, mid, low], axis=0)


def field_to_rows(z, src, first_row, gather, back, c):
    lane_tile = z.tiles_back * SUB
    stride = z.jt * lane_tile
    for jj in range(0, z.jt, 2):
        columns = []
        for n in range(2):
            parts = [None] * (z.by * (z.z // SUB))
            for h in range(z.z // SUB):
                tiles_x = []
                for xi in range(z.xt):
                    row = first_row + (z.xt * (jj + n) + xi) * z.z + h * SUB
                    tiles_x.append(src[pl.ds(pl.multiple_of(row, SUB), SUB), :])
                for p, v in enumerate(group_transpose(tiles_x, z.ps)):
                    parts[p * (z.z // SUB) + h] = v
            columns.append(jnp.concatenate(parts, axis=0))
        block_rows = jnp.concatenate(columns, axis=1)
        rows = jnp.dot(gather, split3(block_rows), preferred_element_type=F32)
        for n in range(2):
            for i in range(z.by):
                g, k = divmod(i, z.most)
                start = g * SUB * stride + (jj + n) * lane_tile + c * z.most + k
                back[pl.ds(start, SUB, stride=stride), :] = rows[
                    i * SUB : (i + 1) * SUB, n * LANES : (n + 1) * LANES
                ]


def face(z, rate, upwind, t, d, x):
    g = rate[pl.ds(pl.multiple_of(d * z.cells + x * z.z, z.z), z.z), :]
    u = upwind[pl.ds(pl.multiple_of((t * 3 + d) * z.cells + x * z.z, z.z), z.z), :].astype(F32)
    if d == 0:
        keep = (x < z.x - 1) | (lax.axis_index("wide") < z.wide - 1)
    elif d == 1:
        keep = (iota((z.z, LANES), 0) < z.z - 1) | (lax.axis_index("depth") < z.depth - 1)
    else:
        keep = iota((z.z, LANES), 1) < LANES - 1
    g = jnp.where(keep, g, 0.0)
    out = g * u
    return out, g - out


def cells_of(z, ref, c, start, count):
    if len(ref.shape) == 3:
        return ref[c, pl.ds(start, count), :]
    return ref[pl.ds(pl.multiple_of(c * z.cells + start, z.z), count), :]


def plane(z, ref, c, x):
    return cells_of(z, ref, c, pl.multiple_of(x * z.z, z.z), z.z)


def matrix_messages(z, mobile, rate, upwind, t, wide_a, wide_b, deep_a, deep_b):
    nc = z.nc
    even_w = lax.rem(lax.axis_index("wide"), 2) == 0
    even_d = lax.rem(lax.axis_index("depth"), 2) == 0
    out, into = face(z, rate, upwind, t, 0, z.x - 1)
    for c in range(nc):
        ahead = plane(z, mobile, c, z.x - 1) * out
        behind = plane(z, mobile, c, 0)
        rows = pl.ds(c * z.z, z.z)
        wide_a[rows, :] = jnp.where(even_w, ahead, behind)
        wide_b[rows, :] = jnp.where(even_w, behind, ahead)
    rows = pl.ds(nc * z.z, z.z)
    wide_a[rows, :] = into
    wide_b[rows, :] = into
    edge = lax.axis_index("depth") < z.depth - 1

    def last_rows(ref, base, h):
        return ref[pl.ds(base + h * SUB * z.z + z.z - 1, SUB, stride=z.z), :]

    for h in range(z.x // SUB):
        g = jnp.where(edge, last_rows(rate, z.cells, h), 0.0)
        u = last_rows(upwind, (t * 3 + 1) * z.cells, h).astype(F32)
        out = g * u
        for c in range(nc):
            ahead = last_rows(mobile, c * z.cells, h) * out
            behind = mobile[pl.ds(c * z.cells + h * SUB * z.z, SUB, stride=z.z), :]
            rows = pl.ds(c * z.x + h * SUB, SUB)
            deep_a[rows, :] = jnp.where(even_d, ahead, behind)
            deep_b[rows, :] = jnp.where(even_d, behind, ahead)
        rows = pl.ds(nc * z.x + h * SUB, SUB)
        deep_a[rows, :] = g - out
        deep_b[rows, :] = g - out


def flash_field(z, moles, mobile, k_ref, low=0, high=None, hop=1, arrived=None,
                planes=FLASH_PLANES):
    inverse, first = k_scalars(k_ref, z.nc)
    step = planes
    high = z.x // step if high is None else high

    def block(n, carry):
        if arrived is not None:
            arrived(n * step)
        start = pl.multiple_of(n * step * z.z, step * z.z)

        def store(c, v):
            mobile[pl.ds(pl.multiple_of(c * z.cells + start, z.z), step * z.z), :] = v

        flash_block(
            lambda c: cells_of(z, moles, c, start, step * z.z), store, inverse, first, z.nc
        )
        return carry

    lax.fori_loop(0, -(-(high - low) // hop), lambda i, a: block(low + i * hop, a), 0)


def first_matrix_kernel(
    z, k_ref, slot_ref, block_ref, moles_hbm, rate_hbm, upwind_hbm, pore_hbm,
    mobile, early, wide_a, wide_b, deep_a, deep_b, tab, gather, rate, upwind, pore,
    moles, sem, part_sem,
):
    reads = [
        pltpu.make_async_copy(src, dst, sem.at[n])
        for n, (src, dst) in enumerate(
            ((rate_hbm, rate), (upwind_hbm, upwind), (pore_hbm, pore))
        )
    ]
    planes = z.x // PARTS
    parts = []
    for n in range(PARTS):
        rows = pl.ds(n * planes * z.z, planes * z.z)
        parts.append(
            pltpu.make_async_copy(moles_hbm.at[:, rows, :], moles.at[:, rows, :], part_sem.at[n])
        )
    for read in parts + reads:
        read.start()
    tables(z, slot_ref, block_ref, tab, gather)

    def arrived(x):
        for n, part in enumerate(parts):

            @pl.when(x == n * planes)
            def _(part=part):
                part.wait()

    flash_field(z, moles, mobile, k_ref, arrived=arrived)
    for read in reads:
        read.wait()
    matrix_messages(z, mobile, rate, upwind, 0, wide_a, wide_b, deep_a, deep_b)
    matrix_update(z, 0, moles, mobile, rate, upwind, pore, None, early)


def frac_messages(z, mobile, coef, tab, t, frac_a, frac_b):
    even = lax.rem(lax.axis_index("wide"), 2) == 0
    last = lax.axis_index("wide") == z.wide - 1
    here = (tab[pl.ds(2 * SUB, 2 * SUB), :] >= 0).astype(F32)
    out = plane(z, coef, 1, z.x - 1) * plane(z, coef, 4 + 3 * t, z.x - 1)
    into = plane(z, coef, 1, z.x - 1) - out
    out = jnp.where(last, 0.0, out)
    into = jnp.where(last, 0.0, into)
    for c in range(z.nc):
        ahead = plane(z, mobile, c, z.x - 1) * out
        behind = plane(z, mobile, c, 0) * here
        rows = pl.ds(c * z.z, z.z)
        frac_a[rows, :] = jnp.where(even, ahead, behind)
        frac_b[rows, :] = jnp.where(even, behind, ahead)
    rows = pl.ds(z.nc * z.z, z.z)
    frac_a[rows, :] = into
    frac_b[rows, :] = into


def staged(z, chunks, js, recv, sem):
    lane_tile = z.tiles_out * SUB
    return [
        pltpu.make_async_copy(
            chunks[s].at[pl.ds(j * lane_tile, lane_tile), :],
            recv.at[pl.ds((sender(z, s) * len(js) + n) * lane_tile, lane_tile), :],
            sem.at[s * len(js) + n],
        )
        for s in range(z.wide)
        for n, j in enumerate(js)
    ]


def unpack_rows(z, tab, recv, js, moles, coef):
    lane_tile = z.tiles_out * SUB
    stride = len(js) * lane_tile
    from_sub = [tab[pl.ds(h * SUB, SUB), :] for h in range(2)]
    shift = [tab[pl.ds(2 * SUB + h * SUB, SUB), :] for h in range(2)]

    def channel(c, dst, first_row, default):
        for t, j in enumerate(js):
            a = [
                recv[
                    pl.ds(
                        g * SUB * stride + t * lane_tile + c * z.most + k, SUB, stride=stride
                    ),
                    :,
                ]
                for g in range(z.groups)
                for k in range(z.most)
            ]
            for xi, v in enumerate(group_transpose(a, z.ps)):
                rolled = [lane_roll(v, n * z.ps) for n in range(z.by)]
                for h in range(2):
                    got = jnp.full((SUB, LANES), default, F32)
                    for n in range(z.by):
                        got = jnp.where(shift[h] == n, sub_gather(rolled[n], from_sub[h]), got)
                    row = first_row + (z.xt * j + xi) * z.z + h * SUB
                    dst[pl.ds(pl.multiple_of(row, SUB), SUB), :] = got

    def amount(c, carry):
        channel(c, moles, c * z.cells, 1.0)
        return carry

    def weight(c, carry):
        channel(z.nc + c, coef, c * z.cells, jnp.where(c == 0, 1.0, 0.0))
        return carry

    unroll = max(1, 8 // len(js))
    lax.fori_loop(0, z.nc, amount, 0, unroll=unroll)
    lax.fori_loop(0, z.coefs, weight, 0, unroll=5)


def frac_edge_kernel(z, k_ref, tab, *refs):
    chunks, refs = refs[: z.wide], refs[z.wide :]
    moles, mobile, coef, frac_a, frac_b, recv_inner, recv, sem, sem_inner = refs
    edge = (0, z.jt - 1)
    now = staged(z, chunks, edge, recv, sem)
    later = staged(z, chunks, tuple(range(1, z.jt - 1)), recv_inner, sem_inner)
    for read in now:
        read.start()
    for read in now:
        read.wait()
    for read in later:
        read.start()
    unpack_rows(z, tab, recv, edge, moles, coef)
    last = z.x // 2
    flash_field(z, moles, mobile, k_ref, 0, last, last - 1, planes=2)
    frac_messages(z, mobile, coef, tab, 0, frac_a, frac_b)
    for read in later:
        read.wait()


def frac_inner_kernel(z, k_ref, tab, recv, moles_in, mobile_in, coef_in, moles, mobile, coef):
    unpack_rows(z, tab, recv, tuple(range(1, z.jt - 1)), moles, coef)
    flash_field(z, moles, mobile, k_ref, 1, z.x // 2 - 1, planes=2)


def each_plane(z, at):
    def middle(x, carry):
        at(x, False, False)
        return carry

    at(0, True, False)
    lax.fori_loop(1, z.x - 1, middle, 0)
    at(z.x - 1, False, True)


def matrix_update(z, t, moles, mobile, rate, upwind, pore, halos, new, mobile_f=None, coef=None):
    wide_a, wide_b = halos or (None, None)
    nc = z.nc
    even_w = lax.rem(lax.axis_index("wide"), 2) == 0
    sub = iota((z.z, LANES), 0)

    def side(a, b, first, row, count):
        rows = pl.ds(row, count)
        if first:
            return jnp.where(even_w, b[rows, :], a[rows, :])
        return jnp.where(even_w, a[rows, :], b[rows, :])

    def at(x, low, high):
        inv = 1.0 / plane(z, pore, 0, x)
        ox, ix = face(z, rate, upwind, t, 0, x)
        oz, iz = face(z, rate, upwind, t, 1, x)
        oy, iy = face(z, rate, upwind, t, 2, x)
        if low:
            pox, pix = (1.0, side(wide_a, wide_b, True, nc * z.z, z.z)) if halos else (0.0, 0.0)
        else:
            pox, pix = face(z, rate, upwind, t, 0, x - 1)
        poz = jnp.where(sub == 0, 0.0, pltpu.roll(oz, 1, 0))
        piz = jnp.where(sub == 0, 0.0, pltpu.roll(iz, 1, 0))
        niz = jnp.where(sub == z.z - 1, 0.0, iz)
        poy, piy = lane_roll(oy, 1), lane_roll(iy, 1)
        own = ox + pix + oz + piz + oy + piy
        if coef is not None:
            w2, w5 = exchange_weights(z, t, coef, x)
            own = own + w2
            w5 = w5 * inv
        own = own * inv
        ax, bx = ix * inv, pox * inv
        az, bz = niz * inv, poz * inv
        ay, by = iy * inv, poy * inv
        for c in range(nc):
            g = plane(z, mobile, c, x)
            v = plane(z, moles, c, x) - own * g
            if not low:
                v = v + bx * plane(z, mobile, c, x - 1)
            elif halos:
                v = v + bx * side(wide_a, wide_b, True, c * z.z, z.z)
            if not high:
                v = v + ax * plane(z, mobile, c, x + 1)
            elif halos:
                v = v + ax * side(wide_a, wide_b, False, c * z.z, z.z)
            zb, za = pltpu.roll(g, 1, 0), pltpu.roll(g, z.z - 1, 0)
            v = v + (az * za + bz * zb)
            v = v + (ay * lane_roll(g, -1) + by * lane_roll(g, 1))
            if coef is not None:
                v = v + w5 * plane(z, mobile_f, c, x)
            new[pl.ds(pl.multiple_of(c * z.cells + x * z.z, z.z), z.z), :] = v

    each_plane(z, at)


def exchange_weights(z, t, coef, x):
    g = plane(z, coef, 3, x)
    into = g * plane(z, coef, 4 + 3 * t + 2, x)
    return into, g - into


def matrix_kernel(
    z, t, k_ref, moles, mobile, mobile_f, coef, rate, upwind, pore, ha, hb, hc, hd, new,
    mobile_new, wide_a, wide_b, deep_a, deep_b,
):
    even_w = lax.rem(lax.axis_index("wide"), 2) == 0
    even_d = lax.rem(lax.axis_index("depth"), 2) == 0
    sub = iota((z.z, LANES), 0)

    def wide_side(first, row):
        rows = pl.ds(row, z.z)
        if first:
            return jnp.where(even_w, hb[rows, :], ha[rows, :])
        return jnp.where(even_w, ha[rows, :], hb[rows, :])

    def deep_side(first, row):
        rows = pl.ds(row, 1)
        v = (
            jnp.where(even_d, hd[rows, :], hc[rows, :])
            if first
            else jnp.where(even_d, hc[rows, :], hd[rows, :])
        )
        return jnp.broadcast_to(v, (z.z, LANES))

    def at(x, low, high):
        inv = 1.0 / plane(z, pore, 0, x)
        w2, w5 = exchange_weights(z, t, coef, x)
        w2 = w2 + jnp.where(sub == 0, deep_side(True, z.nc * z.x + x), 0.0)
        if low:
            w2 = w2 + wide_side(True, z.nc * z.z)
        w2, w5 = w2 * inv, w5 * inv
        bz = jnp.where(sub == 0, inv, 0.0)
        az = jnp.where(sub == z.z - 1, face(z, rate, upwind, t, 1, x)[1] * inv, 0.0)
        ax = face(z, rate, upwind, t, 0, x)[1] * inv if high else None
        for c in range(z.nc):
            v = plane(z, moles, c, x) - w2 * plane(z, mobile, c, x)
            v = v + w5 * plane(z, mobile_f, c, x)
            v = v + (bz * deep_side(True, c * z.x + x) + az * deep_side(False, c * z.x + x))
            if low:
                v = v + inv * wide_side(True, c * z.z)
            if high:
                v = v + ax * wide_side(False, c * z.z)
            new[pl.ds(pl.multiple_of(c * z.cells + x * z.z, z.z), z.z), :] = v

    each_plane(z, at)
    flash_field(z, new, mobile_new, k_ref)
    matrix_messages(z, mobile_new, rate, upwind, t + 1, wide_a, wide_b, deep_a, deep_b)


def last_matrix_kernel(
    z, t, moles, mobile, mobile_f, coef, rate, upwind, pore, ha, hb, new
):
    matrix_update(z, t, moles, mobile, rate, upwind, pore, (ha, hb), new, mobile_f, coef)


def depth_kernel(z, t, before, mobile, rate, upwind, pore, hc, hd, new, result, sem):
    even = lax.rem(lax.axis_index("depth"), 2) == 0
    inner = lax.axis_index("depth") < z.depth - 1

    def layer(ref, base, h, at):
        return ref[pl.ds(base + h * SUB * z.z + at, SUB, stride=z.z), :]

    def side(first, row):
        rows = pl.ds(row, SUB)
        if first:
            return jnp.where(even, hd[rows, :], hc[rows, :])
        return jnp.where(even, hc[rows, :], hd[rows, :])

    for h in range(z.x // SUB):
        face_at = z.z - 1
        g = jnp.where(inner, layer(rate, z.cells, h, face_at), 0.0)
        u = layer(upwind, (t * 3 + 1) * z.cells, h, face_at).astype(F32)
        into = (g - g * u) / layer(pore, 0, h, face_at)
        inv = 1.0 / layer(pore, 0, h, 0)
        back = side(True, z.nc * z.x + h * SUB)
        for c in range(z.nc):
            base = c * z.cells
            first = pl.ds(base + h * SUB * z.z, SUB, stride=z.z)
            last = pl.ds(base + h * SUB * z.z + face_at, SUB, stride=z.z)
            row = c * z.x + h * SUB
            new[first, :] = new[first, :] + inv * (side(True, row) - back * mobile[first, :])
            new[last, :] = new[last, :] + into * side(False, row)
    copy = pltpu.make_async_copy(new, result, sem)
    copy.start()
    copy.wait()


def frac_update(z, t, tab, moles, mobile, mobile_m, coef, frac_a, frac_b, new):
    nc = z.nc
    even = lax.rem(lax.axis_index("wide"), 2) == 0
    here = (tab[pl.ds(2 * SUB, 2 * SUB), :] >= 0).astype(F32)
    beyond = tab[pl.ds(4 * SUB, 2 * SUB), :].astype(F32)
    lane = iota((z.z, LANES), 1)
    next_y = jnp.where(lane == LANES - 1, 0.0, lane_roll(here, -1))

    def side(first, row):
        rows = pl.ds(row, z.z)
        if first:
            return jnp.where(even, frac_b[rows, :], frac_a[rows, :])
        return jnp.where(even, frac_a[rows, :], frac_b[rows, :])

    def split(x, d, mask):
        g = plane(z, coef, 1 + d, x) * mask
        out = g * plane(z, coef, 4 + 3 * t + d, x)
        return out, g - out

    def at(x, low, high):
        inv = 1.0 / plane(z, coef, 0, x)
        ox, ix = split(x, 0, beyond if high else here)
        if low:
            pox, pix = here, side(True, nc * z.z) * here
        else:
            pox, pix = split(x - 1, 0, here)
        oy, iy = split(x, 1, next_y)
        poy, piy = lane_roll(oy, 1), lane_roll(iy, 1)
        w2, w5 = split(x, 2, 1.0)
        own = (ox + pix + oy + piy + w5) * inv
        ax, bx = ix * inv, pox * inv
        ay, by = iy * inv, poy * inv
        w2 = w2 * inv
        for c in range(nc):
            g = plane(z, mobile, c, x)
            before = side(True, c * z.z) if low else plane(z, mobile, c, x - 1)
            after = side(False, c * z.z) if high else plane(z, mobile, c, x + 1)
            v = plane(z, moles, c, x) - own * g + (ax * after + bx * before)
            v = v + (ay * lane_roll(g, -1) + by * lane_roll(g, 1))
            v = v + w2 * plane(z, mobile_m, c, x)
            new[pl.ds(pl.multiple_of(c * z.cells + x * z.z, z.z), z.z), :] = v

    each_plane(z, at)


def frac_kernel(
    z, t, k_ref, tab, moles, mobile, mobile_m, coef, fa, fb, new, mobile_new, frac_a, frac_b
):
    frac_update(z, t, tab, moles, mobile, mobile_m, coef, fa, fb, new)
    flash_field(z, new, mobile_new, k_ref)
    frac_messages(z, mobile_new, coef, tab, t + 1, frac_a, frac_b)


def last_frac_kernel(
    z, t, tab, gather, moles, mobile, mobile_m, coef, fa, fb, *refs
):
    backs, (new, stage, sem) = refs[: z.wide], refs[z.wide :]
    frac_update(z, t, tab, moles, mobile, mobile_m, coef, fa, fb, new)
    maps = gather[:, : 3 * z.blocks].astype(jnp.bfloat16)

    def channel(c, carry):
        field_to_rows(z, new, c * z.cells, maps, stage, c)
        return carry

    lax.fori_loop(0, z.nc, channel, 0, unroll=4)
    size = z.jt * z.tiles_back * SUB
    writes = []
    for s in range(z.wide):
        target = lax.rem(lax.axis_index("wide") + s, z.wide)
        writes.append(
            pltpu.make_async_copy(
                stage.at[pl.ds(target * size, size), :], backs[s], sem.at[s]
            )
        )
        writes[-1].start()
    for copy in writes:
        copy.wait()


def swap(value, axis, ahead, ends=True):
    count = lax.axis_size(axis)
    if ahead:
        pairs = [(i, i ^ 1) for i in range(count)]
    else:
        pairs = [(i, i - 1 if i % 2 == 0 else i + 1) for i in range(count)]
        pairs = [(i, n % count) for i, n in pairs if ends or 0 <= n < count]
    return lax.ppermute(value, axis, pairs)


def call(
    kernel, in_specs, out_shape, args, scratch=(), mib=12, out_specs=None, kept=(),
    aliases=None,
):
    body = kernel
    if kept:
        kept = in_vmem(*kept)
        at, count = len(args), len(kept)
        body = lambda *refs: kernel(*refs[:at], *refs[at + count :])
        args = (*args, *kept)
        in_specs = in_specs + [VMEM] * count
    return pl.pallas_call(
        body,
        out_shape=out_shape,
        in_specs=in_specs,
        out_specs=out_specs or (
            (VMEM,) * len(out_shape) if isinstance(out_shape, tuple) else VMEM
        ),
        scratch_shapes=scratch,
        input_output_aliases=aliases or {},
        compiler_params=pltpu.CompilerParams(vmem_limit_bytes=mib << 20),
        cost_estimate=pl.CostEstimate(
            flops=10**8, bytes_accessed=sum(a.size * 4 for a in args), transcendentals=0
        ),
    )(*args)


def shape(rows, lanes=LANES, space=pltpu.VMEM):
    return space((rows, lanes), F32)


def in_vmem(*values):
    return tuple(pltpu.with_memory_space_constraint(v, pltpu.VMEM) for v in values)


def in_hbm(v):
    return pltpu.with_memory_space_constraint(v, pltpu.HBM)


def local(
    matrix_moles,
    pore_matrix,
    matrix_rate,
    matrix_upwind,
    frac_moles,
    pore_frac,
    frac_rate,
    frac_upwind,
    ff_open,
    kvalues,
    slot_patch,
    patch_block,
):
    z = Sizes(matrix_moles, frac_moles)
    bind = lambda f, *a: functools.partial(f, z, *a)
    blocks, slot_patch, kvalues = in_hbm(patch_block.T), in_hbm(slot_patch), in_hbm(kvalues)
    pore = pore_matrix.reshape(-1, z.y)
    rate = matrix_rate.reshape(-1, z.y)
    upwind = matrix_upwind.reshape(-1, z.y)
    field = shape(z.nc * z.cells)
    msg_w, msg_d = shape((z.nc + 1) * z.z), shape((z.nc + 1) * z.x)
    rows_out = z.wide * z.jt * z.tiles_out * SUB
    rows_back = z.wide * z.jt * z.tiles_back * SUB
    src_rows = z.tiles_out * z.cpt * z.slots
    send = call(
        bind(pack_kernel), [SMEM] * 3 + [HBM] * 4,
        (shape(rows_out // z.wide),) * z.wide,
        (
            slot_patch,
            blocks,
            in_hbm(ff_open.T),
            in_hbm(frac_moles.reshape(-1, z.pc)),
            in_hbm(pore_frac),
            in_hbm(frac_rate.reshape(-1, z.pc)),
            in_hbm(frac_upwind.reshape(-1, z.pc)),
        ),
        scratch=[
            pltpu.VMEM((src_rows, z.pc), F32),
            pltpu.VMEM((3 * SUBSTEPS * z.slots, z.pc), I32),
            pltpu.SemaphoreType.DMA((4,)),
        ],
    )

    def trade(chunks):
        got = [chunks[0]]
        for s in range(1, z.wide):
            pairs = [(i, (i + s) % z.wide) for i in range(z.wide)]
            got.append(lax.ppermute(chunks[s], "wide", pairs))
        return tuple(got)

    def exchange(a, b, axis):
        return swap(a, axis, True), swap(b, axis, False, axis == "wide")

    recv = trade(send)
    mobile_m, early, wa, wb, da, db, tab, gather, rate, upwind, pore = call(
        bind(first_matrix_kernel), [SMEM] * 3 + [HBM] * 4,
        (
            field, field, msg_w, msg_w, msg_d, msg_d, pltpu.VMEM((6 * SUB, LANES), I32),
            shape(z.places, -(-3 * z.blocks // LANES) * LANES),
            shape(3 * z.cells), pltpu.VMEM((3 * SUBSTEPS * z.cells, LANES), I32),
            shape(z.cells),
        ),
        (
            kvalues, slot_patch, blocks, in_hbm(matrix_moles.reshape(z.nc, z.cells, LANES)),
            in_hbm(rate), in_hbm(upwind), in_hbm(pore),
        ),
        scratch=[
            pltpu.VMEM((z.nc, z.cells, LANES), F32),
            pltpu.SemaphoreType.DMA((3,)),
            pltpu.SemaphoreType.DMA((PARTS,)),
        ],
    )
    wide_halos = exchange(wa, wb, "wide")
    deep_halos = exchange(da, db, "depth")
    coef_field = shape(z.coefs * z.cells)
    tiles, inner = z.wide * z.tiles_out * SUB, z.jt - 2
    moles_f, mobile_f, coef, fa, fb, staged_rows = call(
        bind(frac_edge_kernel), [SMEM] + [VMEM] * 2 + [HBM] * (z.wide - 1),
        (field, field, coef_field, msg_w, msg_w, shape(inner * tiles)),
        (kvalues, *in_vmem(tab, recv[0]), *(in_hbm(v) for v in recv[1:])),
        scratch=[
            pltpu.VMEM((2 * tiles, LANES), F32),
            pltpu.SemaphoreType.DMA((2 * z.wide,)),
            pltpu.SemaphoreType.DMA((inner * z.wide,)),
        ],
    )
    fa, fb = exchange(fa, fb, "wide")
    moles_f, mobile_f, coef = call(
        bind(frac_inner_kernel), [SMEM] + [VMEM] * 5,
        (field, field, coef_field),
        (kvalues, *in_vmem(tab, staged_rows, moles_f, mobile_f, coef)),
        aliases={3: 0, 4: 1, 5: 2},
    )
    new_f, new_mobile_f, fa, fb = call(
        bind(frac_kernel, 0), [SMEM] + [VMEM] * 7,
        (field, field, msg_w, msg_w),
        (kvalues, *in_vmem(tab, moles_f, mobile_f, mobile_m, coef, fa, fb)),
    )
    fa, fb = exchange(fa, fb, "wide")
    moles, mobile_m, wa, wb, da, db = call(
        bind(matrix_kernel, 0), [SMEM] + [VMEM] * 11,
        (field, field, msg_w, msg_w, msg_d, msg_d),
        (
            kvalues,
            *in_vmem(early, mobile_m, mobile_f, coef, rate, upwind, pore),
            *in_vmem(*wide_halos, *deep_halos),
        ),
    )
    wide_halos = exchange(wa, wb, "wide")
    deep_halos = exchange(da, db, "depth")
    t = SUBSTEPS - 1
    back = call(
        bind(last_frac_kernel, t), [VMEM] * 8,
        (shape(rows_back // z.wide, space=pltpu.HBM),) * z.wide,
        in_vmem(tab, gather, new_f, new_mobile_f, mobile_m, coef, fa, fb),
        scratch=[
            pltpu.VMEM((z.nc * z.cells, LANES), F32),
            pltpu.VMEM((rows_back, LANES), F32),
            pltpu.SemaphoreType.DMA((z.wide,)),
        ],
        out_specs=(HBM,) * z.wide,
    )
    returned = trade(back)
    moles = call(
        bind(last_matrix_kernel, t), [VMEM] * 9, field,
        in_vmem(moles, mobile_m, new_mobile_f, coef, rate, upwind, pore, *wide_halos),
    )
    _, moles = call(
        bind(depth_kernel, t), [VMEM] * 7,
        (field, shape(z.nc * z.cells, space=pltpu.HBM)),
        in_vmem(moles, mobile_m, rate, upwind, pore, *deep_halos),
        scratch=[pltpu.SemaphoreType.DMA],
        out_specs=(VMEM, HBM),
        aliases={0: 0},
    )
    frac = call(
        bind(spread_kernel), [SMEM] * 2 + [VMEM] * z.wide,
        jax.ShapeDtypeStruct((z.nc * z.slots, z.pc), F32),
        (slot_patch, blocks, *in_vmem(*returned)),
    )
    return moles.reshape(matrix_moles.shape), frac.reshape(frac_moles.shape)


def solution(mesh):
    placed = (
        P(None, "wide", "depth", None),
        P("wide", "depth", None),
        P(None, "wide", "depth", None),
        P(None, None, "wide", "depth", None),
        P(None, ("wide", "depth"), None),
        P(("wide", "depth"), None),
        P(None, ("wide", "depth"), None),
        P(None, None, ("wide", "depth"), None),
        P(("wide", "depth"), None),
        P(),
        P(),
        P(),
    )
    return jax.shard_map(
        local,
        mesh=mesh,
        in_specs=placed,
        out_specs=(P(None, "wide", "depth", None), P(None, ("wide", "depth"), None)),
        check_vma=False,
    )
```

```python
import functools

import jax
import jax.numpy as jnp
from jax import lax
from jax.experimental import pallas as pl
from jax.experimental.pallas import tpu as pltpu
from jax.sharding import PartitionSpec as P


SWEEPS = 4
SUBSTEPS = 2
MOBILITY_RATIO = 4.0
NEVER = 1e30
LANES = 128
SUB = 8
PARTS = 4
FLASH_PLANES = 4
F32 = jnp.float32
I32 = jnp.int32


VMEM = pl.BlockSpec(memory_space=pltpu.VMEM)
SMEM = pl.BlockSpec(memory_space=pltpu.SMEM)
HBM = pl.BlockSpec(memory_space=pltpu.HBM)


class Sizes:
    def __init__(self, matrix_moles, frac_moles):
        self.wide = lax.axis_size("wide")
        self.depth = lax.axis_size("depth")
        self.nc, self.x, self.z, self.y = matrix_moles.shape
        self.slots, self.pc = frac_moles.shape[1:]
        self.ps = 1
        while self.ps * self.ps < self.pc:
            self.ps *= 2
        self.by = self.y // self.ps
        self.half = self.pc // 2
        self.most = max(1, 4 * self.slots // self.wide)
        self.cpt = SUB // self.most
        self.coefs = 4 + 3 * SUBSTEPS
        self.out_ch = self.nc + self.coefs
        self.tiles_out = -(-self.out_ch // self.cpt)
        self.tiles_back = -(-self.nc // self.cpt)
        self.groups = self.wide // SUB
        self.cells = self.x * self.z
        self.places = SUB * self.by
        self.blocks = self.z * self.by
        self.xt = LANES // self.ps
        self.jt = self.half // LANES
        assert self.y == LANES and self.slots == SUB and self.z == 2 * SUB
        assert self.x * self.ps == self.half and self.groups * self.most == self.xt == self.by


def iota(shape, dim):
    return lax.broadcasted_iota(I32, shape, dim)


def lane_roll(v, by):
    by = by % LANES
    return v if by == 0 else pltpu.roll(v, by, 1)


def sub_gather(v, idx):
    return jnp.take_along_axis(v, idx, axis=0, mode="promise_in_bounds")


def group_transpose(a, ps):
    grp = iota((SUB, LANES), 1) // ps
    odd, high = (grp & 1) == 1, (grp & 2) == 2

    def pair(u, v, upper, dist):
        return (
            jnp.where(upper, lane_roll(v, dist), u),
            jnp.where(upper, v, lane_roll(u, -dist)),
        )

    b0, b1 = pair(a[0], a[1], odd, ps)
    c0, c1 = pair(a[2], a[3], odd, ps)
    t0, t2 = pair(b0, c0, high, 2 * ps)
    t1, t3 = pair(b1, c1, high, 2 * ps)
    return [t0, t1, t2, t3]


def tree_sum(terms):
    terms = list(terms)
    while len(terms) > 1:
        terms = [a + b for a, b in zip(terms[::2], terms[1::2])] + (
            [terms[-1]] if len(terms) % 2 else []
        )
    return terms[0]


def flash_block(load, store, inverse, first, nc):
    total = tree_sum([load(c) for c in range(nc)])
    vapour = None
    for _ in range(SWEEPS):
        misfits, slopes = [], []
        for c in range(nc):
            p = first[c] if vapour is None else 1.0 / (vapour + inverse[c])
            r = load(c) * p
            misfits.append(r)
            slopes.append(r * p)
        misfit, slope = running(misfits), running(slopes)
        before = 0.5 if vapour is None else vapour
        vapour = jnp.clip(before + misfit / (slope + total), 0.0, 1.0)
    liquid = (1.0 - vapour) * (1.0 - vapour)
    gas = MOBILITY_RATIO * vapour * vapour
    share = gas / (liquid + gas)
    for c in range(nc):
        p = 1.0 / (vapour + inverse[c])
        store(c, load(c) * p * (share + inverse[c]))


def running(terms):
    sums = [terms[0], terms[1]]
    for n, t in enumerate(terms[2:]):
        sums[n % 2] = sums[n % 2] + t
    return sums[0] + sums[1]


def k_scalars(k_ref, nc):
    inverse, first = [], []
    for c in range(nc):
        e = jnp.full((1, LANES), k_ref[c], F32) - 1.0
        inverse.append(jnp.where(e == 0.0, NEVER, 1.0 / e))
        first.append(1.0 / (0.5 + inverse[c]))
    return inverse, first


def own_slots(z, slot_ref, block_ref, visit):
    me = lax.axis_index("wide") * z.depth + lax.axis_index("depth")
    counts = jnp.int32(0)
    for i in range(z.slots):
        q = slot_ref[me * z.slots + i]
        p0 = block_ref[0, q]
        rank = (counts >> (4 * p0)) & 15
        counts = counts + (jnp.int32(1) << (4 * p0))
        visit(i, p0, rank)


def pack_kernel(
    z, slot_ref, block_ref, open_ref, moles, pore, rate, upwind, *refs
):
    outs, (src, flags, in_sem) = refs[: z.wide], refs[z.wide :]
    nc, slots = z.nc, z.slots
    first = nc * slots
    reads = [
        pltpu.make_async_copy(moles, src.at[pl.ds(0, first), :], in_sem.at[0]),
        pltpu.make_async_copy(pore, src.at[pl.ds(first, slots), :], in_sem.at[1]),
        pltpu.make_async_copy(rate, src.at[pl.ds(first + slots, 3 * slots), :], in_sem.at[2]),
        pltpu.make_async_copy(upwind, flags, in_sem.at[3]),
    ]
    for copy in reads:
        copy.start()
    sub = iota((SUB, LANES), 0)
    picks = [jnp.zeros((SUB, LANES), I32) for _ in range(z.wide)]
    target = [lax.rem(lax.axis_index("wide") + s, z.wide) for s in range(z.wide)]
    opens = [jnp.zeros((SUB, z.pc), I32) for _ in range(2)]
    row_id = iota((SUB, z.pc), 0)

    def visit(i, p0, rank):
        for s in range(z.wide):
            hit = (sub % z.most) == jnp.where(p0 == lax.div(target[s], 2), rank, -1)
            picks[s] = jnp.where(hit, i, picks[s])
        for d in range(2):
            opens[d] = jnp.where(row_id == i, open_ref[d, i], opens[d])

    own_slots(z, slot_ref, block_ref, visit)

    for copy in reads:
        copy.wait()
    cell = iota((slots, z.pc), 1)
    g = first + slots
    open_x = jnp.where(cell // z.ps < z.ps - 1, 1, opens[0]).astype(F32)
    open_y = jnp.where(cell % z.ps < z.ps - 1, 1, opens[1]).astype(F32)
    src[pl.ds(g, slots), :] = src[pl.ds(g, slots), :] * open_x
    src[pl.ds(g + slots, slots), :] = src[pl.ds(g + slots, slots), :] * open_y
    n_flags = 3 * SUBSTEPS * slots
    src[pl.ds(g + 3 * slots, n_flags), :] = flags[...].astype(F32)
    spare = src.shape[0] - (g + 3 * slots + n_flags)
    if spare:
        src[pl.ds(g + 3 * slots + n_flags, spare), :] = jnp.zeros((spare, z.pc), F32)

    def tile(m, carry):
        for s in range(z.wide):
            left = lax.rem(target[s], 2) * z.half
            for j in range(z.jt):
                lanes = pl.ds(pl.multiple_of(left + j * LANES, LANES), LANES)
                v = None
                for cp in range(z.cpt):
                    rows = pl.ds(pl.multiple_of((m * z.cpt + cp) * slots, slots), slots)
                    part = sub_gather(src[rows, lanes], picks[s])
                    v = part if v is None else jnp.where(sub // z.most >= cp, part, v)
                row = (j * z.tiles_out + m) * SUB
                outs[s][pl.ds(pl.multiple_of(row, SUB), SUB), :] = v
        return carry

    lax.fori_loop(0, z.tiles_out, tile, 0)


def sender(z, s):
    return lax.rem(lax.axis_index("wide") + (z.wide - s), z.wide)


def spread_kernel(z, slot_ref, block_ref, *refs):
    chunks, (result, out, sem) = refs[: z.wide], refs[z.wide :]
    sub = iota((SUB, LANES), 0)
    ranks = jnp.zeros((SUB, LANES), I32)
    column = jnp.zeros((SUB, LANES), I32)

    def visit(i, p0, rank):
        nonlocal ranks, column
        ranks = jnp.where(sub == i, rank, ranks)
        column = jnp.where(sub == i, p0, column)

    own_slots(z, slot_ref, block_ref, visit)
    hits = [column == lax.div(sender(z, s), 2) for s in range(z.wide)]

    def tile(m, carry):
        for parity in range(2):
            group = range(parity, z.wide, 2)
            left = lax.rem(lax.axis_index("wide") + parity, 2) * z.half
            for j in range(z.jt):
                rows = pl.ds(pl.multiple_of((j * z.tiles_back + m) * SUB, SUB), SUB)
                parts = [chunks[s][rows, :] for s in group]
                lanes = pl.ds(pl.multiple_of(left + j * LANES, LANES), LANES)
                for cp in range(z.cpt):
                    v = None
                    for s, part in zip(group, parts):
                        got = sub_gather(part, cp * z.most + ranks)
                        v = got if v is None else jnp.where(hits[s], got, v)
                    row = (m * z.cpt + cp) * SUB
                    out[pl.ds(pl.multiple_of(row, SUB), SUB), lanes] = v
        written(m).start()
        return carry

    def written(m):
        rows = pl.ds(pl.multiple_of(m * z.cpt * SUB, SUB), z.cpt * SUB)
        return pltpu.make_async_copy(out.at[rows, :], result.at[rows, :], sem.at[m])

    lax.fori_loop(0, z.tiles_back, tile, 0)
    for m in range(z.tiles_back):
        written(m).wait()


def tables(z, slot_ref, block_ref, tab, gather):
    sub, grp = iota((SUB, LANES), 0), iota((SUB, LANES), 1) // z.ps
    bid = [(sub + SUB * h) * z.by + grp for h in range(2)]
    wide, deep = lax.axis_index("wide"), lax.axis_index("depth")
    here, after = wide // 2, jnp.where(wide + 1 < z.wide, (wide + 1) // 2, -1)

    def visit(w, state):
        v0, v1, n0, n1 = state
        counts = jnp.int32(0)
        for i in range(z.slots):
            q = slot_ref[(w * z.depth + deep) * z.slots + i]
            p0 = block_ref[0, q]
            block = lax.rem(block_ref[1, q], z.z) * z.by + block_ref[2, q]
            rank = (counts >> (4 * p0)) & 15
            counts = counts + (jnp.int32(1) << (4 * p0))
            place = lax.rem(w, SUB) + SUB * (lax.div(w, SUB) * z.most + rank)
            b_here = jnp.where(p0 == here, block, -1)
            b_next = jnp.where(p0 == after, block, -1)
            v0 = jnp.where(bid[0] == b_here, place, v0)
            v1 = jnp.where(bid[1] == b_here, place, v1)
            n0 = jnp.where(bid[0] == b_next, 1, n0)
            n1 = jnp.where(bid[1] == b_next, 1, n1)
            column = lax.rem(block, z.by) * z.z + lax.div(block, z.by)

            @pl.when(p0 == here)
            def _():
                gather[pl.ds(place, 1), :] = (
                    (lane % z.blocks == column) & (lane < 3 * z.blocks)
                ).astype(F32)

        return v0, v1, n0, n1

    gather[...] = jnp.zeros(gather.shape, F32)
    lane = iota((1, gather.shape[1]), 1)
    zero = jnp.zeros((SUB, LANES), I32)
    v0, v1, n0, n1 = lax.fori_loop(0, z.wide, visit, (zero - 1, zero - 1, zero, zero))
    for h, (v, n) in enumerate(((v0, n0), (v1, n1))):
        rows = pl.ds(h * SUB, SUB)
        tab[rows, :] = jnp.where(v >= 0, v & (SUB - 1), 0)
        tab[pl.ds(2 * SUB + h * SUB, SUB), :] = jnp.where(
            v >= 0, (grp - (v >> 3)) & (z.by - 1), -1
        )
        tab[pl.ds(4 * SUB + h * SUB, SUB), :] = n


def split3(v):
    hi = v.astype(jnp.bfloat16)
    rest = v - hi.astype(F32)
    mid = rest.astype(jnp.bfloat16)
    low = (rest - mid.astype(F32)).astype(jnp.bfloat16)
    return jnp.concatenate([hi, mid, low], axis=0)


def field_to_rows(z, src, first_row, gather, back, c):
    lane_tile = z.tiles_back * SUB
    stride = z.jt * lane_tile
    for jj in range(0, z.jt, 2):
        columns = []
        for n in range(2):
            parts = [None] * (z.by * (z.z // SUB))
            for h in range(z.z // SUB):
                tiles_x = []
                for xi in range(z.xt):
                    row = first_row + (z.xt * (jj + n) + xi) * z.z + h * SUB
                    tiles_x.append(src[pl.ds(pl.multiple_of(row, SUB), SUB), :])
                for p, v in enumerate(group_transpose(tiles_x, z.ps)):
                    parts[p * (z.z // SUB) + h] = v
            columns.append(jnp.concatenate(parts, axis=0))
        block_rows = jnp.concatenate(columns, axis=1)
        rows = jnp.dot(gather, split3(block_rows), preferred_element_type=F32)
        for n in range(2):
            for i in range(z.by):
                g, k = divmod(i, z.most)
                start = g * SUB * stride + (jj + n) * lane_tile + c * z.most + k
                back[pl.ds(start, SUB, stride=stride), :] = rows[
                    i * SUB : (i + 1) * SUB, n * LANES : (n + 1) * LANES
                ]


def face(z, rate, upwind, t, d, x):
    g = rate[pl.ds(pl.multiple_of(d * z.cells + x * z.z, z.z), z.z), :]
    u = upwind[pl.ds(pl.multiple_of((t * 3 + d) * z.cells + x * z.z, z.z), z.z), :].astype(F32)
    if d == 0:
        keep = (x < z.x - 1) | (lax.axis_index("wide") < z.wide - 1)
    elif d == 1:
        keep = (iota((z.z, LANES), 0) < z.z - 1) | (lax.axis_index("depth") < z.depth - 1)
    else:
        keep = iota((z.z, LANES), 1) < LANES - 1
    g = jnp.where(keep, g, 0.0)
    out = g * u
    return out, g - out


def cells_of(z, ref, c, start, count):
    if len(ref.shape) == 3:
        return ref[c, pl.ds(start, count), :]
    return ref[pl.ds(pl.multiple_of(c * z.cells + start, z.z), count), :]


def plane(z, ref, c, x):
    return cells_of(z, ref, c, pl.multiple_of(x * z.z, z.z), z.z)


def matrix_messages(z, mobile, rate, upwind, t, wide_a, wide_b, deep_a, deep_b):
    nc = z.nc
    even_w = lax.rem(lax.axis_index("wide"), 2) == 0
    even_d = lax.rem(lax.axis_index("depth"), 2) == 0
    out, into = face(z, rate, upwind, t, 0, z.x - 1)
    for c in range(nc):
        ahead = plane(z, mobile, c, z.x - 1) * out
        behind = plane(z, mobile, c, 0)
        rows = pl.ds(c * z.z, z.z)
        wide_a[rows, :] = jnp.where(even_w, ahead, behind)
        wide_b[rows, :] = jnp.where(even_w, behind, ahead)
    rows = pl.ds(nc * z.z, z.z)
    wide_a[rows, :] = into
    wide_b[rows, :] = into
    edge = lax.axis_index("depth") < z.depth - 1

    def last_rows(ref, base, h):
        return ref[pl.ds(base + h * SUB * z.z + z.z - 1, SUB, stride=z.z), :]

    for h in range(z.x // SUB):
        g = jnp.where(edge, last_rows(rate, z.cells, h), 0.0)
        u = last_rows(upwind, (t * 3 + 1) * z.cells, h).astype(F32)
        out = g * u
        for c in range(nc):
            ahead = last_rows(mobile, c * z.cells, h) * out
            behind = mobile[pl.ds(c * z.cells + h * SUB * z.z, SUB, stride=z.z), :]
            rows = pl.ds(c * z.x + h * SUB, SUB)
            deep_a[rows, :] = jnp.where(even_d, ahead, behind)
            deep_b[rows, :] = jnp.where(even_d, behind, ahead)
        rows = pl.ds(nc * z.x + h * SUB, SUB)
        deep_a[rows, :] = g - out
        deep_b[rows, :] = g - out


def flash_field(z, moles, mobile, k_ref, low=0, high=None, hop=1, arrived=None,
                planes=FLASH_PLANES):
    inverse, first = k_scalars(k_ref, z.nc)
    step = planes
    high = z.x // step if high is None else high

    def block(n, carry):
        if arrived is not None:
            arrived(n * step)
        start = pl.multiple_of(n * step * z.z, step * z.z)

        def store(c, v):
            mobile[pl.ds(pl.multiple_of(c * z.cells + start, z.z), step * z.z), :] = v

        flash_block(
            lambda c: cells_of(z, moles, c, start, step * z.z), store, inverse, first, z.nc
        )
        return carry

    lax.fori_loop(0, -(-(high - low) // hop), lambda i, a: block(low + i * hop, a), 0)


def first_matrix_kernel(
    z, k_ref, slot_ref, block_ref, moles_hbm, rate_hbm, upwind_hbm, pore_hbm,
    mobile, early, wide_a, wide_b, deep_a, deep_b, tab, gather, rate, upwind, pore,
    moles, sem, part_sem,
):
    reads = [
        pltpu.make_async_copy(src, dst, sem.at[n])
        for n, (src, dst) in enumerate(
            ((rate_hbm, rate), (upwind_hbm, upwind), (pore_hbm, pore))
        )
    ]
    planes = z.x // PARTS
    parts = []
    for n in range(PARTS):
        rows = pl.ds(n * planes * z.z, planes * z.z)
        parts.append(
            pltpu.make_async_copy(moles_hbm.at[:, rows, :], moles.at[:, rows, :], part_sem.at[n])
        )
    for read in parts + reads:
        read.start()
    tables(z, slot_ref, block_ref, tab, gather)

    def arrived(x):
        for n, part in enumerate(parts):

            @pl.when(x == n * planes)
            def _(part=part):
                part.wait()

    flash_field(z, moles, mobile, k_ref, arrived=arrived)
    for read in reads:
        read.wait()
    matrix_messages(z, mobile, rate, upwind, 0, wide_a, wide_b, deep_a, deep_b)
    matrix_update(z, 0, moles, mobile, rate, upwind, pore, None, early)


def frac_messages(z, mobile, coef, tab, t, frac_a, frac_b):
    even = lax.rem(lax.axis_index("wide"), 2) == 0
    last = lax.axis_index("wide") == z.wide - 1
    here = (tab[pl.ds(2 * SUB, 2 * SUB), :] >= 0).astype(F32)
    out = plane(z, coef, 1, z.x - 1) * plane(z, coef, 4 + 3 * t, z.x - 1)
    into = plane(z, coef, 1, z.x - 1) - out
    out = jnp.where(last, 0.0, out)
    into = jnp.where(last, 0.0, into)
    for c in range(z.nc):
        ahead = plane(z, mobile, c, z.x - 1) * out
        behind = plane(z, mobile, c, 0) * here
        rows = pl.ds(c * z.z, z.z)
        frac_a[rows, :] = jnp.where(even, ahead, behind)
        frac_b[rows, :] = jnp.where(even, behind, ahead)
    rows = pl.ds(z.nc * z.z, z.z)
    frac_a[rows, :] = into
    frac_b[rows, :] = into


def staged(z, chunks, js, recv, sem):
    lane_tile = z.tiles_out * SUB
    return [
        pltpu.make_async_copy(
            chunks[s].at[pl.ds(j * lane_tile, lane_tile), :],
            recv.at[pl.ds((sender(z, s) * len(js) + n) * lane_tile, lane_tile), :],
            sem.at[s * len(js) + n],
        )
        for s in range(z.wide)
        for n, j in enumerate(js)
    ]


def unpack_rows(z, tab, recv, js, moles, coef):
    lane_tile = z.tiles_out * SUB
    stride = len(js) * lane_tile
    from_sub = [tab[pl.ds(h * SUB, SUB), :] for h in range(2)]
    shift = [tab[pl.ds(2 * SUB + h * SUB, SUB), :] for h in range(2)]

    def channel(c, dst, first_row, default):
        for t, j in enumerate(js):
            a = [
                recv[
                    pl.ds(
                        g * SUB * stride + t * lane_tile + c * z.most + k, SUB, stride=stride
                    ),
                    :,
                ]
                for g in range(z.groups)
                for k in range(z.most)
            ]
            for xi, v in enumerate(group_transpose(a, z.ps)):
                rolled = [lane_roll(v, n * z.ps) for n in range(z.by)]
                for h in range(2):
                    got = jnp.full((SUB, LANES), default, F32)
                    for n in range(z.by):
                        got = jnp.where(shift[h] == n, sub_gather(rolled[n], from_sub[h]), got)
                    row = first_row + (z.xt * j + xi) * z.z + h * SUB
                    dst[pl.ds(pl.multiple_of(row, SUB), SUB), :] = got

    def amount(c, carry):
        channel(c, moles, c * z.cells, 1.0)
        return carry

    def weight(c, carry):
        channel(z.nc + c, coef, c * z.cells, jnp.where(c == 0, 1.0, 0.0))
        return carry

    unroll = max(1, 8 // len(js))
    lax.fori_loop(0, z.nc, amount, 0, unroll=unroll)
    lax.fori_loop(0, z.coefs, weight, 0, unroll=5)


def frac_edge_kernel(z, k_ref, tab, *refs):
    chunks, refs = refs[: z.wide], refs[z.wide :]
    moles, mobile, coef, frac_a, frac_b, recv_inner, recv, sem, sem_inner = refs
    edge = (0, z.jt - 1)
    now = staged(z, chunks, edge, recv, sem)
    later = staged(z, chunks, tuple(range(1, z.jt - 1)), recv_inner, sem_inner)
    for read in now:
        read.start()
    for read in now:
        read.wait()
    for read in later:
        read.start()
    unpack_rows(z, tab, recv, edge, moles, coef)
    last = z.x // 2
    flash_field(z, moles, mobile, k_ref, 0, last, last - 1, planes=2)
    frac_messages(z, mobile, coef, tab, 0, frac_a, frac_b)
    for read in later:
        read.wait()


def frac_inner_kernel(z, k_ref, tab, recv, moles_in, mobile_in, coef_in, moles, mobile, coef):
    unpack_rows(z, tab, recv, tuple(range(1, z.jt - 1)), moles, coef)
    flash_field(z, moles, mobile, k_ref, 1, z.x // 2 - 1, planes=2)


def each_plane(z, at):
    def middle(x, carry):
        at(x, False, False)
        return carry

    at(0, True, False)
    lax.fori_loop(1, z.x - 1, middle, 0)
    at(z.x - 1, False, True)


def matrix_update(z, t, moles, mobile, rate, upwind, pore, halos, new, mobile_f=None, coef=None):
    wide_a, wide_b = halos or (None, None)
    nc = z.nc
    even_w = lax.rem(lax.axis_index("wide"), 2) == 0
    sub = iota((z.z, LANES), 0)

    def side(a, b, first, row, count):
        rows = pl.ds(row, count)
        if first:
            return jnp.where(even_w, b[rows, :], a[rows, :])
        return jnp.where(even_w, a[rows, :], b[rows, :])

    def at(x, low, high):
        inv = 1.0 / plane(z, pore, 0, x)
        ox, ix = face(z, rate, upwind, t, 0, x)
        oz, iz = face(z, rate, upwind, t, 1, x)
        oy, iy = face(z, rate, upwind, t, 2, x)
        if low:
            pox, pix = (1.0, side(wide_a, wide_b, True, nc * z.z, z.z)) if halos else (0.0, 0.0)
        else:
            pox, pix = face(z, rate, upwind, t, 0, x - 1)
        poz = jnp.where(sub == 0, 0.0, pltpu.roll(oz, 1, 0))
        piz = jnp.where(sub == 0, 0.0, pltpu.roll(iz, 1, 0))
        niz = jnp.where(sub == z.z - 1, 0.0, iz)
        poy, piy = lane_roll(oy, 1), lane_roll(iy, 1)
        own = ox + pix + oz + piz + oy + piy
        if coef is not None:
            w2, w5 = exchange_weights(z, t, coef, x)
            own = own + w2
            w5 = w5 * inv
        own = own * inv
        ax, bx = ix * inv, pox * inv
        az, bz = niz * inv, poz * inv
        ay, by = iy * inv, poy * inv
        for c in range(nc):
            g = plane(z, mobile, c, x)
            v = plane(z, moles, c, x) - own * g
            if not low:
                v = v + bx * plane(z, mobile, c, x - 1)
            elif halos:
                v = v + bx * side(wide_a, wide_b, True, c * z.z, z.z)
            if not high:
                v = v + ax * plane(z, mobile, c, x + 1)
            elif halos:
                v = v + ax * side(wide_a, wide_b, False, c * z.z, z.z)
            zb, za = pltpu.roll(g, 1, 0), pltpu.roll(g, z.z - 1, 0)
            v = v + (az * za + bz * zb)
            v = v + (ay * lane_roll(g, -1) + by * lane_roll(g, 1))
            if coef is not None:
                v = v + w5 * plane(z, mobile_f, c, x)
            new[pl.ds(pl.multiple_of(c * z.cells + x * z.z, z.z), z.z), :] = v

    each_plane(z, at)


def exchange_weights(z, t, coef, x):
    g = plane(z, coef, 3, x)
    into = g * plane(z, coef, 4 + 3 * t + 2, x)
    return into, g - into


def matrix_kernel(
    z, t, k_ref, moles, mobile, mobile_f, coef, rate, upwind, pore, ha, hb, hc, hd, new,
    mobile_new, wide_a, wide_b, deep_a, deep_b,
):
    even_w = lax.rem(lax.axis_index("wide"), 2) == 0
    even_d = lax.rem(lax.axis_index("depth"), 2) == 0
    sub = iota((z.z, LANES), 0)

    def wide_side(first, row):
        rows = pl.ds(row, z.z)
        if first:
            return jnp.where(even_w, hb[rows, :], ha[rows, :])
        return jnp.where(even_w, ha[rows, :], hb[rows, :])

    def deep_side(first, row):
        rows = pl.ds(row, 1)
        v = (
            jnp.where(even_d, hd[rows, :], hc[rows, :])
            if first
            else jnp.where(even_d, hc[rows, :], hd[rows, :])
        )
        return jnp.broadcast_to(v, (z.z, LANES))

    def at(x, low, high):
        inv = 1.0 / plane(z, pore, 0, x)
        w2, w5 = exchange_weights(z, t, coef, x)
        w2 = w2 + jnp.where(sub == 0, deep_side(True, z.nc * z.x + x), 0.0)
        if low:
            w2 = w2 + wide_side(True, z.nc * z.z)
        w2, w5 = w2 * inv, w5 * inv
        bz = jnp.where(sub == 0, inv, 0.0)
        az = jnp.where(sub == z.z - 1, face(z, rate, upwind, t, 1, x)[1] * inv, 0.0)
        ax = face(z, rate, upwind, t, 0, x)[1] * inv if high else None
        for c in range(z.nc):
            v = plane(z, moles, c, x) - w2 * plane(z, mobile, c, x)
            v = v + w5 * plane(z, mobile_f, c, x)
            v = v + (bz * deep_side(True, c * z.x + x) + az * deep_side(False, c * z.x + x))
            if low:
                v = v + inv * wide_side(True, c * z.z)
            if high:
                v = v + ax * wide_side(False, c * z.z)
            new[pl.ds(pl.multiple_of(c * z.cells + x * z.z, z.z), z.z), :] = v

    each_plane(z, at)
    flash_field(z, new, mobile_new, k_ref)
    matrix_messages(z, mobile_new, rate, upwind, t + 1, wide_a, wide_b, deep_a, deep_b)


def last_matrix_kernel(
    z, t, moles, mobile, mobile_f, coef, rate, upwind, pore, ha, hb, new
):
    matrix_update(z, t, moles, mobile, rate, upwind, pore, (ha, hb), new, mobile_f, coef)


def depth_kernel(z, t, before, mobile, rate, upwind, pore, hc, hd, new, result, sem):
    even = lax.rem(lax.axis_index("depth"), 2) == 0
    inner = lax.axis_index("depth") < z.depth - 1

    def layer(ref, base, h, at):
        return ref[pl.ds(base + h * SUB * z.z + at, SUB, stride=z.z), :]

    def side(first, row):
        rows = pl.ds(row, SUB)
        if first:
            return jnp.where(even, hd[rows, :], hc[rows, :])
        return jnp.where(even, hc[rows, :], hd[rows, :])

    face_at = z.z - 1
    weights = []
    for h in range(z.x // SUB):
        g = jnp.where(inner, layer(rate, z.cells, h, face_at), 0.0)
        u = layer(upwind, (t * 3 + 1) * z.cells, h, face_at).astype(F32)
        into = (g - g * u) / layer(pore, 0, h, face_at)
        weights.append((into, 1.0 / layer(pore, 0, h, 0), side(True, z.nc * z.x + h * SUB)))
    copies = []
    for c in range(z.nc):
        base = c * z.cells
        for h, (into, inv, back) in enumerate(weights):
            first = pl.ds(base + h * SUB * z.z, SUB, stride=z.z)
            last = pl.ds(base + h * SUB * z.z + face_at, SUB, stride=z.z)
            row = c * z.x + h * SUB
            new[first, :] = new[first, :] + inv * (side(True, row) - back * mobile[first, :])
            new[last, :] = new[last, :] + into * side(False, row)
        rows = pl.ds(base, z.cells)
        copies.append(pltpu.make_async_copy(new.at[rows, :], result.at[rows, :], sem.at[c]))
        copies[-1].start()
    for copy in copies:
        copy.wait()


def frac_update(z, t, tab, moles, mobile, mobile_m, coef, frac_a, frac_b, new):
    nc = z.nc
    even = lax.rem(lax.axis_index("wide"), 2) == 0
    here = (tab[pl.ds(2 * SUB, 2 * SUB), :] >= 0).astype(F32)
    beyond = tab[pl.ds(4 * SUB, 2 * SUB), :].astype(F32)
    lane = iota((z.z, LANES), 1)
    next_y = jnp.where(lane == LANES - 1, 0.0, lane_roll(here, -1))

    def side(first, row):
        rows = pl.ds(row, z.z)
        if first:
            return jnp.where(even, frac_b[rows, :], frac_a[rows, :])
        return jnp.where(even, frac_a[rows, :], frac_b[rows, :])

    def split(x, d, mask):
        g = plane(z, coef, 1 + d, x) * mask
        out = g * plane(z, coef, 4 + 3 * t + d, x)
        return out, g - out

    def at(x, low, high):
        inv = 1.0 / plane(z, coef, 0, x)
        ox, ix = split(x, 0, beyond if high else here)
        if low:
            pox, pix = here, side(True, nc * z.z) * here
        else:
            pox, pix = split(x - 1, 0, here)
        oy, iy = split(x, 1, next_y)
        poy, piy = lane_roll(oy, 1), lane_roll(iy, 1)
        w2, w5 = split(x, 2, 1.0)
        own = (ox + pix + oy + piy + w5) * inv
        ax, bx = ix * inv, pox * inv
        ay, by = iy * inv, poy * inv
        w2 = w2 * inv
        for c in range(nc):
            g = plane(z, mobile, c, x)
            before = side(True, c * z.z) if low else plane(z, mobile, c, x - 1)
            after = side(False, c * z.z) if high else plane(z, mobile, c, x + 1)
            v = plane(z, moles, c, x) - own * g + (ax * after + bx * before)
            v = v + (ay * lane_roll(g, -1) + by * lane_roll(g, 1))
            v = v + w2 * plane(z, mobile_m, c, x)
            new[pl.ds(pl.multiple_of(c * z.cells + x * z.z, z.z), z.z), :] = v

    each_plane(z, at)


def frac_kernel(
    z, t, k_ref, tab, moles, mobile, mobile_m, coef, fa, fb, new, mobile_new, frac_a, frac_b
):
    frac_update(z, t, tab, moles, mobile, mobile_m, coef, fa, fb, new)
    flash_field(z, new, mobile_new, k_ref)
    frac_messages(z, mobile_new, coef, tab, t + 1, frac_a, frac_b)


def last_frac_kernel(
    z, t, tab, gather, moles, mobile, mobile_m, coef, fa, fb, *refs
):
    backs, (new, stage, sem) = refs[: z.wide], refs[z.wide :]
    frac_update(z, t, tab, moles, mobile, mobile_m, coef, fa, fb, new)
    maps = gather[:, : 3 * z.blocks].astype(jnp.bfloat16)

    def channel(c, carry):
        field_to_rows(z, new, c * z.cells, maps, stage, c)
        return carry

    lax.fori_loop(0, z.nc, channel, 0, unroll=4)
    size = z.jt * z.tiles_back * SUB
    writes = []
    for s in range(z.wide):
        target = lax.rem(lax.axis_index("wide") + s, z.wide)
        writes.append(
            pltpu.make_async_copy(
                stage.at[pl.ds(target * size, size), :], backs[s], sem.at[s]
            )
        )
        writes[-1].start()
    for copy in writes:
        copy.wait()


def swap(value, axis, ahead, ends=True):
    count = lax.axis_size(axis)
    if ahead:
        pairs = [(i, i ^ 1) for i in range(count)]
    else:
        pairs = [(i, i - 1 if i % 2 == 0 else i + 1) for i in range(count)]
        pairs = [(i, n % count) for i, n in pairs if ends or 0 <= n < count]
    return lax.ppermute(value, axis, pairs)


def call(
    kernel, in_specs, out_shape, args, scratch=(), mib=12, out_specs=None, kept=(),
    aliases=None,
):
    body = kernel
    if kept:
        kept = in_vmem(*kept)
        at, count = len(args), len(kept)
        body = lambda *refs: kernel(*refs[:at], *refs[at + count :])
        args = (*args, *kept)
        in_specs = in_specs + [VMEM] * count
    return pl.pallas_call(
        body,
        out_shape=out_shape,
        in_specs=in_specs,
        out_specs=out_specs or (
            (VMEM,) * len(out_shape) if isinstance(out_shape, tuple) else VMEM
        ),
        scratch_shapes=scratch,
        input_output_aliases=aliases or {},
        compiler_params=pltpu.CompilerParams(vmem_limit_bytes=mib << 20),
        cost_estimate=pl.CostEstimate(
            flops=10**8, bytes_accessed=sum(a.size * 4 for a in args), transcendentals=0
        ),
    )(*args)


def shape(rows, lanes=LANES, space=pltpu.VMEM):
    return space((rows, lanes), F32)


def in_vmem(*values):
    return tuple(pltpu.with_memory_space_constraint(v, pltpu.VMEM) for v in values)


def in_hbm(v):
    return pltpu.with_memory_space_constraint(v, pltpu.HBM)


def local(
    matrix_moles,
    pore_matrix,
    matrix_rate,
    matrix_upwind,
    frac_moles,
    pore_frac,
    frac_rate,
    frac_upwind,
    ff_open,
    kvalues,
    slot_patch,
    patch_block,
):
    z = Sizes(matrix_moles, frac_moles)
    bind = lambda f, *a: functools.partial(f, z, *a)
    blocks, slot_patch, kvalues = in_hbm(patch_block.T), in_hbm(slot_patch), in_hbm(kvalues)
    pore = pore_matrix.reshape(-1, z.y)
    rate = matrix_rate.reshape(-1, z.y)
    upwind = matrix_upwind.reshape(-1, z.y)
    field = shape(z.nc * z.cells)
    msg_w, msg_d = shape((z.nc + 1) * z.z), shape((z.nc + 1) * z.x)
    rows_out = z.wide * z.jt * z.tiles_out * SUB
    rows_back = z.wide * z.jt * z.tiles_back * SUB
    src_rows = z.tiles_out * z.cpt * z.slots
    send = call(
        bind(pack_kernel), [SMEM] * 3 + [HBM] * 4,
        (shape(rows_out // z.wide),) * z.wide,
        (
            slot_patch,
            blocks,
            in_hbm(ff_open.T),
            in_hbm(frac_moles.reshape(-1, z.pc)),
            in_hbm(pore_frac),
            in_hbm(frac_rate.reshape(-1, z.pc)),
            in_hbm(frac_upwind.reshape(-1, z.pc)),
        ),
        scratch=[
            pltpu.VMEM((src_rows, z.pc), F32),
            pltpu.VMEM((3 * SUBSTEPS * z.slots, z.pc), I32),
            pltpu.SemaphoreType.DMA((4,)),
        ],
    )

    def trade(chunks):
        got = [chunks[0]]
        for s in range(1, z.wide):
            pairs = [(i, (i + s) % z.wide) for i in range(z.wide)]
            got.append(lax.ppermute(chunks[s], "wide", pairs))
        return tuple(got)

    def exchange(a, b, axis):
        return swap(a, axis, True), swap(b, axis, False, axis == "wide")

    recv = trade(send)
    mobile_m, early, wa, wb, da, db, tab, gather, rate, upwind, pore = call(
        bind(first_matrix_kernel), [SMEM] * 3 + [HBM] * 4,
        (
            field, field, msg_w, msg_w, msg_d, msg_d, pltpu.VMEM((6 * SUB, LANES), I32),
            shape(z.places, -(-3 * z.blocks // LANES) * LANES),
            shape(3 * z.cells), pltpu.VMEM((3 * SUBSTEPS * z.cells, LANES), I32),
            shape(z.cells),
        ),
        (
            kvalues, slot_patch, blocks, in_hbm(matrix_moles.reshape(z.nc, z.cells, LANES)),
            in_hbm(rate), in_hbm(upwind), in_hbm(pore),
        ),
        scratch=[
            pltpu.VMEM((z.nc, z.cells, LANES), F32),
            pltpu.SemaphoreType.DMA((3,)),
            pltpu.SemaphoreType.DMA((PARTS,)),
        ],
    )
    wide_halos = exchange(wa, wb, "wide")
    deep_halos = exchange(da, db, "depth")
    coef_field = shape(z.coefs * z.cells)
    tiles, inner = z.wide * z.tiles_out * SUB, z.jt - 2
    moles_f, mobile_f, coef, fa, fb, staged_rows = call(
        bind(frac_edge_kernel), [SMEM] + [VMEM] * 2 + [HBM] * (z.wide - 1),
        (field, field, coef_field, msg_w, msg_w, shape(inner * tiles)),
        (kvalues, *in_vmem(tab, recv[0]), *(in_hbm(v) for v in recv[1:])),
        scratch=[
            pltpu.VMEM((2 * tiles, LANES), F32),
            pltpu.SemaphoreType.DMA((2 * z.wide,)),
            pltpu.SemaphoreType.DMA((inner * z.wide,)),
        ],
    )
    fa, fb = exchange(fa, fb, "wide")
    moles_f, mobile_f, coef = call(
        bind(frac_inner_kernel), [SMEM] + [VMEM] * 5,
        (field, field, coef_field),
        (kvalues, *in_vmem(tab, staged_rows, moles_f, mobile_f, coef)),
        aliases={3: 0, 4: 1, 5: 2},
    )
    new_f, new_mobile_f, fa, fb = call(
        bind(frac_kernel, 0), [SMEM] + [VMEM] * 7,
        (field, field, msg_w, msg_w),
        (kvalues, *in_vmem(tab, moles_f, mobile_f, mobile_m, coef, fa, fb)),
    )
    fa, fb = exchange(fa, fb, "wide")
    moles, mobile_m, wa, wb, da, db = call(
        bind(matrix_kernel, 0), [SMEM] + [VMEM] * 11,
        (field, field, msg_w, msg_w, msg_d, msg_d),
        (
            kvalues,
            *in_vmem(early, mobile_m, mobile_f, coef, rate, upwind, pore),
            *in_vmem(*wide_halos, *deep_halos),
        ),
    )
    wide_halos = exchange(wa, wb, "wide")
    deep_halos = exchange(da, db, "depth")
    t = SUBSTEPS - 1
    back = call(
        bind(last_frac_kernel, t), [VMEM] * 8,
        (shape(rows_back // z.wide, space=pltpu.HBM),) * z.wide,
        in_vmem(tab, gather, new_f, new_mobile_f, mobile_m, coef, fa, fb),
        scratch=[
            pltpu.VMEM((z.nc * z.cells, LANES), F32),
            pltpu.VMEM((rows_back, LANES), F32),
            pltpu.SemaphoreType.DMA((z.wide,)),
        ],
        out_specs=(HBM,) * z.wide,
    )
    returned = trade(back)
    moles = call(
        bind(last_matrix_kernel, t), [VMEM] * 9, field,
        in_vmem(moles, mobile_m, new_mobile_f, coef, rate, upwind, pore, *wide_halos),
    )
    _, moles = call(
        bind(depth_kernel, t), [VMEM] * 7,
        (field, shape(z.nc * z.cells, space=pltpu.HBM)),
        in_vmem(moles, mobile_m, rate, upwind, pore, *deep_halos),
        scratch=[pltpu.SemaphoreType.DMA((z.nc,))],
        out_specs=(VMEM, HBM),
        aliases={0: 0},
    )
    frac = call(
        bind(spread_kernel), [SMEM] * 2 + [VMEM] * z.wide,
        shape(z.nc * z.slots, z.pc, pltpu.HBM),
        (slot_patch, blocks, *in_vmem(*returned)),
        scratch=[pltpu.VMEM((z.nc * z.slots, z.pc), F32), pltpu.SemaphoreType.DMA((z.tiles_back,))],
        out_specs=HBM,
    )
    return moles.reshape(matrix_moles.shape), frac.reshape(frac_moles.shape)


def solution(mesh):
    placed = (
        P(None, "wide", "depth", None),
        P("wide", "depth", None),
        P(None, "wide", "depth", None),
        P(None, None, "wide", "depth", None),
        P(None, ("wide", "depth"), None),
        P(("wide", "depth"), None),
        P(None, ("wide", "depth"), None),
        P(None, None, ("wide", "depth"), None),
        P(("wide", "depth"), None),
        P(),
        P(),
        P(),
    )
    return jax.shard_map(
        local,
        mesh=mesh,
        in_specs=placed,
        out_specs=(P(None, "wide", "depth", None), P(None, ("wide", "depth"), None)),
        check_vma=False,
    )
```
